256 devices in a mesh: seq: 128 (over y, z, x_lo, core), slide: 2 (over x_hi).
Axes of the slice: x: 4 (x_hi: 2, x_lo: 2; x = x_hi * 2 + x_lo), y: 4, z: 8, core: 2. Of those that a mesh axis runs over, the one named last changes fastest.
Arguments:
- layer_input: bfloat16 [2, 32768, 768], P('slide', 'seq'), may hold values from -6 to 6
- cotangent: bfloat16 [2, 32768, 768], P('slide', 'seq'), may hold values from -6 to 6
- layer_norm_gain: float32 [768], replicated, may hold values from 0.25 to 1.75
- layer_norm_bias: float32 [768], replicated, may hold values from -3 to 3
- query_key_value_weight: bfloat16 [768, 2304], replicated, may hold values from -4 to 4
- output_weight: bfloat16 [768, 768], replicated, may hold values from -0.21875 to 0.21875
Outputs:
- layer_output: bfloat16 [2, 32768, 768], P('slide', 'seq')
- input_grad: bfloat16 [2, 32768, 768], P('slide', 'seq')
- grad_qkv: float32 [768, 2304], P('seq')
- grad_out: float32 [768, 768], P('seq')
- grad_gain: float32 [768], replicated
- grad_bias: float32 [768], replicated
The draws below stay inside these ranges and needn't reach their ends.
All inputs are finite; a program needn't handle non-finite values.
Results may differ from the reference program's by a relative error of at most 0.011.
Values may be sent and summed in bfloat16 or wider, within the bound.
No kernel may reach another device: no remote copies, remote signals or barrier semaphores. Data moves between devices by JAX's collectives and lax.ppermute only.
A program may use at most 128 MiB of HBM per device.

```python
import jax
import jax.numpy as jnp
from jax import lax

D = 768
HEADS = 12
BLOCK_TOKENS = 256
TOKENS = 32768
SLIDES = 2
N_SLIDE = 2


def draw_query_key_value_weight(key, part):
    base = jnp.clip(jax.random.normal(key, (D, 3 * D), jnp.float32), -6.0, 6.0) * D ** (-0.5)
    return base.astype(jnp.bfloat16)


def levels(key, shape, split, least, largest):
    gain = 1.0
    for axis_at, parts in split:
        draws = jax.random.uniform(jax.random.fold_in(jax.random.fold_in(key, 6), axis_at), (parts,), jnp.float32, least / len(split), largest / len(split))
        gain = gain * jnp.repeat(jnp.exp(draws), shape[axis_at] // parts).reshape((-1,) + (1,) * (len(shape) - 1 - axis_at))
    return gain


def scatter_about(rng, extent, width, limit, cuts=(), held_as=jnp.bfloat16):
    values = jax.random.normal(rng, extent, jnp.float32) * width
    if len(cuts) > 0:
        values = levels(rng, extent, cuts, -0.22, 0.18) * values
    return jnp.clip(values, min=-limit, max=limit).astype(held_as)


def setup_inputs(seed: int = 0) -> dict:
    key_list = jax.random.split(jax.random.key(seed), 7)
    layer_input = scatter_about(key_list[0], (SLIDES, TOKENS, D), 1.0, 6.0, ((0, 2), (1, 128)))
    cotangent = scatter_about(key_list[1], (SLIDES, TOKENS, D), 1.0, 6.0, ((0, 2), (1, 128)))
    layer_norm_gain = jnp.clip(1.0 + 0.15 * jax.random.normal(key_list[2], (D,), jnp.float32), 0.25, 1.75)
    layer_norm_bias = scatter_about(key_list[3], (D,), 0.5, 3.0, (), jnp.float32)
    query_key_value_weight = draw_query_key_value_weight(jax.random.fold_in(key_list[6], 71), 0)
    output_weight = scatter_about(key_list[5], (D, D), D ** -0.5, 0.21875)
    return dict(layer_input=layer_input, cotangent=cotangent, layer_norm_gain=layer_norm_gain, layer_norm_bias=layer_norm_bias, query_key_value_weight=query_key_value_weight, output_weight=output_weight)


EPS = 1e-05

def apply_layer_norm(token_rows, scale_gain, shift_bias):
    values = token_rows.astype(jnp.float32)
    centered_rows = values - lax.optimization_barrier(jnp.mean(values, axis=-1, keepdims=True))
    inverse_deviation = lax.rsqrt(lax.optimization_barrier(jnp.mean(centered_rows * centered_rows, axis=-1, keepdims=True)) + EPS)
    normalized_rows = centered_rows * inverse_deviation
    return ((normalized_rows * scale_gain + shift_bias).astype(jnp.bfloat16), normalized_rows, inverse_deviation)

def attend(qkv_self, memory_key_value, memory_present):
    token_length = qkv_self.shape[0]
    feature_width = memory_key_value.shape[1] // 2
    head_dim = feature_width // HEADS
    query = qkv_self[:, :feature_width].reshape(token_length, HEADS, head_dim).astype(jnp.float32)
    keys = jnp.concatenate([memory_key_value[:, :feature_width], qkv_self[:, feature_width:2 * feature_width]], 0)
    keys = keys.reshape(2 * token_length, HEADS, head_dim).astype(jnp.float32)
    values = jnp.concatenate([memory_key_value[:, feature_width:], qkv_self[:, 2 * feature_width:]], 0)
    values = values.reshape(2 * token_length, HEADS, head_dim).astype(jnp.float32)
    scores = jnp.einsum('qhe,khe->hqk', query, keys) * head_dim ** (-0.5)
    row_ids = lax.broadcasted_iota(jnp.int32, (token_length, 2 * token_length), 0)
    col_ids = lax.broadcasted_iota(jnp.int32, (token_length, 2 * token_length), 1)
    allowed = jnp.where(col_ids < token_length, memory_present, col_ids - token_length <= row_ids)
    scores = jnp.where(allowed[None], scores, -1e+30)
    top = lax.optimization_barrier(jnp.max(scores, axis=-1, keepdims=True))
    weights = jnp.exp(scores - top)
    probs = weights / lax.optimization_barrier(jnp.sum(weights, axis=-1, keepdims=True))
    probs_b = lax.optimization_barrier(probs.astype(jnp.bfloat16))
    mixed = jnp.einsum('hqk,khe->qhe', probs_b.astype(jnp.float32), values)
    mixed = mixed.reshape(token_length, feature_width).astype(jnp.bfloat16)
    return (mixed, probs, probs_b, query, keys, values)

def attend_back(d_mixed, probs, probs_b, query, keys, values):
    token_length, heads, head_dim = query.shape
    grad_heads = d_mixed.astype(jnp.float32).reshape(token_length, heads, head_dim)
    d_probs = jnp.einsum('qhe,khe->hqk', grad_heads, values)
    d_scores = probs * (d_probs - lax.optimization_barrier(jnp.sum(d_probs * probs, axis=-1, keepdims=True)))
    d_scores_b = lax.optimization_barrier((d_scores * head_dim ** (-0.5)).astype(jnp.bfloat16))
    d_scores_f = d_scores_b.astype(jnp.float32)
    d_query = jnp.einsum('hqk,khe->qhe', d_scores_f, keys).reshape(token_length, -1).astype(jnp.bfloat16)
    d_keys = jnp.einsum('hqk,qhe->khe', d_scores_f, query).reshape(2 * token_length, -1).astype(jnp.bfloat16)
    d_values = jnp.einsum('hqk,qhe->khe', probs_b.astype(jnp.float32), grad_heads)
    d_values = d_values.reshape(2 * token_length, -1).astype(jnp.bfloat16)
    return (d_query, d_keys, d_values)

def block_forward(token_rows, gradient_list, current_query_key_value, memory_key_value, memory_present, current_normed, current_normalized, current_inverse_deviation, query_key_value_weight, output_weight, scale_gain):
    token_length = token_rows.shape[0]
    mixed, probs, probs_b, query, keys, values = attend(current_query_key_value, memory_key_value, memory_present)
    block_output = (token_rows.astype(jnp.float32) + jnp.dot(mixed, output_weight, preferred_element_type=jnp.float32)).astype(jnp.bfloat16)
    d_mixed = jnp.dot(gradient_list, output_weight.T, preferred_element_type=jnp.float32).astype(jnp.bfloat16)
    grad_wout = jnp.dot(mixed.T, gradient_list, preferred_element_type=jnp.float32)
    d_query, d_keys, d_values = attend_back(d_mixed, probs, probs_b, query, keys, values)
    d_own = jnp.concatenate([d_query, d_keys[token_length:], d_values[token_length:]], 1)
    memory_gradient = jnp.concatenate([d_keys[:token_length], d_values[:token_length]], 1)
    grad_wqkv = jnp.dot(current_normed.T, d_own, preferred_element_type=jnp.float32)
    normed_gradient = jnp.dot(d_own, query_key_value_weight.T, preferred_element_type=jnp.float32)
    gain_gradient = lax.optimization_barrier(jnp.sum(normed_gradient * current_normalized, axis=0))
    grad_b = lax.optimization_barrier(jnp.sum(normed_gradient, axis=0))
    normalized_gradient = normed_gradient * scale_gain
    row_gradient = current_inverse_deviation * (normalized_gradient - lax.optimization_barrier(jnp.mean(normalized_gradient, axis=-1, keepdims=True)) - current_normalized * lax.optimization_barrier(jnp.mean(normalized_gradient * current_normalized, axis=-1, keepdims=True)))
    input_gradient = (gradient_list.astype(jnp.float32) + row_gradient).astype(jnp.bfloat16)
    return (block_output, input_gradient, memory_gradient, (grad_wqkv, grad_wout, gain_gradient, grad_b))

def memory_contributions(prior_normed, prior_normalized, memory_gradient, query_key_value_weight):
    feature_width = prior_normed.shape[1]
    key_value_gradient = jnp.dot(prior_normed.T, memory_gradient, preferred_element_type=jnp.float32)
    normed_gradient = jnp.dot(memory_gradient, query_key_value_weight[:, feature_width:].T, preferred_element_type=jnp.float32)
    return (key_value_gradient, lax.optimization_barrier(jnp.sum(normed_gradient * prior_normalized, axis=0)), lax.optimization_barrier(jnp.sum(normed_gradient, axis=0)))

def one_slide(token_rows, gradient_list, scale_gain, shift_bias, query_key_value_weight, output_weight):
    feature_width = token_rows.shape[1]
    count = token_rows.shape[0] // BLOCK_TOKENS
    normed_rows, normalized_rows, inverse_deviation = apply_layer_norm(token_rows, scale_gain, shift_bias)
    query_key_value = jnp.dot(normed_rows, query_key_value_weight, preferred_element_type=jnp.float32).astype(jnp.bfloat16)
    kv_all = query_key_value[:, feature_width:]
    memory_key_value = jnp.concatenate([jnp.zeros((BLOCK_TOKENS, 2 * feature_width), jnp.bfloat16), kv_all[:-BLOCK_TOKENS]], 0)
    prior_normed = jnp.concatenate([jnp.zeros((BLOCK_TOKENS, feature_width), jnp.bfloat16), normed_rows[:-BLOCK_TOKENS]], 0)
    prior_normalized = jnp.concatenate([jnp.zeros((BLOCK_TOKENS, feature_width), jnp.float32), normalized_rows[:-BLOCK_TOKENS]], 0)
    has_memory_flag = jnp.arange(count) > 0

    def block_list(array):
        return array.reshape((count, BLOCK_TOKENS) + array.shape[1:])

    def step(carry, entry_list):
        current_rows, current_gradients, current_query_key_value, current_memory, current_has_memory, current_normed, current_normalized, current_inverse_deviation, current_prior_normed, current_previous_rows = entry_list
        block_output, input_gradient, memory_gradient, term_list = block_forward(current_rows, current_gradients, current_query_key_value, current_memory, current_has_memory, current_normed, current_normalized, current_inverse_deviation, query_key_value_weight, output_weight, scale_gain)
        key_value_gradient, memory_gain, memory_bias = memory_contributions(current_prior_normed, current_previous_rows, memory_gradient, query_key_value_weight)
        acc_qkv, acc_out, acc_gain, acc_bias = carry
        acc_qkv = acc_qkv + term_list[0] + jnp.concatenate([jnp.zeros((feature_width, feature_width), jnp.float32), key_value_gradient], 1)
        return ((acc_qkv, acc_out + term_list[1], acc_gain + term_list[2] + memory_gain, acc_bias + term_list[3] + memory_bias), (block_output, input_gradient))
    init = (jnp.zeros((feature_width, 3 * feature_width), jnp.float32), jnp.zeros((feature_width, feature_width), jnp.float32), jnp.zeros((feature_width,), jnp.float32), jnp.zeros((feature_width,), jnp.float32))
    entry_list = (block_list(token_rows), block_list(gradient_list), block_list(query_key_value), block_list(memory_key_value), has_memory_flag, block_list(normed_rows), block_list(normalized_rows), block_list(inverse_deviation), block_list(prior_normed), block_list(prior_normalized))
    carry, (outputs, d_inputs) = lax.scan(step, init, entry_list)
    return (outputs.reshape(token_rows.shape), d_inputs.reshape(token_rows.shape), carry)

def reference(layer_input, cotangent, layer_norm_gain, layer_norm_bias, query_key_value_weight, output_weight):
    outputs = []
    d_inputs = []
    totals = None
    for which in range(N_SLIDE):
        block_output, input_gradient, carry = one_slide(layer_input[which], cotangent[which], layer_norm_gain, layer_norm_bias, query_key_value_weight, output_weight)
        outputs.append(block_output)
        d_inputs.append(input_gradient)
        totals = carry if totals is None else tuple((a + b for a, b in zip(totals, carry)))
    factor = 1.0 / float(N_SLIDE * layer_input.shape[1]) ** 0.5
    return (jnp.stack(outputs), jnp.stack(d_inputs), totals[0] * factor, totals[1] * factor, totals[2] * factor, totals[3] * factor)
```

```python
import functools

import jax
import jax.numpy as jnp
from jax import lax
from jax.experimental import pallas as pl
from jax.experimental.pallas import tpu as pltpu
from jax.sharding import Mesh
from jax.sharding import PartitionSpec as P

HEADS = 12
EPS = 1e-05
SEQ = ("y", "z", "xl", "c")
PLANE = ("y", "xl", "xh")
COLUMN = ("z", "xh")
T = 256
D = 768
GROUPS = 3
GW = 256
BF = jnp.bfloat16
F32 = jnp.float32
VMEM_LIMIT = 40 * 1024 * 1024


def nn(a, b):
    return lax.dot_general(a, b, (((1,), (0,)), ((), ())), preferred_element_type=F32)


def nt(a, b):
    return lax.dot_general(a, b, (((1,), (1,)), ((), ())), preferred_element_type=F32)


def eye(n):
    rows = lax.broadcasted_iota(jnp.int32, (n, n), 0)
    cols = lax.broadcasted_iota(jnp.int32, (n, n), 1)
    return jnp.where(rows == cols, 1.0, 0.0).astype(BF)


def layer_norm(x_ref, gain_ref, bias_ref):
    values = x_ref[...].astype(F32)
    centered = values - jnp.mean(values, axis=-1, keepdims=True)
    rstd = lax.rsqrt(jnp.mean(centered * centered, axis=-1, keepdims=True) + EPS)
    xhat = centered * rstd
    normed = (xhat * gain_ref[...] + bias_ref[...]).astype(BF)
    return normed, xhat, rstd


def row_order(core):
    p = lax.broadcasted_iota(jnp.int32, (D, 1), 0)
    second = jnp.where(p >= 384, 1, 0)
    q = p - 384 * second
    owner = (q * 171) >> 13
    b = q - 48 * owner
    z = (b * 43) >> 8
    j = b - 6 * z
    y, xl = owner >> 1, owner & 1
    to_core = jnp.where(second == 1, core, 1 - core)
    feature = ((y * 8 + z) * 2 + xl) * 12 + to_core * 6 + j
    cols = lax.broadcasted_iota(jnp.int32, (D, D), 1)
    return jnp.where(cols == feature, 1.0, 0.0).astype(BF)


def own_kernel(core_ref, x_ref, cot_ref, gain_ref, bias_ref, w_ref, wo_ref,
               qkv_ref, dmix_ref, npt_ref, xhat_ref, rstd_ref, mt_ref):
    normed, xhat, rstd = layer_norm(x_ref, gain_ref, bias_ref)
    qkv_ref[...] = nn(normed, w_ref[...]).astype(BF)
    xhat_ref[...] = xhat
    rstd_ref[...] = jnp.broadcast_to(rstd, (T, 128))
    dmix_ref[...] = nt(cot_ref[...], wo_ref[...]).astype(BF)
    mt = row_order(core_ref[0])
    mt_ref[...] = mt
    npt_ref[...] = nt(mt, normed).astype(BF)


def prev_kernel(x_ref, gain_ref, bias_ref, wk_ref, wv_ref, mt_ref, kv_ref, npt_ref, xhat_ref):
    normed, xhat, _ = layer_norm(x_ref, gain_ref, bias_ref)
    kv_ref[:, :D] = nn(normed, wk_ref[...]).astype(BF)
    kv_ref[:, D:] = nn(normed, wv_ref[...]).astype(BF)
    xhat_ref[...] = xhat
    npt_ref[...] = nt(mt_ref[...], normed).astype(BF)


def put_blocks(out_ref, rows):
    for i in range(8):
        for h in range(2):
            out_ref[2 * i + h, 0:48, :] = rows[48 * i : 48 * i + 48, 384 * h : 384 * h + 384]


def group_kernel(first, has_ref, q_ref, k_ref, v_ref, km_ref, vm_ref, dm_ref, npt_ref, nptm_ref,
                 wq_ref, wk_ref, wv_ref, *rest):
    if first:
        send_ref, keep_ref, mixt_ref, dn_ref, dnm_ref = rest
    else:
        dn_in, dnm_in, send_ref, keep_ref, mixt_ref, dn_ref, dnm_ref = rest
    has = has_ref[0] > 0
    lanes = lax.broadcasted_iota(jnp.int32, (T, 128), 1)
    low = lanes < 64
    causal = lax.broadcasted_iota(jnp.int32, (T, T), 0) <= lax.broadcasted_iota(jnp.int32, (T, T), 1)
    unit = eye(128)
    unit2 = eye(T)
    zero = jnp.zeros((), BF)
    dqs, dks, dvs = [], [], []
    for pair in range(2):
        cols = slice(128 * pair, 128 * pair + 128)
        q2 = (q_ref[:, cols].astype(F32) * 0.125).astype(BF)
        k2 = jnp.concatenate([k_ref[:, cols], km_ref[:, cols]], axis=0)
        v2 = jnp.concatenate([v_ref[:, cols], vm_ref[:, cols]], axis=0)
        dm2 = dm_ref[:, cols]
        kt2 = nt(unit, k2).astype(BF)
        vt2 = nt(unit, v2).astype(BF)
        ds_parts, p_parts, q_parts, dm_parts, dqt_parts = [], [], [], [], []
        for half in range(2):
            pick = low if half == 0 else jnp.logical_not(low)
            qa = jnp.where(pick, q2, zero)
            dma = jnp.where(pick, dm2, zero)
            st = nt(k2, qa)
            st_own = jnp.where(causal, st[:T], -1e30)
            st_mem = jnp.where(has, st[T:], -1e30)
            st = jnp.concatenate([st_own, st_mem], axis=0)
            top = jnp.max(st, axis=0, keepdims=True)
            e = jnp.exp(st - top)
            p = e * (1.0 / jnp.sum(e, axis=0, keepdims=True))
            pb = p.astype(BF)
            rows = slice(64 * half, 64 * half + 64)
            mixt_ref[128 * pair + 64 * half : 128 * pair + 64 * half + 64, :] = nn(vt2[rows], pb).astype(BF)
            dp = nt(v2, dma)
            ds = (p * (dp - jnp.sum(dp * p, axis=0, keepdims=True))).astype(BF)
            dqt_parts.append((nn(kt2[rows], ds) * 0.125).astype(BF))
            ds_parts.append(ds)
            p_parts.append(pb)
            q_parts.append(qa)
            dm_parts.append(dma)
        dks.append(nn(jnp.concatenate(ds_parts, axis=1), jnp.concatenate(q_parts, axis=0)).astype(BF))
        dvs.append(nn(jnp.concatenate(p_parts, axis=1), jnp.concatenate(dm_parts, axis=0)).astype(BF))
        dqs.append(nt(unit2, jnp.concatenate(dqt_parts, axis=0)).astype(BF))
    dq = jnp.concatenate(dqs, axis=1)
    dk = jnp.concatenate(dks, axis=1)
    dv = jnp.concatenate(dvs, axis=1)
    npt = npt_ref[...]
    npt_all = jnp.concatenate([npt, nptm_ref[...]], axis=1)
    for which, out_ref in ((0, send_ref), (1, keep_ref)):
        rows = slice(384 * which, 384 * which + 384)
        put_blocks(
            out_ref,
            jnp.concatenate(
                [nn(npt[rows], dq).astype(BF), nn(npt_all[rows], dk).astype(BF), nn(npt_all[rows], dv).astype(BF)],
                axis=1,
            ),
        )
    own = nt(dq, wq_ref[...]) + nt(dk[:T], wk_ref[...]) + nt(dv[:T], wv_ref[...])
    mem = nt(dk[T:], wk_ref[...]) + nt(dv[T:], wv_ref[...])
    if first:
        dn_ref[...] = own
        dnm_ref[...] = mem
    else:
        dn_ref[...] = dn_in[...] + own
        dnm_ref[...] = dnm_in[...] + mem


def out_kernel(m0_ref, m1_ref, m2_ref, mt_ref, cot_ref, dn_ref, dnm_ref, xhat_ref, xhatm_ref,
               send_ref, keep_ref, vec_ref, mixt_ref):
    mixt = jnp.concatenate([m0_ref[...], m1_ref[...], m2_ref[...]], axis=0)
    mixt_ref[...] = mixt
    rows = nn(nn(mt_ref[...], mixt).astype(BF), cot_ref[...]).astype(BF)
    put_blocks(send_ref, rows[:384])
    put_blocks(keep_ref, rows[384:])
    dn, dnm = dn_ref[...], dnm_ref[...]
    vec_ref[0:1, :] = jnp.sum(dn * xhat_ref[...] + dnm * xhatm_ref[...], axis=0, keepdims=True)
    vec_ref[1:2, :] = jnp.sum(dn + dnm, axis=0, keepdims=True)


def token_kernel(x_ref, cot_ref, mixt_ref, wo_ref, dn_ref, xhat_ref, rstd_ref, gain_ref, out_ref, dx_ref):
    mixed = nt(eye(T), mixt_ref[...]).astype(BF)
    out_ref[...] = (x_ref[...].astype(F32) + nn(mixed, wo_ref[...])).astype(BF)
    d_hat = dn_ref[...] * gain_ref[...]
    xhat = xhat_ref[...]
    row = rstd_ref[:, 0:1] * (
        d_hat
        - jnp.mean(d_hat, axis=-1, keepdims=True)
        - xhat * jnp.mean(d_hat * xhat, axis=-1, keepdims=True)
    )
    dx_ref[...] = (cot_ref[...].astype(F32) + row).astype(BF)


def split(value):
    high = value.astype(BF)
    return high, (value - high.astype(F32)).astype(BF)


def last_pair_kernel(keep2_ref, recv2_ref, keep3_ref, recv3_ref, vec_ref, vecr_ref, out_ref):
    add = lambda a, b: (a[...].astype(F32) + b[...].astype(F32)).astype(BF)
    out_ref[:, 0:48, 0:384] = add(keep2_ref, recv2_ref)
    out_ref[:, 0:48, 384:768] = add(keep3_ref, recv3_ref)
    total = vec_ref[...] + vecr_ref[...]
    high, low = split(total)
    rows = jnp.concatenate([high, low, jnp.zeros((4, D), BF)], axis=0)
    for i in range(16):
        out_ref[i, 48:56, :] = rows


def plane_sum_kernel(a_ref, b_ref, c_ref, out_ref):
    def total(ref, rows, cols):
        acc = ref[0, rows, cols].astype(F32)
        for i in range(1, 16):
            acc = acc + ref[i, rows, cols].astype(F32)
        return acc

    grads = slice(0, 48)
    parts = [total(a_ref, grads, slice(None)), total(b_ref, grads, slice(None)), total(c_ref, grads, slice(None))]
    sums = jnp.concatenate(parts, axis=1)
    rows = total(c_ref, slice(48, 56), slice(None))
    gain, bias = rows[0:1] + rows[2:3], rows[1:2] + rows[3:4]
    vec = jnp.concatenate([gain, bias], axis=1)
    high, low = split(vec)
    tail = jnp.concatenate([high.astype(F32), low.astype(F32)], axis=0)
    for z in range(8):
        block = jnp.concatenate([sums[6 * z : 6 * z + 6], tail], axis=0).astype(BF)
        out_ref[2 * z] = block
        out_ref[2 * z + 1] = block


def finish_kernel(factor, in_ref, qkv_ref, wout_ref, gain_ref, bias_ref):
    def total(h):
        acc = in_ref[h].astype(F32)
        for z in range(1, 8):
            acc = acc + in_ref[2 * z + h].astype(F32)
        return acc * factor

    halves = [total(0), total(1)]
    for g in range(GROUPS + 1):
        cols = slice(384 * g, 384 * g + 384)
        full = jnp.concatenate([halves[0][0:6, cols], halves[1][0:6, cols]], axis=1)
        if g < GROUPS:
            for i in range(3):
                at = D * i + GW * g
                qkv_ref[:, at : at + GW] = full[:, GW * i : GW * i + GW]
        else:
            wout_ref[...] = full
    vec = halves[0][6:7] + halves[0][7:8]
    gain_ref[...] = vec[:, :D]
    bias_ref[...] = vec[:, D:]


def call(kernel, name, out_shape, args, in_specs=None):
    vm = pl.BlockSpec(memory_space=pltpu.VMEM)
    if in_specs is None:
        in_specs = [vm] * len(args)
    specs = [vm if s is None else s for s in in_specs]
    many = isinstance(out_shape, (tuple, list))
    return pl.pallas_call(
        kernel,
        name=name,
        grid=(1,),
        in_specs=[whole(a) if s is vm else s for a, s in zip(args, specs)],
        out_specs=[whole(o) for o in out_shape] if many else whole(out_shape),
        out_shape=out_shape,
        compiler_params=pltpu.CompilerParams(vmem_limit_bytes=VMEM_LIMIT),
    )(*args)


def whole(a):
    return pl.BlockSpec(a.shape, lambda i, n=len(a.shape): (0,) * n)


SCALAR = pl.BlockSpec(memory_space=pltpu.SMEM)


def block(shape, *index):
    return pl.BlockSpec(shape, lambda i: index)


def sds(*shape, dtype=BF):
    return jax.ShapeDtypeStruct(shape, dtype)


def own_part(core, x, cot, gain, bias, w, wo):
    return call(
        own_kernel, "own_part",
        [sds(T, 3 * D), sds(T, D), sds(D, T), sds(T, D, dtype=F32), sds(T, 128, dtype=F32), sds(D, D)],
        [core, x, cot, gain, bias, w, wo], [SCALAR] + [None] * 6,
    )


def prev_part(xp, gain, bias, w, mt):
    return call(
        prev_kernel, "prev_part",
        [sds(T, 2 * D), sds(D, T), sds(T, D, dtype=F32)],
        [xp, gain, bias, w, w, mt], [None] * 3 + [block((D, D), 0, 1), block((D, D), 0, 2), None],
    )


def group_part(g, has, qkv, kvm, dmix, npt, nptm, w, sums):
    first = g == 0
    tok = lambda at: block((T, GW), 0, at)
    wt = lambda at: block((D, GW), 0, at)
    args = [has, qkv, qkv, qkv, kvm, kvm, dmix, npt, nptm, w, w, w]
    specs = [SCALAR, tok(g), tok(3 + g), tok(6 + g), tok(g), tok(3 + g), tok(g), None, None, wt(g), wt(3 + g), wt(6 + g)]
    if not first:
        args += list(sums)
        specs += [None, None]
    return call(
        functools.partial(group_kernel, first), "head_group",
        [sds(16, 48, 384), sds(16, 48, 384), sds(GW, T), sds(T, D, dtype=F32), sds(T, D, dtype=F32)],
        args, specs,
    )


def on_device(layer_input, cotangent, gain, bias, w, wo):
    x, cot = layer_input[0], cotangent[0]
    gain, bias = gain.reshape(1, D), bias.reshape(1, D)
    seq = lax.axis_size(SEQ)
    xp = lax.ppermute(x, SEQ, [(i, i + 1) for i in range(seq - 1)])
    core = lax.axis_index("c").astype(jnp.int32).reshape(1)
    has = (lax.axis_index(SEQ) > 0).astype(jnp.int32).reshape(1)
    qkv, dmix, npt, xhat, rstd, mt = own_part(core, x, cot, gain, bias, w, wo)
    kvm, nptm, xhatm = prev_part(xp, gain, bias, w, mt)

    def swap(block):
        return lax.ppermute(block, "c", [(0, 1), (1, 0)])

    def spread(block):
        return lax.all_to_all(block, PLANE, 0, 0, tiled=True)

    mixes, sums, spreads = [], None, []
    for g in range(GROUPS):
        send, keep, mixt, dn, dnm = group_part(g, has, qkv, kvm, dmix, npt, nptm, w, sums)
        sums = (dn, dnm)
        mixes.append(mixt)
        if g < GROUPS - 1:
            spreads.append(spread((keep.astype(F32) + swap(send).astype(F32)).astype(BF)))
        else:
            last = (keep, swap(send))
    send, keep, vec, mixt = call(
        out_kernel, "output_weight_part",
        [sds(16, 48, 384), sds(16, 48, 384), sds(2, D, dtype=F32), sds(D, T)],
        [*mixes, mt, cot, dn, dnm, xhat, xhatm],
    )
    both = call(last_pair_kernel, "pair_sum", sds(16, 56, 768), [*last, keep, swap(send), vec, swap(vec)])
    both = spread(both)
    out, dx = call(
        token_kernel, "token_outputs", [sds(T, D), sds(T, D)],
        [x, cot, mixt, wo, dn, xhat, rstd, gain],
    )
    mine = call(plane_sum_kernel, "plane_sum", sds(16, 8, 1536), [*spreads, both])
    mine = lax.all_to_all(mine, COLUMN, 0, 0, tiled=True)
    factor = 1.0 / float(seq * lax.axis_size("xh") * T) ** 0.5
    grad_qkv, grad_out, grad_gain, grad_bias = call(
        functools.partial(finish_kernel, factor), "finish",
        [sds(6, 3 * D, dtype=F32), sds(6, D, dtype=F32), sds(1, D, dtype=F32), sds(1, D, dtype=F32)],
        [mine],
    )
    return out[None], dx[None], grad_qkv, grad_out, grad_gain.reshape(D), grad_bias.reshape(D)


def solution(mesh):
    torus = Mesh(mesh.devices.reshape(4, 8, 2, 2, 2), ("y", "z", "xl", "c", "xh"))
    return jax.shard_map(
        on_device,
        mesh=torus,
        in_specs=(P("xh", SEQ, None), P("xh", SEQ, None), P(), P(), P(), P()),
        out_specs=(P("xh", SEQ, None), P("xh", SEQ, None), P(SEQ, None), P(SEQ, None), P(), P()),
        check_vma=False,
    )
```

```python
import functools

import jax
import jax.numpy as jnp
from jax import lax
from jax.experimental import pallas as pl
from jax.experimental.pallas import tpu as pltpu
from jax.sharding import Mesh
from jax.sharding import PartitionSpec as P

HEADS = 12
EPS = 1e-05
SEQ = ("y", "z", "xl", "c")
ROW = ("xl", "xh")
T = 256
D = 768
GROUPS = 3
GW = 256
BF = jnp.bfloat16
F32 = jnp.float32
LIMIT = 24


def nn(a, b):
    return lax.dot_general(a, b, (((1,), (0,)), ((), ())), preferred_element_type=F32)


def nt(a, b):
    return lax.dot_general(a, b, (((1,), (1,)), ((), ())), preferred_element_type=F32)


def eye(n):
    rows = lax.broadcasted_iota(jnp.int32, (n, n), 0)
    cols = lax.broadcasted_iota(jnp.int32, (n, n), 1)
    return jnp.where(rows == cols, 1.0, 0.0).astype(BF)


def layer_norm(x_ref, gain, bias):
    values = x_ref[...].astype(F32)
    centered = values - jnp.mean(values, axis=-1, keepdims=True)
    rstd = lax.rsqrt(jnp.mean(centered * centered, axis=-1, keepdims=True) + EPS)
    xhat = centered * rstd
    normed = (xhat * gain + bias).astype(BF)
    return normed, xhat, rstd


def row_order(at_ref):
    p = lax.broadcasted_iota(jnp.int32, (D, 1), 0)
    second = jnp.where(p >= 384, 1, 0)
    q = p - 384 * second
    owner = (q * 171) >> 13
    b = q - 48 * owner
    z = (b * 43) >> 8
    j = b - 6 * z
    y, xl = (owner >> 1) ^ at_ref[0], (owner & 1) ^ at_ref[1]
    to_core = jnp.where(second == 1, at_ref[2], 1 - at_ref[2])
    feature = ((y * 8 + z) * 2 + xl) * 12 + to_core * 6 + j
    cols = lax.broadcasted_iota(jnp.int32, (D, D), 1)
    return jnp.where(cols == feature, 1.0, 0.0).astype(BF)


def own_kernel(at_ref, gain_ref, bias_ref, x_hbm, cot_hbm, w_hbm, wo_hbm,
               qkv_ref, dmix_ref, npt_ref, xhat_ref, rstd_ref, mt_ref,
               x_ref, cot_ref, w_ref, wo_ref, sems):
    copies = [pltpu.make_async_copy(x_hbm, x_ref, sems.at[0])]
    for i in range(3):
        copies.append(pltpu.make_async_copy(w_hbm.at[:, pl.ds(D * i, D)], w_ref.at[i], sems.at[1 + i]))
    copies.append(pltpu.make_async_copy(cot_hbm, cot_ref, sems.at[4]))
    copies.append(pltpu.make_async_copy(wo_hbm, wo_ref, sems.at[5]))
    for copy in copies:
        copy.start()
    mt = row_order(at_ref)
    mt_ref[...] = mt
    copies[0].wait()
    normed, xhat, rstd = layer_norm(x_ref, gain_ref[...].reshape(1, D), bias_ref[...].reshape(1, D))
    xhat_ref[...] = xhat
    rstd_ref[...] = jnp.broadcast_to(rstd, (T, 128))
    npt_ref[...] = nt(mt, normed).astype(BF)
    for i in range(3):
        copies[1 + i].wait()
        qkv_ref[:, D * i : D * i + D] = nn(normed, w_ref[i]).astype(BF)
    copies[4].wait()
    copies[5].wait()
    dmix_ref[...] = nt(cot_ref[...], wo_ref[...]).astype(BF)


def head_group(g, has, qkv_ref, kvm_ref, dmix_ref):
    at = GW * g
    lanes = lax.broadcasted_iota(jnp.int32, (T, 128), 1)
    low = lanes < 64
    causal = lax.broadcasted_iota(jnp.int32, (T, T), 0) <= lax.broadcasted_iota(jnp.int32, (T, T), 1)
    unit = eye(128)
    unit2 = eye(T)
    zero = jnp.zeros((), BF)
    mixts, dqs, dks, dvs = [], [], [], []
    for pair in range(2):
        cq = slice(at + 128 * pair, at + 128 * pair + 128)
        ck = slice(D + cq.start, D + cq.stop)
        cv = slice(2 * D + cq.start, 2 * D + cq.stop)
        q2 = (qkv_ref[:, cq].astype(F32) * 0.125).astype(BF)
        k2 = jnp.concatenate([qkv_ref[:, ck], kvm_ref[:, cq]], axis=0)
        v2 = jnp.concatenate([qkv_ref[:, cv], kvm_ref[:, ck]], axis=0)
        dm2 = dmix_ref[:, cq]
        kt2 = nt(unit, k2).astype(BF)
        vt2 = nt(unit, v2).astype(BF)
        ds_parts, p_parts, q_parts, dm_parts, dqt_parts = [], [], [], [], []
        for half in range(2):
            pick = low if half == 0 else jnp.logical_not(low)
            qa = jnp.where(pick, q2, zero)
            dma = jnp.where(pick, dm2, zero)
            st = nt(k2, qa)
            st_own = jnp.where(causal, st[:T], -1e30)
            st_mem = jnp.where(has, st[T:], -1e30)
            st = jnp.concatenate([st_own, st_mem], axis=0)
            top = jnp.max(st, axis=0, keepdims=True)
            e = jnp.exp(st - top)
            p = e * (1.0 / jnp.sum(e, axis=0, keepdims=True))
            pb = p.astype(BF)
            rows = slice(64 * half, 64 * half + 64)
            mixts.append(nn(vt2[rows], pb).astype(BF))
            dp = nt(v2, dma)
            ds = (p * (dp - jnp.sum(dp * p, axis=0, keepdims=True))).astype(BF)
            dqt_parts.append((nn(kt2[rows], ds) * 0.125).astype(BF))
            ds_parts.append(ds)
            p_parts.append(pb)
            q_parts.append(qa)
            dm_parts.append(dma)
        dks.append(nn(jnp.concatenate(ds_parts, axis=1), jnp.concatenate(q_parts, axis=0)).astype(BF))
        dvs.append(nn(jnp.concatenate(p_parts, axis=1), jnp.concatenate(dm_parts, axis=0)).astype(BF))
        dqs.append(nt(unit2, jnp.concatenate(dqt_parts, axis=0)).astype(BF))
    dq = jnp.concatenate(dqs, axis=1)
    dk = jnp.concatenate(dks, axis=1)
    dv = jnp.concatenate(dvs, axis=1)
    return jnp.concatenate(mixts, axis=0), dq, dk, dv


def put_rows(send_ref, keep_ref, slot, xh, lhs, rhs):
    first, second = rhs[:, :384], rhs[:, 384:]
    mine = xh == 0
    for r in range(2):
        part = jnp.where(mine, first, second) if r == 0 else jnp.where(mine, second, first)
        at = 768 * r + 384 * slot
        send_ref[:, at : at + 384] = nn(lhs[:384], part).astype(BF)
        keep_ref[:, at : at + 384] = nn(lhs[384:], part).astype(BF)


def group_outputs(g, slot, at_ref, npt_all, w_ref, grads, send_ref, keep_ref):
    dq, dk, dv = grads
    rhs = jnp.concatenate([jnp.concatenate([dq, jnp.zeros((T, GW), BF)], axis=0), dk, dv], axis=1)
    put_rows(send_ref, keep_ref, slot, at_ref[3], npt_all, rhs)
    wq, wk, wv = (w_ref[:, D * i + GW * g : D * i + GW * g + GW] for i in range(3))
    own = nt(dq, wq) + nt(dk[:T], wk) + nt(dv[:T], wv)
    mem = nt(dk[T:], wk) + nt(dv[T:], wv)
    return own, mem


def first_kernel(at_ref, gain_ref, bias_ref, xp_ref, w_ref, mt_ref, qkv_ref, dmix_ref, npt_ref,
                 send_ref, keep_ref, mixt_ref, dn_ref, dnm_ref, kvm_ref, npt_all_ref, xhatm_ref):
    normed, xhat, _ = layer_norm(xp_ref, gain_ref[...].reshape(1, D), bias_ref[...].reshape(1, D))
    kvm_ref[...] = nn(normed, w_ref[:, D:]).astype(BF)
    xhatm_ref[...] = xhat
    npt_all_ref[:, :T] = npt_ref[...]
    npt_all_ref[:, T:] = nt(mt_ref[...], normed).astype(BF)
    has = at_ref[4] > 0
    npt_all = npt_all_ref[...]
    for g in range(2):
        mixt, *grads = head_group(g, has, qkv_ref, kvm_ref, dmix_ref)
        mixt_ref[GW * g : GW * g + GW, :] = mixt
        own, mem = group_outputs(g, g, at_ref, npt_all, w_ref, grads, send_ref, keep_ref)
        if g == 0:
            dn_ref[...] = own
            dnm_ref[...] = mem
        else:
            dn_ref[...] += own
            dnm_ref[...] += mem


def second_kernel(at_ref, w_ref, mt_ref, cot_ref, qkv_ref, dmix_ref, mixt_in, dn_in, dnm_in, kvm_ref, npt_all_ref,
                  xhat_ref, xhatm_ref, send_ref, keep_ref, vec_ref, mixt_ref, dn_ref):
    mixt, *grads = head_group(2, at_ref[4] > 0, qkv_ref, kvm_ref, dmix_ref)
    mixt_ref[: 2 * GW, :] = mixt_in[...]
    mixt_ref[2 * GW :, :] = mixt
    own, mem = group_outputs(2, 0, at_ref, npt_all_ref[...], w_ref, grads, send_ref, keep_ref)
    lhs = nn(mt_ref[...], mixt_ref[...]).astype(BF)
    put_rows(send_ref, keep_ref, 1, at_ref[3], lhs, cot_ref[...])
    dn, dnm = dn_in[...] + own, dnm_in[...] + mem
    dn_ref[...] = dn
    vec_ref[0:1, :] = jnp.sum(dn * xhat_ref[...] + dnm * xhatm_ref[...], axis=0, keepdims=True)
    vec_ref[1:2, :] = jnp.sum(dn + dnm, axis=0, keepdims=True)


def token_kernel(gain_ref, x_ref, cot_ref, mixt_ref, wo_ref, dn_ref, xhat_ref, rstd_ref, out_ref, dx_ref):
    mixed = nt(eye(T), mixt_ref[...]).astype(BF)
    out_ref[...] = (x_ref[...].astype(F32) + nn(mixed, wo_ref[...])).astype(BF)
    d_hat = dn_ref[...] * gain_ref[...].reshape(1, D)
    xhat = xhat_ref[...]
    row = rstd_ref[:, 0:1] * (
        d_hat
        - jnp.mean(d_hat, axis=-1, keepdims=True)
        - xhat * jnp.mean(d_hat * xhat, axis=-1, keepdims=True)
    )
    dx_ref[...] = (cot_ref[...].astype(F32) + row).astype(BF)


def split_rows(value):
    high = value.astype(BF)
    low = (value - high.astype(F32)).astype(BF)
    return jnp.concatenate([high, low, jnp.zeros((4, value.shape[1]), BF)], axis=0)


def join_rows(rows):
    return rows[0:2].astype(F32) + rows[2:4].astype(F32)


def tree(a, b, c, d):
    return (a.astype(F32) + b.astype(F32)) + (c.astype(F32) + d.astype(F32))


def pair_a_kernel(keep_ref, recv_ref, *outs):
    for k in range(4):
        rows = slice(96 * k, 96 * k + 96)
        outs[k][...] = (keep_ref[rows, :].astype(F32) + recv_ref[rows, :].astype(F32)).astype(BF)


def pair_b_kernel(keep_ref, recv_ref, vec_ref, vecr_ref, *outs):
    vec = split_rows(vec_ref[...] + vecr_ref[...])
    for k in range(4):
        cols = slice(768 * (k & 1), 768 * (k & 1) + 768)
        for y in range(4):
            rows = slice(96 * y + 48 * (k >> 1), 96 * y + 48 * (k >> 1) + 48)
            outs[k][48 * y : 48 * y + 48, :] = (
                keep_ref[rows, cols].astype(F32) + recv_ref[rows, cols].astype(F32)
            ).astype(BF)
        outs[k][192:200, :] = vec


def mid_a_kernel(a, b, c, d, *outs):
    for k in range(4):
        rows = slice(48 * (k >> 1), 48 * (k >> 1) + 48)
        cols = slice(768 * (k & 1), 768 * (k & 1) + 768)
        outs[k][...] = tree(a[rows, cols], b[rows, cols], c[rows, cols], d[rows, cols]).astype(BF)


def mid_b_kernel(a, b, c, d, *outs):
    vec = split_rows((join_rows(a[192:200]) + join_rows(b[192:200])) + (join_rows(c[192:200]) + join_rows(d[192:200])))
    for k in range(4):
        rows = slice(48 * k, 48 * k + 48)
        outs[k][0:48, :] = tree(a[rows], b[rows], c[rows], d[rows]).astype(BF)
        outs[k][48:56, :] = vec


def plane_kernel(a0, a1, a2, a3, b0, b1, b2, b3, out_ref):
    at = slice(48, 56)
    vec = (join_rows(b0[at]) + join_rows(b1[at])) + (join_rows(b2[at]) + join_rows(b3[at]))
    vec = jnp.concatenate([vec[0:1], vec[1:2]], axis=1)
    high = vec.astype(BF).astype(F32)
    tail = jnp.concatenate([high, vec - high], axis=0)
    g = slice(0, 48)
    sums = jnp.concatenate([tree(a0[...], a1[...], a2[...], a3[...]), tree(b0[g], b1[g], b2[g], b3[g])], axis=1)
    for z in range(8):
        out_ref[z] = jnp.concatenate([sums[6 * z : 6 * z + 6], tail], axis=0).astype(BF)


def column_kernel(factor, in_ref, rows_ref, gain_ref, bias_ref):
    acc = in_ref[0].astype(F32)
    for z in range(1, 8):
        acc = acc + in_ref[z].astype(F32)
    rows_ref[...] = acc.astype(BF)
    vec = (acc[6:7] + acc[7:8]) * factor
    gain_ref[...] = vec[:, :D].reshape(D)
    bias_ref[...] = vec[:, D:].reshape(D)


def finish_kernel(factor, at_ref, mine_ref, other_ref, qkv_ref, wout_ref):
    mine, other = mine_ref[...].astype(F32) * factor, other_ref[...].astype(F32) * factor
    first = at_ref[3] == 0
    halves = [jnp.where(first, mine, other), jnp.where(first, other, mine)]
    for g in range(GROUPS + 1):
        cols = slice(384 * g, 384 * g + 384)
        full = jnp.concatenate([halves[0][0:6, cols], halves[1][0:6, cols]], axis=1)
        if g < GROUPS:
            for i in range(3):
                at = D * i + GW * g
                qkv_ref[:, at : at + GW] = full[:, GW * i : GW * i + GW]
        else:
            wout_ref[...] = full


VM = pl.BlockSpec(memory_space=pltpu.VMEM)
SM = pl.BlockSpec(memory_space=pltpu.SMEM)
ANY = pl.BlockSpec(memory_space=pl.ANY)


def call(kernel, name, out_shape, args, scalars=0, anys=(), scratch=(), limit=16):
    specs = [SM if i < scalars else ANY if i in anys else VM for i in range(len(args))]
    return pl.pallas_call(
        kernel,
        name=name,
        in_specs=specs,
        out_specs=[VM] * len(out_shape),
        out_shape=out_shape,
        scratch_shapes=scratch,
        compiler_params=pltpu.CompilerParams(vmem_limit_bytes=limit * 1024 * 1024),
    )(*args)


def sds(*shape, dtype=BF):
    return jax.ShapeDtypeStruct(shape, dtype)


def on_device(layer_input, cotangent, gain, bias, w, wo):
    x, cot = layer_input[0], cotangent[0]
    seq = lax.axis_size(SEQ)
    xp = lax.ppermute(x, SEQ, [(i, i + 1) for i in range(seq - 1)])
    place = [lax.axis_index(n) for n in ("y", "xl", "c", "xh")] + [lax.axis_index(SEQ) > 0]
    at = jnp.stack([v.astype(jnp.int32) for v in place])
    row, mat, tokens = sds(T, D, dtype=F32), sds(D, D), sds(T, D)
    qkv, dmix, npt, xhat, rstd, mt = call(
        own_kernel, "own_part",
        [sds(T, 3 * D), tokens, sds(D, T), row, sds(T, 128, dtype=F32), mat],
        [at, gain, bias, x, cot, w, wo], 1, (3, 4, 5, 6),
        [pltpu.VMEM((T, D), BF), pltpu.VMEM((T, D), BF), pltpu.VMEM((3, D, D), BF), pltpu.VMEM((D, D), BF),
         pltpu.SemaphoreType.DMA((6,))],
    )
    wide = sds(384, 1536)
    send_a, keep_a, mixt, dn, dnm, kvm, npt_all, xhatm = call(
        first_kernel, "memory_and_heads",
        [wide, wide, sds(2 * GW, T), row, row, sds(T, 2 * D), sds(D, 2 * T), row],
        [at, gain, bias, xp, w, mt, qkv, dmix, npt], 1, limit=LIMIT,
    )
    send_b, keep_b, vec, mixt, dn = call(
        second_kernel, "heads_and_output_weight",
        [wide, wide, sds(2, D, dtype=F32), sds(D, T), row],
        [at, w, mt, cot, qkv, dmix, mixt, dn, dnm, kvm, npt_all, xhat, xhatm], 1, limit=LIMIT,
    )

    def swap(block):
        return lax.ppermute(block, "c", [(0, 1), (1, 0)])

    def exchange(parts, axes):
        n = lax.axis_size(axes)
        return [parts[0]] + [lax.ppermute(parts[k], axes, [(i, i ^ k) for i in range(n)]) for k in (1, 3, 2)]

    def ordered(parts):
        own, one, three, two = parts
        return [own, one, two, three]

    parts_a = call(pair_a_kernel, "pair_sum_a", [sds(96, 1536)] * 4, [keep_a, swap(send_a)])
    parts_b = call(pair_b_kernel, "pair_sum_b", [sds(200, 768)] * 4, [keep_b, swap(send_b), vec, swap(vec)])
    parts_a = ordered(exchange(parts_a, "y"))
    parts_b = ordered(exchange(parts_b, ROW))
    out, dx = call(
        token_kernel, "token_outputs", [tokens, tokens],
        [gain, x, cot, mixt, wo, dn, xhat, rstd],
    )
    parts_a = call(mid_a_kernel, "middle_sum_a", [sds(48, 768)] * 4, parts_a)
    parts_b = call(mid_b_kernel, "middle_sum_b", [sds(56, 768)] * 4, parts_b)
    parts_a = ordered(exchange(parts_a, ROW))
    parts_b = ordered(exchange(parts_b, "y"))
    (mine,) = call(plane_kernel, "plane_sum", [sds(8, 8, 1536)], [*parts_a, *parts_b])
    mine = lax.all_to_all(mine, "z", 0, 0, tiled=True)
    factor = 1.0 / float(seq * lax.axis_size("xh") * T) ** 0.5
    mine, grad_gain, grad_bias = call(
        functools.partial(column_kernel, factor), "column_sum",
        [sds(8, 1536), sds(D, dtype=F32), sds(D, dtype=F32)], [mine],
    )
    other = lax.ppermute(mine, "xh", [(0, 1), (1, 0)])
    grad_qkv, grad_out = call(
        functools.partial(finish_kernel, factor), "finish",
        [sds(6, 3 * D, dtype=F32), sds(6, D, dtype=F32)], [at, mine, other], 1,
    )
    return out[None], dx[None], grad_qkv, grad_out, grad_gain, grad_bias


def solution(mesh):
    torus = Mesh(mesh.devices.reshape(4, 8, 2, 2, 2), ("y", "z", "xl", "c", "xh"))
    return jax.shard_map(
        on_device,
        mesh=torus,
        in_specs=(P("xh", SEQ, None), P("xh", SEQ, None), P(), P(), P(), P()),
        out_specs=(P("xh", SEQ, None), P("xh", SEQ, None), P(SEQ, None), P(SEQ, None), P(), P()),
        check_vma=False,
    )
```

```python
import functools

import jax
import jax.numpy as jnp
from jax import lax
from jax.experimental import pallas as pl
from jax.experimental.pallas import tpu as pltpu
from jax.sharding import Mesh
from jax.sharding import PartitionSpec as P

HEADS = 12
EPS = 1e-05
SEQ = ("y", "z", "xl", "c")
ROW = ("xl", "xh")
T = 256
D = 768
GROUPS = 3
GW = 256
BF = jnp.bfloat16
F32 = jnp.float32
LIMIT = 24


def nn(a, b):
    return lax.dot_general(a, b, (((1,), (0,)), ((), ())), preferred_element_type=F32)


def nt(a, b):
    return lax.dot_general(a, b, (((1,), (1,)), ((), ())), preferred_element_type=F32)


def eye(n):
    rows = lax.broadcasted_iota(jnp.int32, (n, n), 0)
    cols = lax.broadcasted_iota(jnp.int32, (n, n), 1)
    return jnp.where(rows == cols, 1.0, 0.0).astype(BF)


def layer_norm(x_ref, gain, bias):
    values = x_ref[...].astype(F32)
    centered = values - jnp.mean(values, axis=-1, keepdims=True)
    rstd = lax.rsqrt(jnp.mean(centered * centered, axis=-1, keepdims=True) + EPS)
    xhat = centered * rstd
    normed = (xhat * gain + bias).astype(BF)
    return normed, xhat, rstd


def row_order(at_ref):
    p = lax.broadcasted_iota(jnp.int32, (D, 1), 0)
    second = jnp.where(p >= 384, 1, 0)
    q = p - 384 * second
    owner = (q * 171) >> 13
    b = q - 48 * owner
    z = (b * 43) >> 8
    j = b - 6 * z
    y, xl = (owner >> 1) ^ at_ref[0], (owner & 1) ^ at_ref[1]
    to_core = jnp.where(second == 1, at_ref[2], 1 - at_ref[2])
    feature = ((y * 8 + z) * 2 + xl) * 12 + to_core * 6 + j
    cols = lax.broadcasted_iota(jnp.int32, (D, D), 1)
    return jnp.where(cols == feature, 1.0, 0.0).astype(BF)


def own_kernel(at_ref, gain_hbm, bias_hbm, x_hbm, cot_hbm, w_hbm, wo_hbm,
               qkv_ref, dmix_ref, npt_ref, xhat_ref, rstd_ref, mt_ref,
               gain_ref, bias_ref, x_ref, cot_ref, w_ref, wo_ref, sems):
    copies = [
        pltpu.make_async_copy(x_hbm, x_ref, sems.at[0]),
        pltpu.make_async_copy(gain_hbm, gain_ref, sems.at[1]),
        pltpu.make_async_copy(bias_hbm, bias_ref, sems.at[2]),
        pltpu.make_async_copy(cot_hbm, cot_ref, sems.at[3]),
        pltpu.make_async_copy(wo_hbm, wo_ref, sems.at[4]),
    ]
    for i in range(3):
        copies.append(pltpu.make_async_copy(w_hbm.at[:, pl.ds(D * i, D)], w_ref.at[i], sems.at[5 + i]))
    for copy in copies:
        copy.start()
    mt = row_order(at_ref)
    mt_ref[...] = mt
    for copy in copies[:3]:
        copy.wait()
    normed, xhat, rstd = layer_norm(x_ref, gain_ref[...].reshape(1, D), bias_ref[...].reshape(1, D))
    xhat_ref[...] = xhat
    rstd_ref[...] = jnp.broadcast_to(rstd, (T, 128))
    npt_ref[...] = nt(mt, normed).astype(BF)
    copies[3].wait()
    copies[4].wait()
    dmix_ref[...] = nt(cot_ref[...], wo_ref[...]).astype(BF)
    for i in range(3):
        copies[5 + i].wait()
        qkv_ref[:, D * i : D * i + D] = nn(normed, w_ref[i]).astype(BF)


def head_group(g, has, qkv_ref, kvm_ref, dmix_ref):
    at = GW * g
    lanes = lax.broadcasted_iota(jnp.int32, (T, 128), 1)
    low = lanes < 64
    causal = lax.broadcasted_iota(jnp.int32, (T, T), 0) <= lax.broadcasted_iota(jnp.int32, (T, T), 1)
    unit = eye(128)
    unit2 = eye(T)
    zero = jnp.zeros((), BF)
    mixts, dqs, dks, dvs = [], [], [], []
    for pair in range(2):
        cq = slice(at + 128 * pair, at + 128 * pair + 128)
        ck = slice(D + cq.start, D + cq.stop)
        cv = slice(2 * D + cq.start, 2 * D + cq.stop)
        q2 = (qkv_ref[:, cq].astype(F32) * 0.125).astype(BF)
        k2 = jnp.concatenate([qkv_ref[:, ck], kvm_ref[:, cq]], axis=0)
        v2 = jnp.concatenate([qkv_ref[:, cv], kvm_ref[:, ck]], axis=0)
        dm2 = dmix_ref[:, cq]
        kt2 = nt(unit, k2).astype(BF)
        vt2 = nt(unit, v2).astype(BF)
        ds_parts, p_parts, q_parts, dm_parts, dqt_parts = [], [], [], [], []
        for half in range(2):
            pick = low if half == 0 else jnp.logical_not(low)
            qa = jnp.where(pick, q2, zero)
            dma = jnp.where(pick, dm2, zero)
            st = nt(k2, qa)
            st_own = jnp.where(causal, st[:T], -1e30)
            st_mem = jnp.where(has, st[T:], -1e30)
            st = jnp.concatenate([st_own, st_mem], axis=0)
            top = jnp.max(st, axis=0, keepdims=True)
            e = jnp.exp(st - top)
            p = e * (1.0 / jnp.sum(e, axis=0, keepdims=True))
            pb = p.astype(BF)
            rows = slice(64 * half, 64 * half + 64)
            mixts.append(nn(vt2[rows], pb).astype(BF))
            dp = nt(v2, dma)
            ds = (p * (dp - jnp.sum(dp * p, axis=0, keepdims=True))).astype(BF)
            dqt_parts.append((nn(kt2[rows], ds) * 0.125).astype(BF))
            ds_parts.append(ds)
            p_parts.append(pb)
            q_parts.append(qa)
            dm_parts.append(dma)
        dks.append(nn(jnp.concatenate(ds_parts, axis=1), jnp.concatenate(q_parts, axis=0)).astype(BF))
        dvs.append(nn(jnp.concatenate(p_parts, axis=1), jnp.concatenate(dm_parts, axis=0)).astype(BF))
        dqs.append(nt(unit2, jnp.concatenate(dqt_parts, axis=0)).astype(BF))
    dq = jnp.concatenate(dqs, axis=1)
    dk = jnp.concatenate(dks, axis=1)
    dv = jnp.concatenate(dvs, axis=1)
    return jnp.concatenate(mixts, axis=0), dq, dk, dv


def put_rows(send_ref, keep_ref, slot, xh, lhs, rhs):
    first, second = rhs[:, :384], rhs[:, 384:]
    mine = xh == 0
    for r in range(2):
        part = jnp.where(mine, first, second) if r == 0 else jnp.where(mine, second, first)
        at = 768 * r + 384 * slot
        send_ref[:, at : at + 384] = nn(lhs[:384], part).astype(BF)
        keep_ref[:, at : at + 384] = nn(lhs[384:], part).astype(BF)


def group_outputs(g, slot, at_ref, npt_all, w_ref, grads, send_ref, keep_ref):
    dq, dk, dv = grads
    rhs = jnp.concatenate([jnp.concatenate([dq, jnp.zeros((T, GW), BF)], axis=0), dk, dv], axis=1)
    put_rows(send_ref, keep_ref, slot, at_ref[3], npt_all, rhs)
    wq, wk, wv = (w_ref[:, D * i + GW * g : D * i + GW * g + GW] for i in range(3))
    own = nt(dq, wq) + nt(dk[:T], wk) + nt(dv[:T], wv)
    mem = nt(dk[T:], wk) + nt(dv[T:], wv)
    return own, mem


def first_kernel(at_ref, gain_ref, bias_ref, xp_ref, w_ref, mt_ref, qkv_ref, dmix_ref, npt_ref,
                 send_ref, keep_ref, mixt_ref, dn_ref, dnm_ref, kvm_ref, npt_all_ref, xhatm_ref):
    normed, xhat, _ = layer_norm(xp_ref, gain_ref[...].reshape(1, D), bias_ref[...].reshape(1, D))
    kvm_ref[...] = nn(normed, w_ref[:, D:]).astype(BF)
    xhatm_ref[...] = xhat
    npt_all_ref[:, :T] = npt_ref[...]
    npt_all_ref[:, T:] = nt(mt_ref[...], normed).astype(BF)
    has = at_ref[4] > 0
    npt_all = npt_all_ref[...]
    for g in range(2):
        mixt, *grads = head_group(g, has, qkv_ref, kvm_ref, dmix_ref)
        mixt_ref[GW * g : GW * g + GW, :] = mixt
        own, mem = group_outputs(g, g, at_ref, npt_all, w_ref, grads, send_ref, keep_ref)
        if g == 0:
            dn_ref[...] = own
            dnm_ref[...] = mem
        else:
            dn_ref[...] += own
            dnm_ref[...] += mem


def second_kernel(at_ref, w_ref, mt_ref, cot_ref, qkv_ref, dmix_ref, mixt_in, dn_in, dnm_in, kvm_ref, npt_all_ref,
                  xhat_ref, xhatm_ref, send_ref, keep_ref, vec_ref, mixt_ref, dn_ref):
    mixt, *grads = head_group(2, at_ref[4] > 0, qkv_ref, kvm_ref, dmix_ref)
    mixt_ref[: 2 * GW, :] = mixt_in[...]
    mixt_ref[2 * GW :, :] = mixt
    own, mem = group_outputs(2, 0, at_ref, npt_all_ref[...], w_ref, grads, send_ref, keep_ref)
    lhs = nn(mt_ref[...], mixt_ref[...]).astype(BF)
    put_rows(send_ref, keep_ref, 1, at_ref[3], lhs, cot_ref[...])
    dn, dnm = dn_in[...] + own, dnm_in[...] + mem
    dn_ref[...] = dn
    vec_ref[0:1, :] = jnp.sum(dn * xhat_ref[...] + dnm * xhatm_ref[...], axis=0, keepdims=True)
    vec_ref[1:2, :] = jnp.sum(dn + dnm, axis=0, keepdims=True)


def token_kernel(gain_ref, x_ref, cot_ref, mixt_ref, wo_ref, dn_ref, xhat_ref, rstd_ref, out_ref, dx_ref):
    mixed = nt(eye(T), mixt_ref[...]).astype(BF)
    out_ref[...] = (x_ref[...].astype(F32) + nn(mixed, wo_ref[...])).astype(BF)
    d_hat = dn_ref[...] * gain_ref[...].reshape(1, D)
    xhat = xhat_ref[...]
    row = rstd_ref[:, 0:1] * (
        d_hat
        - jnp.mean(d_hat, axis=-1, keepdims=True)
        - xhat * jnp.mean(d_hat * xhat, axis=-1, keepdims=True)
    )
    dx_ref[...] = (cot_ref[...].astype(F32) + row).astype(BF)


def split_rows(value):
    high = value.astype(BF)
    low = (value - high.astype(F32)).astype(BF)
    return jnp.concatenate([high, low, jnp.zeros((4, value.shape[1]), BF)], axis=0)


def join_rows(rows):
    return rows[0:2].astype(F32) + rows[2:4].astype(F32)


def tree(a, b, c, d):
    return (a.astype(F32) + b.astype(F32)) + (c.astype(F32) + d.astype(F32))


def pair_a_kernel(keep_ref, recv_ref, *outs):
    for k in range(4):
        rows = slice(96 * k, 96 * k + 96)
        outs[k][...] = (keep_ref[rows, :].astype(F32) + recv_ref[rows, :].astype(F32)).astype(BF)


def pair_b_kernel(keep_ref, recv_ref, vec_ref, vecr_ref, *outs):
    vec = split_rows(vec_ref[...] + vecr_ref[...])
    for k in range(4):
        cols = slice(768 * (k & 1), 768 * (k & 1) + 768)
        for y in range(4):
            rows = slice(96 * y + 48 * (k >> 1), 96 * y + 48 * (k >> 1) + 48)
            outs[k][48 * y : 48 * y + 48, :] = (
                keep_ref[rows, cols].astype(F32) + recv_ref[rows, cols].astype(F32)
            ).astype(BF)
        outs[k][192:200, :] = vec


def mid_a_kernel(a, b, c, d, *outs):
    for k in range(4):
        rows = slice(48 * (k >> 1), 48 * (k >> 1) + 48)
        cols = slice(768 * (k & 1), 768 * (k & 1) + 768)
        outs[k][...] = tree(a[rows, cols], b[rows, cols], c[rows, cols], d[rows, cols]).astype(BF)


def mid_b_kernel(a, b, c, d, *outs):
    vec = split_rows((join_rows(a[192:200]) + join_rows(b[192:200])) + (join_rows(c[192:200]) + join_rows(d[192:200])))
    for k in range(4):
        rows = slice(48 * k, 48 * k + 48)
        outs[k][0:48, :] = tree(a[rows], b[rows], c[rows], d[rows]).astype(BF)
        outs[k][48:56, :] = vec


def plane_kernel(a0, a1, a2, a3, b0, b1, b2, b3, out_ref):
    at = slice(48, 56)
    vec = (join_rows(b0[at]) + join_rows(b1[at])) + (join_rows(b2[at]) + join_rows(b3[at]))
    vec = jnp.concatenate([vec[0:1], vec[1:2]], axis=1)
    high = vec.astype(BF).astype(F32)
    tail = jnp.concatenate([high, vec - high], axis=0)
    g = slice(0, 48)
    sums = jnp.concatenate([tree(a0[...], a1[...], a2[...], a3[...]), tree(b0[g], b1[g], b2[g], b3[g])], axis=1)
    for z in range(8):
        out_ref[z] = jnp.concatenate([sums[6 * z : 6 * z + 6], tail], axis=0).astype(BF)


def column_kernel(factor, in_ref, rows_ref, gain_ref, bias_ref):
    acc = in_ref[0].astype(F32)
    for z in range(1, 8):
        acc = acc + in_ref[z].astype(F32)
    rows_ref[...] = acc.astype(BF)
    vec = (acc[6:7] + acc[7:8]) * factor
    gain_ref[...] = vec[:, :D].reshape(D)
    bias_ref[...] = vec[:, D:].reshape(D)


def finish_kernel(factor, at_ref, mine_ref, other_ref, qkv_ref, wout_ref):
    mine, other = mine_ref[...].astype(F32) * factor, other_ref[...].astype(F32) * factor
    first = at_ref[3] == 0
    halves = [jnp.where(first, mine, other), jnp.where(first, other, mine)]
    for g in range(GROUPS + 1):
        cols = slice(384 * g, 384 * g + 384)
        full = jnp.concatenate([halves[0][0:6, cols], halves[1][0:6, cols]], axis=1)
        if g < GROUPS:
            for i in range(3):
                at = D * i + GW * g
                qkv_ref[:, at : at + GW] = full[:, GW * i : GW * i + GW]
        else:
            wout_ref[...] = full


VM = pl.BlockSpec(memory_space=pltpu.VMEM)
SM = pl.BlockSpec(memory_space=pltpu.SMEM)
HBM = pl.BlockSpec(memory_space=pltpu.MemorySpace.HBM)


def call(kernel, name, out_shape, args, scalars=0, anys=(), scratch=(), limit=16):
    specs = [SM if i < scalars else HBM if i in anys else VM for i in range(len(args))]
    args = [pltpu.with_memory_space_constraint(a, pltpu.MemorySpace.HBM) if i in anys else a for i, a in enumerate(args)]
    return pl.pallas_call(
        kernel,
        name=name,
        in_specs=specs,
        out_specs=[VM] * len(out_shape),
        out_shape=out_shape,
        scratch_shapes=scratch,
        compiler_params=pltpu.CompilerParams(vmem_limit_bytes=limit * 1024 * 1024),
    )(*args)


def sds(*shape, dtype=BF):
    return jax.ShapeDtypeStruct(shape, dtype)


def on_device(layer_input, cotangent, gain, bias, w, wo):
    x, cot = layer_input[0], cotangent[0]
    seq = lax.axis_size(SEQ)
    xp = lax.ppermute(x, SEQ, [(i, i + 1) for i in range(seq - 1)])
    place = [lax.axis_index(n) for n in ("y", "xl", "c", "xh")] + [lax.axis_index(SEQ) > 0]
    at = jnp.stack([v.astype(jnp.int32) for v in place])
    row, mat, tokens = sds(T, D, dtype=F32), sds(D, D), sds(T, D)
    one = pltpu.VMEM((D,), F32)
    qkv, dmix, npt, xhat, rstd, mt = call(
        own_kernel, "own_part",
        [sds(T, 3 * D), tokens, sds(D, T), row, sds(T, 128, dtype=F32), mat],
        [at, gain, bias, x, cot, w, wo], 1, (1, 2, 3, 4, 5, 6),
        [one, one, pltpu.VMEM((T, D), BF), pltpu.VMEM((T, D), BF), pltpu.VMEM((3, D, D), BF), pltpu.VMEM((D, D), BF),
         pltpu.SemaphoreType.DMA((8,))],
    )
    wide = sds(384, 1536)
    send_a, keep_a, mixt, dn, dnm, kvm, npt_all, xhatm = call(
        first_kernel, "memory_and_heads",
        [wide, wide, sds(2 * GW, T), row, row, sds(T, 2 * D), sds(D, 2 * T), row],
        [at, gain, bias, xp, w, mt, qkv, dmix, npt], 1, limit=LIMIT,
    )
    send_b, keep_b, vec, mixt, dn = call(
        second_kernel, "heads_and_output_weight",
        [wide, wide, sds(2, D, dtype=F32), sds(D, T), row],
        [at, w, mt, cot, qkv, dmix, mixt, dn, dnm, kvm, npt_all, xhat, xhatm], 1, limit=LIMIT,
    )

    def swap(block):
        return lax.ppermute(block, "c", [(0, 1), (1, 0)])

    def exchange(parts, axes):
        n = lax.axis_size(axes)
        return [parts[0]] + [lax.ppermute(parts[k], axes, [(i, i ^ k) for i in range(n)]) for k in (1, 3, 2)]

    def ordered(parts):
        own, one, three, two = parts
        return [own, one, two, three]

    parts_a = call(pair_a_kernel, "pair_sum_a", [sds(96, 1536)] * 4, [keep_a, swap(send_a)])
    parts_b = call(pair_b_kernel, "pair_sum_b", [sds(200, 768)] * 4, [keep_b, swap(send_b), vec, swap(vec)])
    parts_a = ordered(exchange(parts_a, "y"))
    parts_b = ordered(exchange(parts_b, ROW))
    out, dx = call(
        token_kernel, "token_outputs", [tokens, tokens],
        [gain, x, cot, mixt, wo, dn, xhat, rstd],
    )
    parts_a = call(mid_a_kernel, "middle_sum_a", [sds(48, 768)] * 4, parts_a)
    parts_b = call(mid_b_kernel, "middle_sum_b", [sds(56, 768)] * 4, parts_b)
    parts_a = ordered(exchange(parts_a, ROW))
    parts_b = ordered(exchange(parts_b, "y"))
    (mine,) = call(plane_kernel, "plane_sum", [sds(8, 8, 1536)], [*parts_a, *parts_b])
    mine = lax.all_to_all(mine, "z", 0, 0, tiled=True)
    factor = 1.0 / float(seq * lax.axis_size("xh") * T) ** 0.5
    mine, grad_gain, grad_bias = call(
        functools.partial(column_kernel, factor), "column_sum",
        [sds(8, 1536), sds(D, dtype=F32), sds(D, dtype=F32)], [mine],
    )
    other = lax.ppermute(mine, "xh", [(0, 1), (1, 0)])
    grad_qkv, grad_out = call(
        functools.partial(finish_kernel, factor), "finish",
        [sds(6, 3 * D, dtype=F32), sds(6, D, dtype=F32)], [at, mine, other], 1,
    )
    return out[None], dx[None], grad_qkv, grad_out, grad_gain, grad_bias


def solution(mesh):
    torus = Mesh(mesh.devices.reshape(4, 8, 2, 2, 2), ("y", "z", "xl", "c", "xh"))
    return jax.shard_map(
        on_device,
        mesh=torus,
        in_specs=(P("xh", SEQ, None), P("xh", SEQ, None), P(), P(), P(), P()),
        out_specs=(P("xh", SEQ, None), P("xh", SEQ, None), P(SEQ, None), P(SEQ, None), P(), P()),
        check_vma=False,
    )
```

```python
import functools

import jax
import jax.numpy as jnp
from jax import lax
from jax.experimental import pallas as pl
from jax.experimental.pallas import tpu as pltpu
from jax.sharding import Mesh
from jax.sharding import PartitionSpec as P

HEADS = 12
EPS = 1e-05
SEQ = ("y", "z", "xl", "c")
PLANE = ("y", "xl", "xh")
T = 256
D = 768
GROUPS = 3
GW = 256
BF = jnp.bfloat16
F32 = jnp.float32
LIMIT = 32


def nn(a, b):
    return lax.dot_general(a, b, (((1,), (0,)), ((), ())), preferred_element_type=F32)


def nt(a, b):
    return lax.dot_general(a, b, (((1,), (1,)), ((), ())), preferred_element_type=F32)


def eye(n):
    rows = lax.broadcasted_iota(jnp.int32, (n, n), 0)
    cols = lax.broadcasted_iota(jnp.int32, (n, n), 1)
    return jnp.where(rows == cols, 1.0, 0.0).astype(BF)


def layer_norm(x_ref, gain, bias):
    values = x_ref[...].astype(F32)
    centered = values - jnp.mean(values, axis=-1, keepdims=True)
    rstd = lax.rsqrt(jnp.mean(centered * centered, axis=-1, keepdims=True) + EPS)
    xhat = centered * rstd
    normed = (xhat * gain + bias).astype(BF)
    return normed, xhat, rstd


def row_order(at_ref):
    p = lax.broadcasted_iota(jnp.int32, (D, 1), 0)
    second = jnp.where(p >= 384, 1, 0)
    q = p - 384 * second
    owner = (q * 171) >> 13
    b = q - 48 * owner
    z = (b * 43) >> 8
    j = b - 6 * z
    y, xl = owner >> 1, owner & 1
    to_core = jnp.where(second == 1, at_ref[0], 1 - at_ref[0])
    feature = ((y * 8 + z) * 2 + xl) * 12 + to_core * 6 + j
    cols = lax.broadcasted_iota(jnp.int32, (D, D), 1)
    return jnp.where(cols == feature, 1.0, 0.0).astype(BF)


def own_kernel(at_ref, gain_hbm, bias_hbm, x_hbm, cot_hbm, w_hbm, wo_hbm,
               qkv_ref, dmix_ref, npt_ref, mt_ref, xhat_hbm, rstd_hbm,
               gain_ref, bias_ref, x_ref, cot_ref, w_ref, wo_ref, xhat_ref, rstd_ref, sems):
    copies = [
        pltpu.make_async_copy(x_hbm, x_ref, sems.at[0]),
        pltpu.make_async_copy(gain_hbm, gain_ref, sems.at[1]),
        pltpu.make_async_copy(bias_hbm, bias_ref, sems.at[2]),
        pltpu.make_async_copy(cot_hbm, cot_ref, sems.at[3]),
        pltpu.make_async_copy(wo_hbm, wo_ref, sems.at[4]),
    ]
    for i in range(3):
        copies.append(pltpu.make_async_copy(w_hbm.at[:, pl.ds(D * i, D)], w_ref.at[i], sems.at[5 + i]))
    for copy in copies:
        copy.start()
    mt = row_order(at_ref)
    mt_ref[...] = mt
    for copy in copies[:3]:
        copy.wait()
    normed, xhat, rstd = layer_norm(x_ref, gain_ref[...].reshape(1, D), bias_ref[...].reshape(1, D))
    xhat_ref[...] = xhat
    rstd_ref[...] = jnp.broadcast_to(rstd, (T, 128))
    stores = [
        pltpu.make_async_copy(xhat_ref, xhat_hbm, sems.at[8]),
        pltpu.make_async_copy(rstd_ref, rstd_hbm, sems.at[9]),
    ]
    for copy in stores:
        copy.start()
    npt_ref[...] = nt(mt, normed).astype(BF)
    copies[3].wait()
    copies[4].wait()
    dmix_ref[...] = nt(cot_ref[...], wo_ref[...]).astype(BF)
    for i in range(3):
        copies[5 + i].wait()
        qkv_ref[:, D * i : D * i + D] = nn(normed, w_ref[i]).astype(BF)
    for copy in stores:
        copy.wait()


def qkv_slices(qkv_ref, kvm_ref, dmix_ref, g):
    tiles = []
    for pair in range(2):
        at = GW * g + 128 * pair
        q, k, v = (slice(D * i + at, D * i + at + 128) for i in range(3))
        tiles.append((qkv_ref[:, q], qkv_ref[:, k], qkv_ref[:, v], kvm_ref[:, q], kvm_ref[:, k], dmix_ref[:, q]))
    return tiles


def head_group(tiles, has):
    lanes = lax.broadcasted_iota(jnp.int32, (T, 128), 1)
    low = lanes < 64
    causal = lax.broadcasted_iota(jnp.int32, (T, T), 0) <= lax.broadcasted_iota(jnp.int32, (T, T), 1)
    unit = eye(128)
    unit2 = eye(T)
    zero = jnp.zeros((), BF)
    mixts, dqs, dks, dvs = [], [], [], []
    for q2, k2, v2, km2, vm2, dm2 in tiles:
        q2 = (q2.astype(F32) * 0.125).astype(BF)
        k2 = jnp.concatenate([k2, km2], axis=0)
        v2 = jnp.concatenate([v2, vm2], axis=0)
        kt2 = nt(unit, k2).astype(BF)
        vt2 = nt(unit, v2).astype(BF)
        ds_parts, p_parts, q_parts, dm_parts, dqt_parts = [], [], [], [], []
        for half in range(2):
            pick = low if half == 0 else jnp.logical_not(low)
            qa = jnp.where(pick, q2, zero)
            dma = jnp.where(pick, dm2, zero)
            st = nt(k2, qa)
            st_own = jnp.where(causal, st[:T], -1e30)
            st_mem = jnp.where(has, st[T:], -1e30)
            st = jnp.concatenate([st_own, st_mem], axis=0)
            top = jnp.max(st, axis=0, keepdims=True)
            e = jnp.exp(st - top)
            p = e * (1.0 / jnp.sum(e, axis=0, keepdims=True))
            pb = p.astype(BF)
            rows = slice(64 * half, 64 * half + 64)
            mixts.append(nn(vt2[rows], pb).astype(BF))
            dp = nt(v2, dma)
            ds = (p * (dp - jnp.sum(dp * p, axis=0, keepdims=True))).astype(BF)
            dqt_parts.append((nn(kt2[rows], ds) * 0.125).astype(BF))
            ds_parts.append(ds)
            p_parts.append(pb)
            q_parts.append(qa)
            dm_parts.append(dma)
        dks.append(nn(jnp.concatenate(ds_parts, axis=1), jnp.concatenate(q_parts, axis=0)).astype(BF))
        dvs.append(nn(jnp.concatenate(p_parts, axis=1), jnp.concatenate(dm_parts, axis=0)).astype(BF))
        dqs.append(nt(unit2, jnp.concatenate(dqt_parts, axis=0)).astype(BF))
    dq = jnp.concatenate(dqs, axis=1)
    dk = jnp.concatenate(dks, axis=1)
    dv = jnp.concatenate(dvs, axis=1)
    return jnp.concatenate(mixts, axis=0), dq, dk, dv


def put_rows(send_ref, keep_ref, slot, lhs, rhs):
    for h in range(2):
        part = rhs[:, 384 * h : 384 * h + 384]
        for k, out_ref in enumerate((send_ref, keep_ref)):
            rows = nn(lhs[384 * k : 384 * k + 384], part).astype(BF)
            for i in range(8):
                out_ref[2 * i + h, :, 384 * slot : 384 * slot + 384] = rows[48 * i : 48 * i + 48]


def put_group(slot, npt_all, grads, send_ref, keep_ref):
    dq, dk, dv = grads
    rhs = jnp.concatenate([jnp.concatenate([dq, jnp.zeros((T, GW), BF)], axis=0), dk, dv], axis=1)
    put_rows(send_ref, keep_ref, slot, npt_all, rhs)


def d_normed(wq, wk, wv, dq, dk, dv):
    own = nt(dq, wq) + nt(dk[:T], wk) + nt(dv[:T], wv)
    mem = nt(dk[T:], wk) + nt(dv[T:], wv)
    return own, mem


def first_kernel(at_ref, gain_ref, bias_ref, xp_ref, w_ref, mt_ref, qkv_ref, dmix_ref, npt_ref,
                 send_ref, keep_ref, dq_ref, dkv_ref, mixt_hbm, kvm_hbm, npt_hbm, xhatm_hbm,
                 mixt_ref, kvm_ref, npt_all_ref, xhatm_ref, sems):
    normed, xhat, _ = layer_norm(xp_ref, gain_ref[...].reshape(1, D), bias_ref[...].reshape(1, D))
    kvm_ref[...] = nn(normed, w_ref[:, D:]).astype(BF)
    xhatm_ref[...] = xhat
    npt_all_ref[:, :T] = npt_ref[...]
    npt_all_ref[:, T:] = nt(mt_ref[...], normed).astype(BF)
    copies = [
        pltpu.make_async_copy(kvm_ref, kvm_hbm, sems.at[0]),
        pltpu.make_async_copy(npt_all_ref, npt_hbm, sems.at[1]),
        pltpu.make_async_copy(xhatm_ref, xhatm_hbm, sems.at[2]),
    ]
    for copy in copies:
        copy.start()
    has = at_ref[2] > 0
    npt_all = npt_all_ref[...]
    for g in range(2):
        mixt, dq, dk, dv = head_group(qkv_slices(qkv_ref, kvm_ref, dmix_ref, g), has)
        mixt_ref[GW * g : GW * g + GW, :] = mixt
        if g == 1:
            copies.append(pltpu.make_async_copy(mixt_ref, mixt_hbm, sems.at[3]))
            copies[3].start()
        dq_ref[:, GW * g : GW * g + GW] = dq
        dkv_ref[:, GW * g : GW * g + GW] = dk
        dkv_ref[:, GW * (g + 2) : GW * (g + 2) + GW] = dv
        put_group(g, npt_all, (dq, dk, dv), send_ref, keep_ref)
    for copy in copies:
        copy.wait()


def d_normed_kernel(w_ref, dq_ref, dkv_ref, dn_hbm, dnm_hbm, dn_ref, dnm_ref, sems):
    own, mem = None, None
    for g in range(2):
        cols, vcols = slice(GW * g, GW * g + GW), slice(GW * (g + 2), GW * (g + 2) + GW)
        wq, wk, wv = (w_ref[:, D * i + GW * g : D * i + GW * g + GW] for i in range(3))
        a, b = d_normed(wq, wk, wv, dq_ref[:, cols], dkv_ref[:, cols], dkv_ref[:, vcols])
        own, mem = (a, b) if own is None else (own + a, mem + b)
    dn_ref[...] = own
    dnm_ref[...] = mem
    copies = [pltpu.make_async_copy(dn_ref, dn_hbm, sems.at[0]), pltpu.make_async_copy(dnm_ref, dnm_hbm, sems.at[1])]
    for copy in copies:
        copy.start()
    for copy in copies:
        copy.wait()


def second_kernel(at_ref, qkv_hbm, kvm_hbm, dmix_hbm, npt_hbm, mt_hbm, mixt_hbm, cot_hbm, w_hbm, dn_hbm, dnm_hbm,
                  xhat_hbm, xhatm_hbm, send_ref, keep_ref, vec_ref, mixt_ref, dn_ref,
                  q_ref, k_ref, v_ref, km_ref, vm_ref, dm_ref, npt_ref, mt_ref, cot_ref, wq_ref, wk_ref, wv_ref,
                  dnin_ref, dnmin_ref, xhat_ref, xhatm_ref, sems):
    last = 2 * GW
    col = lambda ref, i: ref.at[:, pl.ds(D * i + last, GW)]
    pairs = [
        (col(qkv_hbm, 0), q_ref), (col(qkv_hbm, 1), k_ref), (col(qkv_hbm, 2), v_ref),
        (col(kvm_hbm, 0), km_ref), (col(kvm_hbm, 1), vm_ref), (col(dmix_hbm, 0), dm_ref),
        (npt_hbm, npt_ref), (mt_hbm, mt_ref), (mixt_hbm, mixt_ref.at[pl.ds(0, last), :]), (cot_hbm, cot_ref),
        (col(w_hbm, 0), wq_ref), (col(w_hbm, 1), wk_ref), (col(w_hbm, 2), wv_ref),
        (dn_hbm, dnin_ref), (dnm_hbm, dnmin_ref), (xhat_hbm, xhat_ref), (xhatm_hbm, xhatm_ref),
    ]
    copies = [pltpu.make_async_copy(src, dst, sems.at[i]) for i, (src, dst) in enumerate(pairs)]
    for copy in copies:
        copy.start()
    for copy in copies[:6]:
        copy.wait()
    tiles = [tuple(ref[:, 128 * i : 128 * i + 128] for ref in (q_ref, k_ref, v_ref, km_ref, vm_ref, dm_ref)) for i in range(2)]
    mixt, *grads = head_group(tiles, at_ref[2] > 0)
    mixt_ref[last:, :] = mixt
    copies[6].wait()
    put_group(0, npt_ref[...], grads, send_ref, keep_ref)
    for copy in copies[7:10]:
        copy.wait()
    lhs = nn(mt_ref[...], mixt_ref[...]).astype(BF)
    put_rows(send_ref, keep_ref, 1, lhs, cot_ref[...])
    for copy in copies[10:]:
        copy.wait()
    own, mem = d_normed(wq_ref[...], wk_ref[...], wv_ref[...], *grads)
    dn, dnm = dnin_ref[...] + own, dnmin_ref[...] + mem
    dn_ref[...] = dn
    vec_ref[0:1, :] = jnp.sum(dn * xhat_ref[...] + dnm * xhatm_ref[...], axis=0, keepdims=True)
    vec_ref[1:2, :] = jnp.sum(dn + dnm, axis=0, keepdims=True)


def token_kernel(gain_ref, x_ref, cot_ref, mixt_ref, wo_ref, dn_ref, xhat_ref, rstd_ref, out_ref, dx_ref):
    mixed = nt(eye(T), mixt_ref[...]).astype(BF)
    out_ref[...] = (x_ref[...].astype(F32) + nn(mixed, wo_ref[...])).astype(BF)
    d_hat = dn_ref[...] * gain_ref[...].reshape(1, D)
    xhat = xhat_ref[...]
    row = rstd_ref[:, 0:1] * (
        d_hat
        - jnp.mean(d_hat, axis=-1, keepdims=True)
        - xhat * jnp.mean(d_hat * xhat, axis=-1, keepdims=True)
    )
    dx_ref[...] = (cot_ref[...].astype(F32) + row).astype(BF)


def split_rows(value):
    high = value.astype(BF)
    low = (value - high.astype(F32)).astype(BF)
    return jnp.concatenate([high, low, jnp.zeros((4, value.shape[1]), BF)], axis=0)


def join_rows(rows):
    return rows[0:2].astype(F32) + rows[2:4].astype(F32)


def pair_a_kernel(keep_ref, recv_ref, out_ref):
    out_ref[...] = (keep_ref[...].astype(F32) + recv_ref[...].astype(F32)).astype(BF)


def pair_b_kernel(keep_ref, recv_ref, vec_ref, vecr_ref, out_ref):
    vec = split_rows(vec_ref[...] + vecr_ref[...])
    out_ref[:, 0:48, :] = (keep_ref[...].astype(F32) + recv_ref[...].astype(F32)).astype(BF)
    for i in range(16):
        out_ref[i, 48:56, :] = vec


def plane_kernel(a_hbm, b_ref, out_ref, a_ref, sem):
    load = pltpu.make_async_copy(a_hbm, a_ref, sem)
    load.start()
    vec = join_rows(b_ref[0, 48:56, :])
    for i in range(1, 16):
        vec = vec + join_rows(b_ref[i, 48:56, :])
    vec = jnp.concatenate([vec[0:1], vec[1:2]], axis=1)
    high = vec.astype(BF).astype(F32)
    tail = jnp.concatenate([high, vec - high], axis=0)
    acc = b_ref[0, 0:48, :].astype(F32)
    for i in range(1, 16):
        acc = acc + b_ref[i, 0:48, :].astype(F32)
    load.wait()
    for k, half in enumerate((a_ref[0].astype(F32), acc)):
        cols = slice(768 * k, 768 * k + 768)
        for z in range(8):
            out_ref[z, :, cols] = jnp.concatenate([half[6 * z : 6 * z + 6], tail[:, cols]], axis=0).astype(BF)


def column_kernel(factor, in_ref, rows_ref, gain_ref, bias_ref):
    acc = in_ref[0].astype(F32)
    for z in range(1, 8):
        acc = acc + in_ref[z].astype(F32)
    rows_ref[...] = acc.astype(BF)
    vec = (acc[6:7] + acc[7:8]) * factor
    gain_ref[...] = vec[:, :D].reshape(D)
    bias_ref[...] = vec[:, D:].reshape(D)


def finish_kernel(factor, at_ref, mine_ref, other_ref, qkv_ref, wout_ref):
    mine, other = mine_ref[...].astype(F32) * factor, other_ref[...].astype(F32) * factor
    first = at_ref[1] == 0
    halves = [jnp.where(first, mine, other), jnp.where(first, other, mine)]
    for g in range(GROUPS + 1):
        cols = slice(384 * g, 384 * g + 384)
        full = jnp.concatenate([halves[0][0:6, cols], halves[1][0:6, cols]], axis=1)
        if g < GROUPS:
            for i in range(3):
                at = D * i + GW * g
                qkv_ref[:, at : at + GW] = full[:, GW * i : GW * i + GW]
        else:
            wout_ref[...] = full


VM = pl.BlockSpec(memory_space=pltpu.VMEM)
SM = pl.BlockSpec(memory_space=pltpu.SMEM)
HBM = pl.BlockSpec(memory_space=pltpu.MemorySpace.HBM)


def call(kernel, name, out_shape, args, scalars=0, hbm=(), hbm_outs=(), scratch=(), limit=16):
    args = [pltpu.with_memory_space_constraint(a, pltpu.MemorySpace.HBM) if i in hbm else a for i, a in enumerate(args)]
    return pl.pallas_call(
        kernel,
        name=name,
        in_specs=[SM if i < scalars else HBM if i in hbm else VM for i in range(len(args))],
        out_specs=[HBM if i in hbm_outs else VM for i in range(len(out_shape))],
        out_shape=[pltpu.MemorySpace.HBM(o.shape, o.dtype) if i in hbm_outs else o for i, o in enumerate(out_shape)],
        scratch_shapes=scratch,
        compiler_params=pltpu.CompilerParams(vmem_limit_bytes=limit * 1024 * 1024),
    )(*args)


def vmem(*shape, dtype=BF):
    return pltpu.VMEM(shape, dtype)


def dmas(n):
    return pltpu.SemaphoreType.DMA((n,))


def sds(*shape, dtype=BF):
    return jax.ShapeDtypeStruct(shape, dtype)


def on_device(layer_input, cotangent, gain, bias, w, wo):
    x, cot = layer_input[0], cotangent[0]
    seq = lax.axis_size(SEQ)
    xp = lax.ppermute(x, SEQ, [(i, i + 1) for i in range(seq - 1)])
    place = [lax.axis_index("c"), lax.axis_index("xh"), lax.axis_index(SEQ) > 0]
    at = jnp.stack([v.astype(jnp.int32) for v in place])
    row, mat, tokens = sds(T, D, dtype=F32), sds(D, D), sds(T, D)
    one, tile, mat_v, row_v = vmem(D, dtype=F32), vmem(T, GW), vmem(D, D), vmem(T, D, dtype=F32)
    qkv, dmix, npt, mt, xhat, rstd = call(
        own_kernel, "own_part",
        [sds(T, 3 * D), tokens, sds(D, T), mat, row, sds(T, 128, dtype=F32)],
        [at, gain, bias, x, cot, w, wo], 1, range(1, 7), (4, 5),
        [one, one, vmem(T, D), vmem(T, D), vmem(3, D, D), mat_v, row_v, vmem(T, 128, dtype=F32), dmas(10)],
    )
    wide = sds(16, 48, 768)
    send_a, keep_a, dq, dkv, mixt, kvm, npt_all, xhatm = call(
        first_kernel, "memory_and_heads",
        [wide, wide, sds(T, 2 * GW), sds(2 * T, 4 * GW), sds(2 * GW, T), sds(T, 2 * D), sds(D, 2 * T), row],
        [at, gain, bias, xp, w, mt, qkv, dmix, npt], 1, hbm_outs=range(4, 8),
        scratch=[vmem(2 * GW, T), vmem(T, 2 * D), vmem(D, 2 * T), row_v, dmas(4)], limit=LIMIT,
    )

    def swap(block):
        return lax.ppermute(block, "c", [(0, 1), (1, 0)])

    def spread(block):
        return lax.all_to_all(block, PLANE, 0, 0, tiled=True)

    dn, dnm = call(
        d_normed_kernel, "d_normed", [row, row], [w, dq, dkv], hbm_outs=(0, 1), scratch=[row_v, row_v, dmas(2)],
    )
    (parts_a,) = call(pair_a_kernel, "pair_sum_a", [wide], [keep_a, swap(send_a)])
    parts_a, kvm, dn, dnm = lax.optimization_barrier((parts_a, kvm, dn, dnm))
    parts_a = lax.psum_scatter(parts_a, "y", scatter_dimension=0, tiled=True)
    parts_a = lax.psum_scatter(parts_a, ("xl", "xh"), scatter_dimension=0, tiled=True)
    send_b, keep_b, vec, mixt, dn = call(
        second_kernel, "heads_and_output_weight",
        [wide, wide, sds(2, D, dtype=F32), sds(D, T), row],
        [at, qkv, kvm, dmix, npt_all, mt, mixt, cot, w, dn, dnm, xhat, xhatm], 1, range(1, 13),
        scratch=[tile] * 6 + [vmem(D, 2 * T), mat_v, vmem(T, D)] + [vmem(D, GW)] * 3 + [row_v] * 4 + [dmas(17)], limit=LIMIT,
    )
    (parts_b,) = call(pair_b_kernel, "pair_sum_b", [sds(16, 56, 768)], [keep_b, swap(send_b), vec, swap(vec)])
    out, dx = call(
        token_kernel, "token_outputs", [tokens, tokens],
        [gain, x, cot, mixt, wo, dn, xhat, rstd],
    )
    parts_b, out, dx = lax.optimization_barrier((parts_b, out, dx))
    parts_b = spread(parts_b)
    (mine,) = call(plane_kernel, "plane_sum", [sds(8, 8, 1536)], [parts_a, parts_b], hbm=(0,), scratch=[vmem(1, 48, 768), pltpu.SemaphoreType.DMA])
    mine = lax.all_to_all(mine, "z", 0, 0, tiled=True)
    factor = 1.0 / float(seq * lax.axis_size("xh") * T) ** 0.5
    mine, grad_gain, grad_bias = call(
        functools.partial(column_kernel, factor), "column_sum",
        [sds(8, 1536), sds(D, dtype=F32), sds(D, dtype=F32)], [mine],
    )
    other = lax.ppermute(mine, "xh", [(0, 1), (1, 0)])
    grad_qkv, grad_out = call(
        functools.partial(finish_kernel, factor), "finish",
        [sds(6, 3 * D, dtype=F32), sds(6, D, dtype=F32)], [at, mine, other], 1,
    )
    return out[None], dx[None], grad_qkv, grad_out, grad_gain, grad_bias


def solution(mesh):
    torus = Mesh(mesh.devices.reshape(4, 8, 2, 2, 2), ("y", "z", "xl", "c", "xh"))
    return jax.shard_map(
        on_device,
        mesh=torus,
        in_specs=(P("xh", SEQ, None), P("xh", SEQ, None), P(), P(), P(), P()),
        out_specs=(P("xh", SEQ, None), P("xh", SEQ, None), P(SEQ, None), P(SEQ, None), P(), P()),
        check_vma=False,
    )
```

```python
import functools

import jax
import jax.numpy as jnp
from jax import lax
from jax.experimental import pallas as pl
from jax.experimental.pallas import tpu as pltpu
from jax.sharding import Mesh
from jax.sharding import PartitionSpec as P

HEADS = 12
EPS = 1e-05
SEQ = ("y", "z", "xl", "c")
ROW = ("xl", "xh")
T = 256
D = 768
GROUPS = 3
GW = 256
BF = jnp.bfloat16
F32 = jnp.float32
LIMIT = 24


def nn(a, b):
    return lax.dot_general(a, b, (((1,), (0,)), ((), ())), preferred_element_type=F32)


def nt(a, b):
    return lax.dot_general(a, b, (((1,), (1,)), ((), ())), preferred_element_type=F32)


def tn(a, b):
    return lax.dot_general(a, b, (((0,), (0,)), ((), ())), preferred_element_type=F32)


def layer_norm(x_ref, gain, bias):
    values = x_ref[...].astype(F32)
    centered = values - jnp.mean(values, axis=-1, keepdims=True)
    rstd = lax.rsqrt(jnp.mean(centered * centered, axis=-1, keepdims=True) + EPS)
    xhat = centered * rstd
    normed = (xhat * gain + bias).astype(BF)
    return normed, xhat, rstd


def row_order(at_ref):
    p = lax.broadcasted_iota(jnp.int32, (D, 1), 0)
    second = jnp.where(p >= 384, 1, 0)
    q = p - 384 * second
    owner = (q * 171) >> 13
    b = q - 48 * owner
    z = (b * 43) >> 8
    j = b - 6 * z
    y, xl = (owner >> 1) ^ at_ref[0], (owner & 1) ^ at_ref[1]
    to_core = jnp.where(second == 1, at_ref[2], 1 - at_ref[2])
    feature = ((y * 8 + z) * 2 + xl) * 12 + to_core * 6 + j
    cols = lax.broadcasted_iota(jnp.int32, (D, D), 1)
    return jnp.where(cols == feature, 1.0, 0.0).astype(BF)


def own_kernel(at_ref, gain_hbm, bias_hbm, x_hbm, cot_hbm, w_hbm, wo_hbm,
               qkv_ref, dmix_ref, npt_ref, xhat_ref, rstd_ref, mt_ref, gain_ref, bias_ref, cot_ref, w_ref,
               x_ref, wo_ref, sems):
    copies = [
        pltpu.make_async_copy(x_hbm, x_ref, sems.at[0]),
        pltpu.make_async_copy(gain_hbm, gain_ref, sems.at[1]),
        pltpu.make_async_copy(bias_hbm, bias_ref, sems.at[2]),
        pltpu.make_async_copy(cot_hbm, cot_ref, sems.at[3]),
        pltpu.make_async_copy(wo_hbm, wo_ref, sems.at[4]),
    ]
    for i in range(3):
        copies.append(pltpu.make_async_copy(w_hbm.at[:, pl.ds(D * i, D)], w_ref.at[i], sems.at[5 + i]))
    for copy in copies:
        copy.start()
    mt = row_order(at_ref)
    mt_ref[...] = mt
    for copy in copies[:3]:
        copy.wait()
    normed, xhat, rstd = layer_norm(x_ref, gain_ref[...].reshape(1, D), bias_ref[...].reshape(1, D))
    xhat_ref[...] = xhat
    rstd_ref[...] = jnp.broadcast_to(rstd, (T, 128))
    npt_ref[...] = nt(mt, normed).astype(BF)
    copies[3].wait()
    copies[4].wait()
    dmix_ref[...] = nt(cot_ref[...], wo_ref[...]).astype(BF)
    for i in range(3):
        copies[5 + i].wait()
        qkv_ref[:, D * i : D * i + D] = nn(normed, w_ref[i]).astype(BF)


def head_group(g, has, qkv_ref, kvm_ref, dmix_ref):
    at = GW * g
    lanes = lax.broadcasted_iota(jnp.int32, (T, 128), 1)
    low = lanes < 64
    causal = lax.broadcasted_iota(jnp.int32, (T, T), 0) <= lax.broadcasted_iota(jnp.int32, (T, T), 1)
    low_keys = lax.broadcasted_iota(jnp.int32, (2 * T, 128), 1) < 64
    zero = jnp.zeros((), BF)
    mixes, dqs, dks, dvs = [], [], [], []
    for pair in range(2):
        cq = slice(at + 128 * pair, at + 128 * pair + 128)
        ck = slice(D + cq.start, D + cq.stop)
        cv = slice(2 * D + cq.start, 2 * D + cq.stop)
        q2 = (qkv_ref[:, cq].astype(F32) * 0.125).astype(BF)
        k2 = jnp.concatenate([qkv_ref[:, ck], kvm_ref[:, cq]], axis=0)
        v2 = jnp.concatenate([qkv_ref[:, cv], kvm_ref[:, ck]], axis=0)
        dm2 = dmix_ref[:, cq]
        k_parts = [jnp.where(low_keys, k2, zero), jnp.where(low_keys, zero, k2)]
        v_parts = [jnp.where(low_keys, v2, zero), jnp.where(low_keys, zero, v2)]
        ds_parts, p_parts, q_parts, dm_parts = [], [], [], []
        for half in range(2):
            pick = low if half == 0 else jnp.logical_not(low)
            qa = jnp.where(pick, q2, zero)
            dma = jnp.where(pick, dm2, zero)
            st = nt(k2, qa)
            st_own = jnp.where(causal, st[:T], -1e30)
            st_mem = jnp.where(has, st[T:], -1e30)
            st = jnp.concatenate([st_own, st_mem], axis=0)
            top = jnp.max(st, axis=0, keepdims=True)
            e = jnp.exp(st - top)
            p = e * (1.0 / jnp.sum(e, axis=0, keepdims=True))
            pb = p.astype(BF)
            dp = nt(v2, dma)
            ds = (p * (dp - jnp.sum(dp * p, axis=0, keepdims=True))).astype(BF)
            ds_parts.append(ds)
            p_parts.append(pb)
            q_parts.append(qa)
            dm_parts.append(dma)
        dks.append(nn(jnp.concatenate(ds_parts, axis=1), jnp.concatenate(q_parts, axis=0)).astype(BF))
        dvs.append(nn(jnp.concatenate(p_parts, axis=1), jnp.concatenate(dm_parts, axis=0)).astype(BF))
        mixes.append(tn(jnp.concatenate(p_parts, axis=0), jnp.concatenate(v_parts, axis=0)).astype(BF))
        dqs.append((tn(jnp.concatenate(ds_parts, axis=0), jnp.concatenate(k_parts, axis=0)) * 0.125).astype(BF))
    dq = jnp.concatenate(dqs, axis=1)
    dk = jnp.concatenate(dks, axis=1)
    dv = jnp.concatenate(dvs, axis=1)
    return jnp.concatenate(mixes, axis=1), dq, dk, dv


def put_rows(send_ref, keep_ref, slot, xh, lhs, rhs):
    first, second = rhs[:, :384], rhs[:, 384:]
    mine = xh == 0
    for r in range(2):
        part = jnp.where(mine, first, second) if r == 0 else jnp.where(mine, second, first)
        at = 768 * r + 384 * slot
        send_ref[:, at : at + 384] = nn(lhs[:384], part).astype(BF)
        keep_ref[:, at : at + 384] = nn(lhs[384:], part).astype(BF)


def group_outputs(g, slot, at_ref, npt_all, w_ref, grads, send_ref, keep_ref):
    dq, dk, dv = grads
    rhs = jnp.concatenate([jnp.concatenate([dq, jnp.zeros((T, GW), BF)], axis=0), dk, dv], axis=1)
    put_rows(send_ref, keep_ref, slot, at_ref[3], npt_all, rhs)
    wq, wk, wv = (w_ref[i, :, GW * g : GW * g + GW] for i in range(3))
    own = nt(dq, wq) + nt(dk[:T], wk) + nt(dv[:T], wv)
    mem = nt(dk[T:], wk) + nt(dv[T:], wv)
    return own, mem


def first_kernel(at_ref, gain_ref, bias_ref, xp_ref, w_ref, mt_ref, qkv_ref, dmix_ref, npt_ref,
                 send_ref, keep_ref, mixed_ref, dn_ref, dnm_ref, kvm_ref, npt_all_ref, xhatm_ref):
    normed, xhat, _ = layer_norm(xp_ref, gain_ref[...].reshape(1, D), bias_ref[...].reshape(1, D))
    for i in range(2):
        kvm_ref[:, D * i : D * i + D] = nn(normed, w_ref[1 + i]).astype(BF)
    xhatm_ref[...] = xhat
    npt_all_ref[:, :T] = npt_ref[...]
    npt_all_ref[:, T:] = nt(mt_ref[...], normed).astype(BF)
    has = at_ref[4] > 0
    npt_all = npt_all_ref[...]
    for g in range(2):
        mixed, *grads = head_group(g, has, qkv_ref, kvm_ref, dmix_ref)
        mixed_ref[:, GW * g : GW * g + GW] = mixed
        own, mem = group_outputs(g, g, at_ref, npt_all, w_ref, grads, send_ref, keep_ref)
        if g == 0:
            dn_ref[...] = own
            dnm_ref[...] = mem
        else:
            dn_ref[...] += own
            dnm_ref[...] += mem


def second_kernel(at_ref, w_ref, mt_ref, cot_ref, qkv_ref, dmix_ref, mixed_in, dn_in, dnm_in, kvm_ref, npt_all_ref,
                  xhat_ref, xhatm_ref, send_ref, keep_ref, vec_ref, mixed_ref, dn_ref):
    mixed, *grads = head_group(2, at_ref[4] > 0, qkv_ref, kvm_ref, dmix_ref)
    mixed_ref[:, : 2 * GW] = mixed_in[...]
    mixed_ref[:, 2 * GW :] = mixed
    own, mem = group_outputs(2, 0, at_ref, npt_all_ref[...], w_ref, grads, send_ref, keep_ref)
    lhs = nt(mt_ref[...], mixed_ref[...]).astype(BF)
    put_rows(send_ref, keep_ref, 1, at_ref[3], lhs, cot_ref[...])
    dn, dnm = dn_in[...] + own, dnm_in[...] + mem
    dn_ref[...] = dn
    vec_ref[0:1, :] = jnp.sum(dn * xhat_ref[...] + dnm * xhatm_ref[...], axis=0, keepdims=True)
    vec_ref[1:2, :] = jnp.sum(dn + dnm, axis=0, keepdims=True)


def token_kernel(gain_ref, x_ref, cot_ref, mixed_ref, wo_ref, dn_ref, xhat_ref, rstd_ref, out_ref, dx_ref):
    out_ref[...] = (x_ref[...].astype(F32) + nn(mixed_ref[...], wo_ref[...])).astype(BF)
    d_hat = dn_ref[...] * gain_ref[...].reshape(1, D)
    xhat = xhat_ref[...]
    row = rstd_ref[:, 0:1] * (
        d_hat
        - jnp.mean(d_hat, axis=-1, keepdims=True)
        - xhat * jnp.mean(d_hat * xhat, axis=-1, keepdims=True)
    )
    dx_ref[...] = (cot_ref[...].astype(F32) + row).astype(BF)


def split_rows(value):
    high = value.astype(BF)
    low = (value - high.astype(F32)).astype(BF)
    return jnp.concatenate([high, low, jnp.zeros((4, value.shape[1]), BF)], axis=0)


def join_rows(rows):
    return rows[0:2].astype(F32) + rows[2:4].astype(F32)


def tree(a, b, c, d):
    return (a.astype(F32) + b.astype(F32)) + (c.astype(F32) + d.astype(F32))


def pair_a_kernel(keep_ref, recv_ref, *outs):
    for k in range(4):
        rows = slice(96 * k, 96 * k + 96)
        outs[k][...] = (keep_ref[rows, :].astype(F32) + recv_ref[rows, :].astype(F32)).astype(BF)


def pair_b_kernel(keep_ref, recv_ref, vec_ref, vecr_ref, *outs):
    vec = split_rows(vec_ref[...] + vecr_ref[...])
    for k in range(4):
        cols = slice(768 * (k & 1), 768 * (k & 1) + 768)
        for y in range(4):
            rows = slice(96 * y + 48 * (k >> 1), 96 * y + 48 * (k >> 1) + 48)
            outs[k][48 * y : 48 * y + 48, :] = (
                keep_ref[rows, cols].astype(F32) + recv_ref[rows, cols].astype(F32)
            ).astype(BF)
        outs[k][192:200, :] = vec


def mid_a_kernel(a, b, c, d, *outs):
    for k in range(4):
        rows = slice(48 * (k >> 1), 48 * (k >> 1) + 48)
        cols = slice(768 * (k & 1), 768 * (k & 1) + 768)
        outs[k][...] = tree(a[rows, cols], b[rows, cols], c[rows, cols], d[rows, cols]).astype(BF)


def mid_b_kernel(a, b, c, d, *outs):
    vec = split_rows((join_rows(a[192:200]) + join_rows(b[192:200])) + (join_rows(c[192:200]) + join_rows(d[192:200])))
    for k in range(4):
        rows = slice(48 * k, 48 * k + 48)
        outs[k][0:48, :] = tree(a[rows], b[rows], c[rows], d[rows]).astype(BF)
        outs[k][48:56, :] = vec


def plane_kernel(a0, a1, a2, a3, b0, b1, b2, b3, out_ref):
    at = slice(48, 56)
    vec = (join_rows(b0[at]) + join_rows(b1[at])) + (join_rows(b2[at]) + join_rows(b3[at]))
    vec = jnp.concatenate([vec[0:1], vec[1:2]], axis=1)
    high = vec.astype(BF).astype(F32)
    tail = jnp.concatenate([high, vec - high], axis=0)
    g = slice(0, 48)
    sums = jnp.concatenate([tree(a0[...], a1[...], a2[...], a3[...]), tree(b0[g], b1[g], b2[g], b3[g])], axis=1)
    for z in range(8):
        out_ref[z] = jnp.concatenate([sums[6 * z : 6 * z + 6], tail], axis=0).astype(BF)


def column_kernel(factor, in_ref, rows_ref, gain_ref, bias_ref):
    acc = in_ref[0].astype(F32)
    for z in range(1, 8):
        acc = acc + in_ref[z].astype(F32)
    rows_ref[...] = acc.astype(BF)
    vec = (acc[6:7] + acc[7:8]) * factor
    gain_ref[...] = vec[:, :D].reshape(D)
    bias_ref[...] = vec[:, D:].reshape(D)


def finish_kernel(factor, at_ref, mine_ref, other_ref, qkv_ref, wout_ref):
    mine, other = mine_ref[...].astype(F32) * factor, other_ref[...].astype(F32) * factor
    first = at_ref[3] == 0
    halves = [jnp.where(first, mine, other), jnp.where(first, other, mine)]
    for g in range(GROUPS + 1):
        cols = slice(384 * g, 384 * g + 384)
        full = jnp.concatenate([halves[0][0:6, cols], halves[1][0:6, cols]], axis=1)
        if g < GROUPS:
            for i in range(3):
                at = D * i + GW * g
                qkv_ref[:, at : at + GW] = full[:, GW * i : GW * i + GW]
        else:
            wout_ref[...] = full


VM = pl.BlockSpec(memory_space=pltpu.VMEM)
SM = pl.BlockSpec(memory_space=pltpu.SMEM)
HBM = pl.BlockSpec(memory_space=pltpu.MemorySpace.HBM)


def call(kernel, name, out_shape, args, scalars=0, anys=(), scratch=(), limit=16):
    specs = [SM if i < scalars else HBM if i in anys else VM for i in range(len(args))]
    args = [pltpu.with_memory_space_constraint(a, pltpu.MemorySpace.HBM) if i in anys else a for i, a in enumerate(args)]
    return pl.pallas_call(
        kernel,
        name=name,
        in_specs=specs,
        out_specs=[VM] * len(out_shape),
        out_shape=out_shape,
        scratch_shapes=scratch,
        compiler_params=pltpu.CompilerParams(vmem_limit_bytes=limit * 1024 * 1024),
    )(*args)


def sds(*shape, dtype=BF):
    return jax.ShapeDtypeStruct(shape, dtype)


def on_device(layer_input, cotangent, gain, bias, w, wo):
    x, cot = layer_input[0], cotangent[0]
    seq = lax.axis_size(SEQ)
    xp = lax.ppermute(x, SEQ, [(i, i + 1) for i in range(seq - 1)])
    place = [lax.axis_index(n) for n in ("y", "xl", "c", "xh")] + [lax.axis_index(SEQ) > 0]
    at = jnp.stack([v.astype(jnp.int32) for v in place])
    row, mat, tokens = sds(T, D, dtype=F32), sds(D, D), sds(T, D)
    one = sds(D, dtype=F32)
    qkv, dmix, npt, xhat, rstd, mt, gain_v, bias_v, cot_v, w = call(
        own_kernel, "own_part",
        [sds(T, 3 * D), tokens, sds(D, T), row, sds(T, 128, dtype=F32), mat, one, one, tokens, sds(3, D, D)],
        [at, gain, bias, x, cot, w, wo], 1, (1, 2, 3, 4, 5, 6),
        [pltpu.VMEM((T, D), BF), pltpu.VMEM((D, D), BF), pltpu.SemaphoreType.DMA((8,))],
    )
    wide = sds(384, 1536)
    send_a, keep_a, mixed, dn, dnm, kvm, npt_all, xhatm = call(
        first_kernel, "memory_and_heads",
        [wide, wide, sds(T, 2 * GW), row, row, sds(T, 2 * D), sds(D, 2 * T), row],
        [at, gain_v, bias_v, xp, w, mt, qkv, dmix, npt], 1, limit=LIMIT,
    )
    send_b, keep_b, vec, mixed, dn = call(
        second_kernel, "heads_and_output_weight",
        [wide, wide, sds(2, D, dtype=F32), tokens, row],
        [at, w, mt, cot_v, qkv, dmix, mixed, dn, dnm, kvm, npt_all, xhat, xhatm], 1, limit=LIMIT,
    )

    def swap(block):
        return lax.ppermute(block, "c", [(0, 1), (1, 0)])

    def exchange(parts, axes):
        n = lax.axis_size(axes)
        return [parts[0]] + [lax.ppermute(parts[k], axes, [(i, i ^ k) for i in range(n)]) for k in (1, 3, 2)]

    def ordered(parts):
        own, one, three, two = parts
        return [own, one, two, three]

    parts_a = call(pair_a_kernel, "pair_sum_a", [sds(96, 1536)] * 4, [keep_a, swap(send_a)])
    parts_b = call(pair_b_kernel, "pair_sum_b", [sds(200, 768)] * 4, [keep_b, swap(send_b), vec, swap(vec)])
    parts_a = ordered(exchange(parts_a, "y"))
    parts_b = ordered(exchange(parts_b, ROW))
    out, dx = call(
        token_kernel, "token_outputs", [tokens, tokens],
        [gain, x, cot, mixed, wo, dn, xhat, rstd],
    )
    parts_a = call(mid_a_kernel, "middle_sum_a", [sds(48, 768)] * 4, parts_a)
    parts_b = call(mid_b_kernel, "middle_sum_b", [sds(56, 768)] * 4, parts_b)
    parts_a = ordered(exchange(parts_a, ROW))
    parts_b = ordered(exchange(parts_b, "y"))
    (mine,) = call(plane_kernel, "plane_sum", [sds(8, 8, 1536)], [*parts_a, *parts_b])
    mine = lax.all_to_all(mine, "z", 0, 0, tiled=True)
    factor = 1.0 / float(seq * lax.axis_size("xh") * T) ** 0.5
    mine, grad_gain, grad_bias = call(
        functools.partial(column_kernel, factor), "column_sum",
        [sds(8, 1536), sds(D, dtype=F32), sds(D, dtype=F32)], [mine],
    )
    other = lax.ppermute(mine, "xh", [(0, 1), (1, 0)])
    grad_qkv, grad_out = call(
        functools.partial(finish_kernel, factor), "finish",
        [sds(6, 3 * D, dtype=F32), sds(6, D, dtype=F32)], [at, mine, other], 1,
    )
    return out[None], dx[None], grad_qkv, grad_out, grad_gain, grad_bias


def solution(mesh):
    torus = Mesh(mesh.devices.reshape(4, 8, 2, 2, 2), ("y", "z", "xl", "c", "xh"))
    return jax.shard_map(
        on_device,
        mesh=torus,
        in_specs=(P("xh", SEQ, None), P("xh", SEQ, None), P(), P(), P(), P()),
        out_specs=(P("xh", SEQ, None), P("xh", SEQ, None), P(SEQ, None), P(SEQ, None), P(), P()),
        check_vma=False,
    )
```

```python
import functools

import jax
import jax.numpy as jnp
from jax import lax
from jax.experimental import pallas as pl
from jax.experimental.pallas import tpu as pltpu
from jax.sharding import Mesh
from jax.sharding import PartitionSpec as P

HEADS = 12
EPS = 1e-05
SEQ = ("y", "z", "xl", "c")
ROW = ("xl", "xh")
T = 256
D = 768
GROUPS = 3
GW = 256
BF = jnp.bfloat16
F32 = jnp.float32
LIMIT = 24


def nn(a, b):
    return lax.dot_general(a, b, (((1,), (0,)), ((), ())), preferred_element_type=F32)


def nt(a, b):
    return lax.dot_general(a, b, (((1,), (1,)), ((), ())), preferred_element_type=F32)


def tn(a, b):
    return lax.dot_general(a, b, (((0,), (0,)), ((), ())), preferred_element_type=F32)


def layer_norm(x_ref, gain, bias):
    values = x_ref[...].astype(F32)
    centered = values - jnp.mean(values, axis=-1, keepdims=True)
    rstd = lax.rsqrt(jnp.mean(centered * centered, axis=-1, keepdims=True) + EPS)
    xhat = centered * rstd
    normed = (xhat * gain + bias).astype(BF)
    return normed, xhat, rstd


def row_order(at_ref):
    p = lax.broadcasted_iota(jnp.int32, (D, 1), 0)
    second = jnp.where(p >= 384, 1, 0)
    q = p - 384 * second
    owner = (q * 171) >> 13
    b = q - 48 * owner
    z = (b * 43) >> 8
    j = b - 6 * z
    y, xl = (owner >> 1) ^ at_ref[0], (owner & 1) ^ at_ref[1]
    to_core = jnp.where(second == 1, at_ref[2], 1 - at_ref[2])
    feature = ((y * 8 + z) * 2 + xl) * 12 + to_core * 6 + j
    cols = lax.broadcasted_iota(jnp.int32, (D, D), 1)
    return jnp.where(cols == feature, 1.0, 0.0).astype(BF)


def own_kernel(at_ref, gain_hbm, bias_hbm, x_hbm, cot_hbm, w_hbm, wo_hbm,
               qkv_ref, dmix_ref, npt_ref, xhat_ref, rstd_ref, mt_ref, gain_ref, bias_ref, cot_ref, w_ref,
               x_ref, wo_ref, sems):
    copies = [
        pltpu.make_async_copy(x_hbm, x_ref, sems.at[0]),
        pltpu.make_async_copy(gain_hbm, gain_ref, sems.at[1]),
        pltpu.make_async_copy(bias_hbm, bias_ref, sems.at[2]),
        pltpu.make_async_copy(cot_hbm, cot_ref, sems.at[3]),
        pltpu.make_async_copy(wo_hbm, wo_ref, sems.at[4]),
    ]
    for i in range(3):
        copies.append(pltpu.make_async_copy(w_hbm.at[:, pl.ds(D * i, D)], w_ref.at[i], sems.at[5 + i]))
    for copy in copies:
        copy.start()
    mt = row_order(at_ref)
    mt_ref[...] = mt
    for copy in copies[:3]:
        copy.wait()
    normed, xhat, rstd = layer_norm(x_ref, gain_ref[...].reshape(1, D), bias_ref[...].reshape(1, D))
    xhat_ref[...] = xhat
    rstd_ref[...] = jnp.broadcast_to(rstd, (T, 128))
    npt_ref[...] = nt(mt, normed).astype(BF)
    copies[3].wait()
    copies[4].wait()
    dmix_ref[...] = nt(cot_ref[...], wo_ref[...]).astype(BF)
    for i in range(3):
        copies[5 + i].wait()
        qkv_ref[:, D * i : D * i + D] = nn(normed, w_ref[i]).astype(BF)


def head_group(g, has, qkv_ref, kvm_ref, dmix_ref):
    at = GW * g
    lanes = lax.broadcasted_iota(jnp.int32, (T, 128), 1)
    low = lanes < 64
    causal = lax.broadcasted_iota(jnp.int32, (T, T), 0) <= lax.broadcasted_iota(jnp.int32, (T, T), 1)
    low_keys = lax.broadcasted_iota(jnp.int32, (2 * T, 128), 1) < 64
    zero = jnp.zeros((), BF)
    mixes, dqs, dks, dvs = [], [], [], []
    for pair in range(2):
        cq = slice(at + 128 * pair, at + 128 * pair + 128)
        ck = slice(D + cq.start, D + cq.stop)
        cv = slice(2 * D + cq.start, 2 * D + cq.stop)
        q2 = (qkv_ref[:, cq].astype(F32) * 0.125).astype(BF)
        k2 = jnp.concatenate([qkv_ref[:, ck], kvm_ref[:, cq]], axis=0)
        v2 = jnp.concatenate([qkv_ref[:, cv], kvm_ref[:, ck]], axis=0)
        dm2 = dmix_ref[:, cq]
        k_parts = [jnp.where(low_keys, k2, zero), jnp.where(low_keys, zero, k2)]
        v_parts = [jnp.where(low_keys, v2, zero), jnp.where(low_keys, zero, v2)]
        ds_parts, p_parts, q_parts, dm_parts = [], [], [], []
        for half in range(2):
            pick = low if half == 0 else jnp.logical_not(low)
            qa = jnp.where(pick, q2, zero)
            dma = jnp.where(pick, dm2, zero)
            st = nt(k2, qa)
            st_own = jnp.where(causal, st[:T], -1e30)
            st_mem = jnp.where(has, st[T:], -1e30)
            st = jnp.concatenate([st_own, st_mem], axis=0)
            top = jnp.max(st, axis=0, keepdims=True)
            e = jnp.exp(st - top)
            p = e * (1.0 / jnp.sum(e, axis=0, keepdims=True))
            pb = p.astype(BF)
            dp = nt(v2, dma)
            ds = (p * (dp - jnp.sum(dp * p, axis=0, keepdims=True))).astype(BF)
            ds_parts.append(ds)
            p_parts.append(pb)
            q_parts.append(qa)
            dm_parts.append(dma)
        dks.append(nn(jnp.concatenate(ds_parts, axis=1), jnp.concatenate(q_parts, axis=0)).astype(BF))
        dvs.append(nn(jnp.concatenate(p_parts, axis=1), jnp.concatenate(dm_parts, axis=0)).astype(BF))
        mixes.append(tn(jnp.concatenate(p_parts, axis=0), jnp.concatenate(v_parts, axis=0)).astype(BF))
        dqs.append((tn(jnp.concatenate(ds_parts, axis=0), jnp.concatenate(k_parts, axis=0)) * 0.125).astype(BF))
    dq = jnp.concatenate(dqs, axis=1)
    dk = jnp.concatenate(dks, axis=1)
    dv = jnp.concatenate(dvs, axis=1)
    return jnp.concatenate(mixes, axis=1), dq, dk, dv


def put_rows(send_ref, keep_ref, slot, xh, lhs, rhs):
    first, second = rhs[:, :384], rhs[:, 384:]
    mine = xh == 0
    for r in range(2):
        part = jnp.where(mine, first, second) if r == 0 else jnp.where(mine, second, first)
        at = 768 * r + 384 * slot
        send_ref[:, at : at + 384] = nn(lhs[:384], part).astype(BF)
        keep_ref[:, at : at + 384] = nn(lhs[384:], part).astype(BF)


def group_outputs(g, slot, at_ref, npt_all, w_ref, grads, send_ref, keep_ref):
    dq, dk, dv = grads
    rhs = jnp.concatenate([jnp.concatenate([dq, jnp.zeros((T, GW), BF)], axis=0), dk, dv], axis=1)
    put_rows(send_ref, keep_ref, slot, at_ref[3], npt_all, rhs)
    wq, wk, wv = (w_ref[i, :, GW * g : GW * g + GW] for i in range(3))
    own = nt(dq, wq) + nt(dk[:T], wk) + nt(dv[:T], wv)
    mem = nt(dk[T:], wk) + nt(dv[T:], wv)
    return own, mem


def first_kernel(at_ref, gain_ref, bias_ref, xp_ref, w_ref, mt_ref, qkv_ref, dmix_ref, npt_ref,
                 send_ref, keep_ref, mixed_ref, dn_ref, dnm_ref, kvm_ref, npt_all_ref, xhatm_ref):
    normed, xhat, _ = layer_norm(xp_ref, gain_ref[...].reshape(1, D), bias_ref[...].reshape(1, D))
    for i in range(2):
        kvm_ref[:, D * i : D * i + D] = nn(normed, w_ref[1 + i]).astype(BF)
    xhatm_ref[...] = xhat
    npt_all_ref[:, :T] = npt_ref[...]
    npt_all_ref[:, T:] = nt(mt_ref[...], normed).astype(BF)
    has = at_ref[4] > 0
    npt_all = npt_all_ref[...]
    for g in range(2):
        mixed, *grads = head_group(g, has, qkv_ref, kvm_ref, dmix_ref)
        mixed_ref[:, GW * g : GW * g + GW] = mixed
        own, mem = group_outputs(g, g, at_ref, npt_all, w_ref, grads, send_ref, keep_ref)
        if g == 0:
            dn_ref[...] = own
            dnm_ref[...] = mem
        else:
            dn_ref[...] += own
            dnm_ref[...] += mem


def second_kernel(at_ref, w_ref, mt_ref, cot_ref, qkv_ref, dmix_ref, mixed_in, dn_in, dnm_in, kvm_ref, npt_all_ref,
                  xhat_ref, xhatm_ref, send_ref, keep_ref, vec_ref, mixed_ref, dn_ref):
    mixed, *grads = head_group(2, at_ref[4] > 0, qkv_ref, kvm_ref, dmix_ref)
    mixed_ref[:, : 2 * GW] = mixed_in[...]
    mixed_ref[:, 2 * GW :] = mixed
    own, mem = group_outputs(2, 0, at_ref, npt_all_ref[...], w_ref, grads, send_ref, keep_ref)
    lhs = nt(mt_ref[...], mixed_ref[...]).astype(BF)
    put_rows(send_ref, keep_ref, 1, at_ref[3], lhs, cot_ref[...])
    dn, dnm = dn_in[...] + own, dnm_in[...] + mem
    dn_ref[...] = dn
    vec_ref[0:1, :] = jnp.sum(dn * xhat_ref[...] + dnm * xhatm_ref[...], axis=0, keepdims=True)
    vec_ref[1:2, :] = jnp.sum(dn + dnm, axis=0, keepdims=True)


def token_kernel(gain_ref, x_ref, cot_ref, mixed_ref, wo_ref, dn_ref, xhat_ref, rstd_ref, out_ref, dx_ref):
    out_ref[...] = (x_ref[...].astype(F32) + nn(mixed_ref[...], wo_ref[...])).astype(BF)
    d_hat = dn_ref[...] * gain_ref[...].reshape(1, D)
    xhat = xhat_ref[...]
    row = rstd_ref[:, 0:1] * (
        d_hat
        - jnp.mean(d_hat, axis=-1, keepdims=True)
        - xhat * jnp.mean(d_hat * xhat, axis=-1, keepdims=True)
    )
    dx_ref[...] = (cot_ref[...].astype(F32) + row).astype(BF)


def split_rows(value):
    high = value.astype(BF)
    low = (value - high.astype(F32)).astype(BF)
    return jnp.concatenate([high, low, jnp.zeros((4, value.shape[1]), BF)], axis=0)


def join_rows(rows):
    return rows[0:2].astype(F32) + rows[2:4].astype(F32)


def fold_rows(value):
    high = value.astype(BF)
    low = (value - high.astype(F32)).astype(BF)
    return jnp.concatenate([high[:, :384], high[:, 384:], low[:, :384], low[:, 384:]], axis=0)


def unfold_rows(rows):
    rows = rows.astype(F32)
    return jnp.concatenate([rows[0:2] + rows[4:6], rows[2:4] + rows[6:8]], axis=1)


def tree(a, b, c, d):
    return (a.astype(F32) + b.astype(F32)) + (c.astype(F32) + d.astype(F32))


RING_Y = (1, 3, 2)
RING_X = (2, 3, 1)


def halving_order(ring):
    one, two, far = ring
    return [((one, far), (0, two)), ((two, far), (0, one))]


def pair_a_kernel(keep_ref, recv_ref, *outs):
    for part, groups in enumerate(halving_order(RING_Y)):
        cols = slice(768 * part, 768 * part + 768)
        for kept, places in enumerate(groups):
            for i, k in enumerate(places):
                rows = slice(96 * k, 96 * k + 96)
                outs[2 * part + kept][96 * i : 96 * i + 96, :] = (
                    keep_ref[rows, cols].astype(F32) + recv_ref[rows, cols].astype(F32)
                ).astype(BF)


def pair_b_kernel(keep_ref, recv_ref, vec_ref, vecr_ref, *outs):
    for part, groups in enumerate(halving_order(RING_X)):
        for kept, places in enumerate(groups):
            out = outs[2 * part + kept]
            for i, k in enumerate(places):
                at = 768 * (k & 1) + 384 * part
                for y in range(4):
                    rows = slice(96 * y + 48 * (k >> 1), 96 * y + 48 * (k >> 1) + 48)
                    out[192 * i + 48 * y : 192 * i + 48 * y + 48, :] = (
                        keep_ref[rows, at : at + 384].astype(F32) + recv_ref[rows, at : at + 384].astype(F32)
                    ).astype(BF)
    vec = fold_rows(vec_ref[...] + vecr_ref[...])
    outs[0][384:392, :] = vec
    outs[1][384:392, :] = vec


def step_a_kernel(recv0_ref, keep0_ref, recv1_ref, keep1_ref, send0_ref, send1_ref, own_ref):
    for part, (recv, keep, send) in enumerate(((recv0_ref, keep0_ref, send0_ref), (recv1_ref, keep1_ref, send1_ref))):
        add = lambda rows: keep[rows, :].astype(F32) + recv[rows, :].astype(F32)
        own_ref[:, 768 * part : 768 * part + 768] = add(slice(0, 96))
        send[...] = add(slice(96, 192)).astype(BF)


def step_b_kernel(recv0_ref, keep0_ref, recv1_ref, keep1_ref, send0_ref, send1_ref, own_ref, vec_ref):
    for part, (recv, keep, send) in enumerate(((recv0_ref, keep0_ref, send0_ref), (recv1_ref, keep1_ref, send1_ref))):
        add = lambda rows: keep[rows, :].astype(F32) + recv[rows, :].astype(F32)
        own_ref[:, 384 * part : 384 * part + 384] = add(slice(0, 192))
        send[0:192, :] = add(slice(192, 384)).astype(BF)
    vec = unfold_rows(keep0_ref[384:392, :]) + unfold_rows(recv0_ref[384:392, :])
    rows = fold_rows(vec)
    vec_ref[...] = unfold_rows(rows)
    send0_ref[192:200, :] = rows


def mid_a_kernel(own_ref, recv0_ref, recv1_ref, *outs):
    for k in range(4):
        rows = slice(48 * (k >> 1), 48 * (k >> 1) + 48)
        recv = recv1_ref if k & 1 else recv0_ref
        outs[k][...] = (own_ref[rows, 768 * (k & 1) : 768 * (k & 1) + 768] + recv[rows, :].astype(F32)).astype(BF)


def mid_b_kernel(own_ref, vec_ref, recv0_ref, recv1_ref, *outs):
    vec = split_rows(vec_ref[...] + unfold_rows(recv0_ref[192:200, :]))
    for k in range(4):
        rows = slice(48 * k, 48 * k + 48)
        outs[k][0:48, 0:384] = (own_ref[rows, 0:384] + recv0_ref[rows, :].astype(F32)).astype(BF)
        outs[k][0:48, 384:768] = (own_ref[rows, 384:768] + recv1_ref[rows, :].astype(F32)).astype(BF)
        outs[k][48:56, :] = vec


def plane_kernel(a0, a1, a2, a3, b0, b1, b2, b3, out_ref):
    at = slice(48, 56)
    vec = (join_rows(b0[at]) + join_rows(b1[at])) + (join_rows(b2[at]) + join_rows(b3[at]))
    vec = jnp.concatenate([vec[0:1], vec[1:2]], axis=1)
    high = vec.astype(BF).astype(F32)
    tail = jnp.concatenate([high, vec - high], axis=0)
    g = slice(0, 48)
    sums = jnp.concatenate([tree(a0[...], a1[...], a2[...], a3[...]), tree(b0[g], b1[g], b2[g], b3[g])], axis=1)
    for z in range(8):
        out_ref[z] = jnp.concatenate([sums[6 * z : 6 * z + 6], tail], axis=0).astype(BF)


def column_kernel(factor, in_ref, rows_ref, gain_ref, bias_ref):
    acc = in_ref[0].astype(F32)
    for z in range(1, 8):
        acc = acc + in_ref[z].astype(F32)
    rows_ref[...] = acc.astype(BF)
    vec = (acc[6:7] + acc[7:8]) * factor
    gain_ref[...] = vec[:, :D].reshape(D)
    bias_ref[...] = vec[:, D:].reshape(D)


def finish_kernel(factor, at_ref, mine_ref, other_ref, qkv_ref, wout_ref):
    mine, other = mine_ref[...].astype(F32) * factor, other_ref[...].astype(F32) * factor
    first = at_ref[3] == 0
    halves = [jnp.where(first, mine, other), jnp.where(first, other, mine)]
    for g in range(GROUPS + 1):
        cols = slice(384 * g, 384 * g + 384)
        full = jnp.concatenate([halves[0][0:6, cols], halves[1][0:6, cols]], axis=1)
        if g < GROUPS:
            for i in range(3):
                at = D * i + GW * g
                qkv_ref[:, at : at + GW] = full[:, GW * i : GW * i + GW]
        else:
            wout_ref[...] = full


VM = pl.BlockSpec(memory_space=pltpu.VMEM)
SM = pl.BlockSpec(memory_space=pltpu.SMEM)
HBM = pl.BlockSpec(memory_space=pltpu.MemorySpace.HBM)


def call(kernel, name, out_shape, args, scalars=0, anys=(), scratch=(), limit=16):
    specs = [SM if i < scalars else HBM if i in anys else VM for i in range(len(args))]
    args = [pltpu.with_memory_space_constraint(a, pltpu.MemorySpace.HBM) if i in anys else a for i, a in enumerate(args)]
    return pl.pallas_call(
        kernel,
        name=name,
        in_specs=specs,
        out_specs=[VM] * len(out_shape),
        out_shape=out_shape,
        scratch_shapes=scratch,
        compiler_params=pltpu.CompilerParams(vmem_limit_bytes=limit * 1024 * 1024),
    )(*args)


def sds(*shape, dtype=BF):
    return jax.ShapeDtypeStruct(shape, dtype)


def on_device(layer_input, cotangent, gain, bias, w, wo):
    x, cot = layer_input[0], cotangent[0]
    seq = lax.axis_size(SEQ)
    xp = lax.ppermute(x, SEQ, [(i, i + 1) for i in range(seq - 1)])
    place = [lax.axis_index(n) for n in ("y", "xl", "c", "xh")] + [lax.axis_index(SEQ) > 0]
    at = jnp.stack([v.astype(jnp.int32) for v in place])
    row, mat, tokens = sds(T, D, dtype=F32), sds(D, D), sds(T, D)
    one = sds(D, dtype=F32)
    qkv, dmix, npt, xhat, rstd, mt, gain_v, bias_v, cot_v, w = call(
        own_kernel, "own_part",
        [sds(T, 3 * D), tokens, sds(D, T), row, sds(T, 128, dtype=F32), mat, one, one, tokens, sds(3, D, D)],
        [at, gain, bias, x, cot, w, wo], 1, (1, 2, 3, 4, 5, 6),
        [pltpu.VMEM((T, D), BF), pltpu.VMEM((D, D), BF), pltpu.SemaphoreType.DMA((8,))],
    )
    wide = sds(384, 1536)
    send_a, keep_a, mixed, dn, dnm, kvm, npt_all, xhatm = call(
        first_kernel, "memory_and_heads",
        [wide, wide, sds(T, 2 * GW), row, row, sds(T, 2 * D), sds(D, 2 * T), row],
        [at, gain_v, bias_v, xp, w, mt, qkv, dmix, npt], 1, limit=LIMIT,
    )
    send_b, keep_b, vec, mixed, dn = call(
        second_kernel, "heads_and_output_weight",
        [wide, wide, sds(2, D, dtype=F32), tokens, row],
        [at, w, mt, cot_v, qkv, dmix, mixed, dn, dnm, kvm, npt_all, xhat, xhatm], 1, limit=LIMIT,
    )

    def swap(block):
        return lax.ppermute(block, "c", [(0, 1), (1, 0)])

    def permute(block, axes, k):
        n = lax.axis_size(axes)
        return lax.ppermute(block, axes, [(i, i ^ k) for i in range(n)])

    def exchange(parts, axes):
        return [parts[0]] + [permute(parts[k], axes, k) for k in (1, 2, 3)]

    half = sds(192, 768)
    send0_a, keep0_a, send1_a, keep1_a = call(pair_a_kernel, "pair_sum_a", [half] * 4, [keep_a, swap(send_a)])
    send0_b, keep0_b, send1_b, keep1_b = call(
        pair_b_kernel, "pair_sum_b", [sds(392, 384), sds(392, 384), sds(384, 384), sds(384, 384)],
        [keep_b, swap(send_b), vec, swap(vec)],
    )
    got_a = [permute(send0_a, "y", RING_Y[0]), permute(send1_a, "y", RING_Y[1])]
    got_b = [permute(send0_b, ROW, RING_X[0]), permute(send1_b, ROW, RING_X[1])]
    out, dx = call(
        token_kernel, "token_outputs", [tokens, tokens],
        [gain, x, cot, mixed, wo, dn, xhat, rstd],
    )
    send0_a, send1_a, own_a = call(
        step_a_kernel, "step_sum_a", [sds(96, 768), sds(96, 768), sds(96, 1536, dtype=F32)],
        [got_a[0], keep0_a, got_a[1], keep1_a],
    )
    got_a = [permute(send0_a, "y", RING_Y[1]), permute(send1_a, "y", RING_Y[0])]
    send0_b, send1_b, own_b, vec = call(
        step_b_kernel, "step_sum_b", [sds(200, 384), sds(192, 384), sds(192, 768, dtype=F32), sds(2, D, dtype=F32)],
        [got_b[0], keep0_b, got_b[1], keep1_b],
    )
    got_b = [permute(send0_b, ROW, RING_X[1]), permute(send1_b, ROW, RING_X[0])]
    parts_a = call(mid_a_kernel, "middle_sum_a", [sds(48, 768)] * 4, [own_a, *got_a])
    parts_b = call(mid_b_kernel, "middle_sum_b", [sds(56, 768)] * 4, [own_b, vec, *got_b])
    parts_a = exchange(parts_a, ROW)
    parts_b = exchange(parts_b, "y")
    (mine,) = call(plane_kernel, "plane_sum", [sds(8, 8, 1536)], [*parts_a, *parts_b])
    mine = lax.all_to_all(mine, "z", 0, 0, tiled=True)
    factor = 1.0 / float(seq * lax.axis_size("xh") * T) ** 0.5
    mine, grad_gain, grad_bias = call(
        functools.partial(column_kernel, factor), "column_sum",
        [sds(8, 1536), sds(D, dtype=F32), sds(D, dtype=F32)], [mine],
    )
    other = lax.ppermute(mine, "xh", [(0, 1), (1, 0)])
    grad_qkv, grad_out = call(
        functools.partial(finish_kernel, factor), "finish",
        [sds(6, 3 * D, dtype=F32), sds(6, D, dtype=F32)], [at, mine, other], 1,
    )
    return out[None], dx[None], grad_qkv, grad_out, grad_gain, grad_bias


def solution(mesh):
    torus = Mesh(mesh.devices.reshape(4, 8, 2, 2, 2), ("y", "z", "xl", "c", "xh"))
    return jax.shard_map(
        on_device,
        mesh=torus,
        in_specs=(P("xh", SEQ, None), P("xh", SEQ, None), P(), P(), P(), P()),
        out_specs=(P("xh", SEQ, None), P("xh", SEQ, None), P(SEQ, None), P(SEQ, None), P(), P()),
        check_vma=False,
    )
```

```python
import functools

import jax
import jax.numpy as jnp
from jax import lax
from jax.experimental import pallas as pl
from jax.experimental.pallas import tpu as pltpu
from jax.sharding import Mesh
from jax.sharding import PartitionSpec as P

HEADS = 12
EPS = 1e-05
SEQ = ("y", "z", "xl", "c")
ROW = ("xl", "xh")
T = 256
D = 768
GROUPS = 3
GW = 256
BF = jnp.bfloat16
F32 = jnp.float32
LIMIT = 24


def nn(a, b):
    return lax.dot_general(a, b, (((1,), (0,)), ((), ())), preferred_element_type=F32)


def nt(a, b):
    return lax.dot_general(a, b, (((1,), (1,)), ((), ())), preferred_element_type=F32)


def tn(a, b):
    return lax.dot_general(a, b, (((0,), (0,)), ((), ())), preferred_element_type=F32)


def layer_norm(x_ref, gain, bias):
    values = x_ref[...].astype(F32)
    centered = values - jnp.mean(values, axis=-1, keepdims=True)
    rstd = lax.rsqrt(jnp.mean(centered * centered, axis=-1, keepdims=True) + EPS)
    xhat = centered * rstd
    normed = (xhat * gain + bias).astype(BF)
    return normed, xhat, rstd


def row_order(at_ref):
    p = lax.broadcasted_iota(jnp.int32, (D, 1), 0)
    second = jnp.where(p >= 384, 1, 0)
    q = p - 384 * second
    owner = (q * 171) >> 13
    b = q - 48 * owner
    z = (b * 43) >> 8
    j = b - 6 * z
    y, xl = (owner >> 1) ^ at_ref[0], (owner & 1) ^ at_ref[1]
    to_core = jnp.where(second == 1, at_ref[2], 1 - at_ref[2])
    feature = ((y * 8 + z) * 2 + xl) * 12 + to_core * 6 + j
    cols = lax.broadcasted_iota(jnp.int32, (D, D), 1)
    return jnp.where(cols == feature, 1.0, 0.0).astype(BF)


def own_kernel(at_ref, gain_hbm, bias_hbm, x_hbm, cot_hbm, w_hbm, wo_hbm,
               qkv_ref, dmix_ref, npt_ref, xhat_ref, rstd_ref, mt_ref, gain_ref, bias_ref, cot_ref, w_ref,
               x_ref, wo_ref, sems):
    copies = [
        pltpu.make_async_copy(x_hbm, x_ref, sems.at[0]),
        pltpu.make_async_copy(gain_hbm, gain_ref, sems.at[1]),
        pltpu.make_async_copy(bias_hbm, bias_ref, sems.at[2]),
        pltpu.make_async_copy(cot_hbm, cot_ref, sems.at[3]),
        pltpu.make_async_copy(wo_hbm, wo_ref, sems.at[4]),
    ]
    for i in range(3):
        copies.append(pltpu.make_async_copy(w_hbm.at[:, pl.ds(D * i, D)], w_ref.at[i], sems.at[5 + i]))
    for copy in copies:
        copy.start()
    mt = row_order(at_ref)
    mt_ref[...] = mt
    for copy in copies[:3]:
        copy.wait()
    normed, xhat, rstd = layer_norm(x_ref, gain_ref[...].reshape(1, D), bias_ref[...].reshape(1, D))
    xhat_ref[...] = xhat
    rstd_ref[...] = jnp.broadcast_to(rstd, (T, 128))
    npt_ref[...] = nt(mt, normed).astype(BF)
    copies[3].wait()
    copies[4].wait()
    dmix_ref[...] = nt(cot_ref[...], wo_ref[...]).astype(BF)
    for i in range(3):
        copies[5 + i].wait()
        qkv_ref[:, D * i : D * i + D] = nn(normed, w_ref[i]).astype(BF)


def head_group(g, has, qkv_ref, kvm_ref, dmix_ref):
    at = GW * g
    lanes = lax.broadcasted_iota(jnp.int32, (T, 128), 1)
    low = lanes < 64
    causal = lax.broadcasted_iota(jnp.int32, (T, T), 0) <= lax.broadcasted_iota(jnp.int32, (T, T), 1)
    low_keys = lax.broadcasted_iota(jnp.int32, (2 * T, 128), 1) < 64
    zero = jnp.zeros((), BF)
    mixes, dqs, dks, dvs = [], [], [], []
    for pair in range(2):
        cq = slice(at + 128 * pair, at + 128 * pair + 128)
        ck = slice(D + cq.start, D + cq.stop)
        cv = slice(2 * D + cq.start, 2 * D + cq.stop)
        q2 = (qkv_ref[:, cq].astype(F32) * 0.125).astype(BF)
        k2 = jnp.concatenate([qkv_ref[:, ck], kvm_ref[:, cq]], axis=0)
        v2 = jnp.concatenate([qkv_ref[:, cv], kvm_ref[:, ck]], axis=0)
        dm2 = dmix_ref[:, cq]
        k_parts = [jnp.where(low_keys, k2, zero), jnp.where(low_keys, zero, k2)]
        v_parts = [jnp.where(low_keys, v2, zero), jnp.where(low_keys, zero, v2)]
        ds_parts, p_parts, q_parts, dm_parts = [], [], [], []
        for half in range(2):
            pick = low if half == 0 else jnp.logical_not(low)
            qa = jnp.where(pick, q2, zero)
            dma = jnp.where(pick, dm2, zero)
            st = nt(k2, qa)
            st_own = jnp.where(causal, st[:T], -1e30)
            st_mem = jnp.where(has, st[T:], -1e30)
            st = jnp.concatenate([st_own, st_mem], axis=0)
            top = jnp.max(st, axis=0, keepdims=True)
            e = jnp.exp(st - top)
            p = e * (1.0 / jnp.sum(e, axis=0, keepdims=True))
            pb = p.astype(BF)
            dp = nt(v2, dma)
            ds = (p * (dp - jnp.sum(dp * p, axis=0, keepdims=True))).astype(BF)
            ds_parts.append(ds)
            p_parts.append(pb)
            q_parts.append(qa)
            dm_parts.append(dma)
        dks.append(nn(jnp.concatenate(ds_parts, axis=1), jnp.concatenate(q_parts, axis=0)).astype(BF))
        dvs.append(nn(jnp.concatenate(p_parts, axis=1), jnp.concatenate(dm_parts, axis=0)).astype(BF))
        mixes.append(tn(jnp.concatenate(p_parts, axis=0), jnp.concatenate(v_parts, axis=0)).astype(BF))
        dqs.append((tn(jnp.concatenate(ds_parts, axis=0), jnp.concatenate(k_parts, axis=0)) * 0.125).astype(BF))
    dq = jnp.concatenate(dqs, axis=1)
    dk = jnp.concatenate(dks, axis=1)
    dv = jnp.concatenate(dvs, axis=1)
    return jnp.concatenate(mixes, axis=1), dq, dk, dv


def put_rows(send_ref, keep_ref, slot, xh, lhs, rhs):
    first, second = rhs[:, :384], rhs[:, 384:]
    mine = xh == 0
    rhs = jnp.concatenate([jnp.where(mine, first, second), jnp.where(mine, second, first)], axis=1)
    for out_ref, rows in ((send_ref, lhs[:384]), (keep_ref, lhs[384:])):
        sums = nn(rows, rhs).astype(BF)
        for r in range(2):
            at = 768 * r + 384 * slot
            out_ref[0:384, at : at + 384] = sums[:, 384 * r : 384 * r + 384]


def group_outputs(g, slot, at_ref, npt_all, w_ref, grads, send_ref, keep_ref):
    dq, dk, dv = grads
    rhs = jnp.concatenate([jnp.concatenate([dq, jnp.zeros((T, GW), BF)], axis=0), dk, dv], axis=1)
    put_rows(send_ref, keep_ref, slot, at_ref[3], npt_all, rhs)
    wq, wk, wv = (w_ref[i, :, GW * g : GW * g + GW] for i in range(3))
    own = nt(dq, wq) + nt(dk[:T], wk) + nt(dv[:T], wv)
    mem = nt(dk[T:], wk) + nt(dv[T:], wv)
    return own, mem


def first_kernel(at_ref, gain_ref, bias_ref, xp_ref, w_ref, mt_ref, qkv_ref, dmix_ref, npt_ref,
                 send_ref, keep_ref, mixed_ref, dn_ref, dnm_ref, kvm_ref, npt_all_ref, xhatm_ref):
    normed, xhat, _ = layer_norm(xp_ref, gain_ref[...].reshape(1, D), bias_ref[...].reshape(1, D))
    for i in range(2):
        kvm_ref[:, D * i : D * i + D] = nn(normed, w_ref[1 + i]).astype(BF)
    xhatm_ref[...] = xhat
    npt_all_ref[:, :T] = npt_ref[...]
    npt_all_ref[:, T:] = nt(mt_ref[...], normed).astype(BF)
    has = at_ref[4] > 0
    npt_all = npt_all_ref[...]
    for g in range(2):
        mixed, *grads = head_group(g, has, qkv_ref, kvm_ref, dmix_ref)
        mixed_ref[:, GW * g : GW * g + GW] = mixed
        own, mem = group_outputs(g, g, at_ref, npt_all, w_ref, grads, send_ref, keep_ref)
        if g == 0:
            dn_ref[...] = own
            dnm_ref[...] = mem
        else:
            dn_ref[...] += own
            dnm_ref[...] += mem


def second_kernel(at_ref, w_ref, mt_ref, cot_ref, qkv_ref, dmix_ref, mixed_in, dn_in, dnm_in, kvm_ref, npt_all_ref,
                  xhat_ref, xhatm_ref, send_ref, keep_ref, mixed_ref, dn_ref):
    mixed, *grads = head_group(2, at_ref[4] > 0, qkv_ref, kvm_ref, dmix_ref)
    mixed_ref[:, : 2 * GW] = mixed_in[...]
    mixed_ref[:, 2 * GW :] = mixed
    own, mem = group_outputs(2, 0, at_ref, npt_all_ref[...], w_ref, grads, send_ref, keep_ref)
    lhs = nt(mt_ref[...], mixed_ref[...]).astype(BF)
    put_rows(send_ref, keep_ref, 1, at_ref[3], lhs, cot_ref[...])
    dn, dnm = dn_in[...] + own, dnm_in[...] + mem
    dn_ref[...] = dn
    vec = jnp.concatenate(
        [jnp.sum(dn * xhat_ref[...] + dnm * xhatm_ref[...], axis=0, keepdims=True), jnp.sum(dn + dnm, axis=0, keepdims=True)],
        axis=0,
    )
    rows = split_rows(vec)
    for out_ref in (send_ref, keep_ref):
        out_ref[384:392, 0:D] = rows


def token_kernel(gain_ref, x_ref, cot_ref, mixed_ref, wo_ref, dn_ref, xhat_ref, rstd_ref, out_ref, dx_ref):
    out_ref[...] = (x_ref[...].astype(F32) + nn(mixed_ref[...], wo_ref[...])).astype(BF)
    d_hat = dn_ref[...] * gain_ref[...].reshape(1, D)
    xhat = xhat_ref[...]
    row = rstd_ref[:, 0:1] * (
        d_hat
        - jnp.mean(d_hat, axis=-1, keepdims=True)
        - xhat * jnp.mean(d_hat * xhat, axis=-1, keepdims=True)
    )
    dx_ref[...] = (cot_ref[...].astype(F32) + row).astype(BF)


def split_rows(value):
    high = value.astype(BF)
    low = (value - high.astype(F32)).astype(BF)
    return jnp.concatenate([high, low, jnp.zeros((4, value.shape[1]), BF)], axis=0)


def join_rows(rows):
    return rows[0:2].astype(F32) + rows[2:4].astype(F32)


def fold_rows(value):
    high = value.astype(BF)
    low = (value - high.astype(F32)).astype(BF)
    return jnp.concatenate([high[:, :384], high[:, 384:], low[:, :384], low[:, 384:]], axis=0)


def unfold_rows(rows):
    rows = rows.astype(F32)
    return jnp.concatenate([rows[0:2] + rows[4:6], rows[2:4] + rows[6:8]], axis=1)


def tree(a, b, c, d):
    return (a.astype(F32) + b.astype(F32)) + (c.astype(F32) + d.astype(F32))


RING_Y = (1, 3, 2)
RING_X = (2, 3, 1)


def halving_order(ring):
    one, two, far = ring
    return [((one, far), (0, two)), ((two, far), (0, one))]


def pair_a_kernel(keep_ref, recv_ref, *outs):
    for part, groups in enumerate(halving_order(RING_Y)):
        cols = slice(768 * part, 768 * part + 768)
        for kept, places in enumerate(groups):
            for i, k in enumerate(places):
                rows = slice(96 * k, 96 * k + 96)
                outs[2 * part + kept][96 * i : 96 * i + 96, :] = (
                    keep_ref[rows, cols].astype(F32) + recv_ref[rows, cols].astype(F32)
                ).astype(BF)


def pair_b_kernel(keep_ref, recv_ref, *outs):
    for part, groups in enumerate(halving_order(RING_X)):
        for kept, places in enumerate(groups):
            out = outs[2 * part + kept]
            for i, k in enumerate(places):
                at = 768 * (k & 1) + 384 * part
                for y in range(4):
                    rows = slice(96 * y + 48 * (k >> 1), 96 * y + 48 * (k >> 1) + 48)
                    out[192 * i + 48 * y : 192 * i + 48 * y + 48, :] = (
                        keep_ref[rows, at : at + 384].astype(F32) + recv_ref[rows, at : at + 384].astype(F32)
                    ).astype(BF)
    vec = fold_rows(join_rows(keep_ref[384:392, 0:D]) + join_rows(recv_ref[384:392, 0:D]))
    outs[0][384:392, :] = vec
    outs[1][384:392, :] = vec


def step_a_kernel(recv0_ref, keep0_ref, recv1_ref, keep1_ref, send0_ref, send1_ref, own_ref):
    for part, (recv, keep, send) in enumerate(((recv0_ref, keep0_ref, send0_ref), (recv1_ref, keep1_ref, send1_ref))):
        add = lambda rows: keep[rows, :].astype(F32) + recv[rows, :].astype(F32)
        own_ref[:, 768 * part : 768 * part + 768] = add(slice(0, 96))
        send[...] = add(slice(96, 192)).astype(BF)


def step_b_kernel(recv0_ref, keep0_ref, recv1_ref, keep1_ref, send0_ref, send1_ref, own_ref, vec_ref):
    for part, (recv, keep, send) in enumerate(((recv0_ref, keep0_ref, send0_ref), (recv1_ref, keep1_ref, send1_ref))):
        add = lambda rows: keep[rows, :].astype(F32) + recv[rows, :].astype(F32)
        own_ref[:, 384 * part : 384 * part + 384] = add(slice(0, 192))
        send[0:192, :] = add(slice(192, 384)).astype(BF)
    vec = unfold_rows(keep0_ref[384:392, :]) + unfold_rows(recv0_ref[384:392, :])
    rows = fold_rows(vec)
    vec_ref[...] = unfold_rows(rows)
    send0_ref[192:200, :] = rows


def mid_a_kernel(own_ref, recv0_ref, recv1_ref, *outs):
    for k in range(4):
        rows = slice(48 * (k >> 1), 48 * (k >> 1) + 48)
        recv = recv1_ref if k & 1 else recv0_ref
        outs[k][...] = (own_ref[rows, 768 * (k & 1) : 768 * (k & 1) + 768] + recv[rows, :].astype(F32)).astype(BF)


def mid_b_kernel(own_ref, vec_ref, recv0_ref, recv1_ref, *outs):
    vec = split_rows(vec_ref[...] + unfold_rows(recv0_ref[192:200, :]))
    for k in range(4):
        rows = slice(48 * k, 48 * k + 48)
        outs[k][0:48, 0:384] = (own_ref[rows, 0:384] + recv0_ref[rows, :].astype(F32)).astype(BF)
        outs[k][0:48, 384:768] = (own_ref[rows, 384:768] + recv1_ref[rows, :].astype(F32)).astype(BF)
        outs[k][48:56, :] = vec


def plane_kernel(a0, a1, a2, a3, b0, b1, b2, b3, out_ref):
    at = slice(48, 56)
    vec = (join_rows(b0[at]) + join_rows(b1[at])) + (join_rows(b2[at]) + join_rows(b3[at]))
    vec = jnp.concatenate([vec[0:1], vec[1:2]], axis=1)
    high = vec.astype(BF).astype(F32)
    tail = jnp.concatenate([high, vec - high], axis=0)
    g = slice(0, 48)
    sums = jnp.concatenate([tree(a0[...], a1[...], a2[...], a3[...]), tree(b0[g], b1[g], b2[g], b3[g])], axis=1)
    for z in range(8):
        out_ref[z] = jnp.concatenate([sums[6 * z : 6 * z + 6], tail], axis=0).astype(BF)


def column_kernel(factor, in_ref, rows_ref, gain_ref, bias_ref):
    acc = in_ref[0].astype(F32)
    for z in range(1, 8):
        acc = acc + in_ref[z].astype(F32)
    rows_ref[...] = acc.astype(BF)
    vec = (acc[6:7] + acc[7:8]) * factor
    gain_ref[...] = vec[:, :D].reshape(D)
    bias_ref[...] = vec[:, D:].reshape(D)


def finish_kernel(factor, at_ref, mine_ref, other_ref, qkv_ref, wout_ref):
    mine, other = mine_ref[...].astype(F32) * factor, other_ref[...].astype(F32) * factor
    first = at_ref[3] == 0
    halves = [jnp.where(first, mine, other), jnp.where(first, other, mine)]
    for g in range(GROUPS + 1):
        cols = slice(384 * g, 384 * g + 384)
        full = jnp.concatenate([halves[0][0:6, cols], halves[1][0:6, cols]], axis=1)
        if g < GROUPS:
            for i in range(3):
                at = D * i + GW * g
                qkv_ref[:, at : at + GW] = full[:, GW * i : GW * i + GW]
        else:
            wout_ref[...] = full


VM = pl.BlockSpec(memory_space=pltpu.VMEM)
SM = pl.BlockSpec(memory_space=pltpu.SMEM)
HBM = pl.BlockSpec(memory_space=pltpu.MemorySpace.HBM)


def call(kernel, name, out_shape, args, scalars=0, anys=(), scratch=(), limit=16):
    specs = [SM if i < scalars else HBM if i in anys else VM for i in range(len(args))]
    args = [pltpu.with_memory_space_constraint(a, pltpu.MemorySpace.HBM) if i in anys else a for i, a in enumerate(args)]
    return pl.pallas_call(
        kernel,
        name=name,
        in_specs=specs,
        out_specs=[VM] * len(out_shape),
        out_shape=out_shape,
        scratch_shapes=scratch,
        compiler_params=pltpu.CompilerParams(vmem_limit_bytes=limit * 1024 * 1024),
    )(*args)


def sds(*shape, dtype=BF):
    return jax.ShapeDtypeStruct(shape, dtype)


def on_device(layer_input, cotangent, gain, bias, w, wo):
    x, cot = layer_input[0], cotangent[0]
    seq = lax.axis_size(SEQ)
    xp = lax.ppermute(x, SEQ, [(i, i + 1) for i in range(seq - 1)])
    place = [lax.axis_index(n) for n in ("y", "xl", "c", "xh")] + [lax.axis_index(SEQ) > 0]
    at = jnp.stack([v.astype(jnp.int32) for v in place])
    row, mat, tokens = sds(T, D, dtype=F32), sds(D, D), sds(T, D)
    one = sds(D, dtype=F32)
    qkv, dmix, npt, xhat, rstd, mt, gain_v, bias_v, cot_v, w = call(
        own_kernel, "own_part",
        [sds(T, 3 * D), tokens, sds(D, T), row, sds(T, 128, dtype=F32), mat, one, one, tokens, sds(3, D, D)],
        [at, gain, bias, x, cot, w, wo], 1, (1, 2, 3, 4, 5, 6),
        [pltpu.VMEM((T, D), BF), pltpu.VMEM((D, D), BF), pltpu.SemaphoreType.DMA((8,))],
    )
    wide = sds(384, 1536)
    send_a, keep_a, mixed, dn, dnm, kvm, npt_all, xhatm = call(
        first_kernel, "memory_and_heads",
        [wide, wide, sds(T, 2 * GW), row, row, sds(T, 2 * D), sds(D, 2 * T), row],
        [at, gain_v, bias_v, xp, w, mt, qkv, dmix, npt], 1, limit=LIMIT,
    )
    send_b, keep_b, mixed, dn = call(
        second_kernel, "heads_and_output_weight",
        [sds(392, 1536), sds(392, 1536), tokens, row],
        [at, w, mt, cot_v, qkv, dmix, mixed, dn, dnm, kvm, npt_all, xhat, xhatm], 1, limit=LIMIT,
    )

    def swap(block):
        return lax.ppermute(block, "c", [(0, 1), (1, 0)])

    def permute(block, axes, k):
        n = lax.axis_size(axes)
        return lax.ppermute(block, axes, [(i, i ^ k) for i in range(n)])

    def exchange(parts, axes):
        return [parts[0]] + [permute(parts[k], axes, k) for k in (1, 2, 3)]

    half = sds(192, 768)
    send0_a, keep0_a, send1_a, keep1_a = call(pair_a_kernel, "pair_sum_a", [half] * 4, [keep_a, swap(send_a)])
    send0_b, keep0_b, send1_b, keep1_b = call(
        pair_b_kernel, "pair_sum_b", [sds(392, 384), sds(392, 384), sds(384, 384), sds(384, 384)],
        [keep_b, swap(send_b)],
    )
    got_a = [permute(send0_a, "y", RING_Y[0]), permute(send1_a, "y", RING_Y[1])]
    got_b = [permute(send0_b, ROW, RING_X[0]), permute(send1_b, ROW, RING_X[1])]
    out, dx = call(
        token_kernel, "token_outputs", [tokens, tokens],
        [gain, x, cot, mixed, wo, dn, xhat, rstd],
    )
    send0_a, send1_a, own_a = call(
        step_a_kernel, "step_sum_a", [sds(96, 768), sds(96, 768), sds(96, 1536, dtype=F32)],
        [got_a[0], keep0_a, got_a[1], keep1_a],
    )
    got_a = [permute(send0_a, "y", RING_Y[1]), permute(send1_a, "y", RING_Y[0])]
    send0_b, send1_b, own_b, vec = call(
        step_b_kernel, "step_sum_b", [sds(200, 384), sds(192, 384), sds(192, 768, dtype=F32), sds(2, D, dtype=F32)],
        [got_b[0], keep0_b, got_b[1], keep1_b],
    )
    got_b = [permute(send0_b, ROW, RING_X[1]), permute(send1_b, ROW, RING_X[0])]
    parts_a = call(mid_a_kernel, "middle_sum_a", [sds(48, 768)] * 4, [own_a, *got_a])
    parts_b = call(mid_b_kernel, "middle_sum_b", [sds(56, 768)] * 4, [own_b, vec, *got_b])
    parts_a = exchange(parts_a, ROW)
    parts_b = exchange(parts_b, "y")
    (mine,) = call(plane_kernel, "plane_sum", [sds(8, 8, 1536)], [*parts_a, *parts_b])
    mine = lax.all_to_all(mine, "z", 0, 0, tiled=True)
    factor = 1.0 / float(seq * lax.axis_size("xh") * T) ** 0.5
    mine, grad_gain, grad_bias = call(
        functools.partial(column_kernel, factor), "column_sum",
        [sds(8, 1536), sds(D, dtype=F32), sds(D, dtype=F32)], [mine],
    )
    other = lax.ppermute(mine, "xh", [(0, 1), (1, 0)])
    grad_qkv, grad_out = call(
        functools.partial(finish_kernel, factor), "finish",
        [sds(6, 3 * D, dtype=F32), sds(6, D, dtype=F32)], [at, mine, other], 1,
    )
    return out[None], dx[None], grad_qkv, grad_out, grad_gain, grad_bias


def solution(mesh):
    torus = Mesh(mesh.devices.reshape(4, 8, 2, 2, 2), ("y", "z", "xl", "c", "xh"))
    return jax.shard_map(
        on_device,
        mesh=torus,
        in_specs=(P("xh", SEQ, None), P("xh", SEQ, None), P(), P(), P(), P()),
        out_specs=(P("xh", SEQ, None), P("xh", SEQ, None), P(SEQ, None), P(SEQ, None), P(), P()),
        check_vma=False,
    )
```

```python
import functools

import jax
import jax.numpy as jnp
from jax import lax
from jax.experimental import pallas as pl
from jax.experimental.pallas import tpu as pltpu
from jax.sharding import Mesh
from jax.sharding import PartitionSpec as P

HEADS = 12
EPS = 1e-05
SEQ = ("y", "z", "xl", "c")
ROW = ("xl", "xh")
T = 256
D = 768
GROUPS = 3
GW = 256
BF = jnp.bfloat16
F32 = jnp.float32
LIMIT = 24


def nn(a, b):
    return lax.dot_general(a, b, (((1,), (0,)), ((), ())), preferred_element_type=F32)


def nt(a, b):
    return lax.dot_general(a, b, (((1,), (1,)), ((), ())), preferred_element_type=F32)


def tn(a, b):
    return lax.dot_general(a, b, (((0,), (0,)), ((), ())), preferred_element_type=F32)


def layer_norm(x_ref, gain, bias):
    values = x_ref[...].astype(F32)
    centered = values - jnp.mean(values, axis=-1, keepdims=True)
    rstd = lax.rsqrt(jnp.mean(centered * centered, axis=-1, keepdims=True) + EPS)
    xhat = centered * rstd
    normed = (xhat * gain + bias).astype(BF)
    return normed, xhat, rstd


def row_order(at_ref):
    p = lax.broadcasted_iota(jnp.int32, (D, 1), 0)
    second = jnp.where(p >= 384, 1, 0)
    q = p - 384 * second
    owner = (q * 171) >> 13
    b = q - 48 * owner
    z = (b * 43) >> 8
    j = b - 6 * z
    y, xl = (owner >> 1) ^ at_ref[0], (owner & 1) ^ at_ref[1]
    to_core = jnp.where(second == 1, at_ref[2], 1 - at_ref[2])
    feature = ((y * 8 + z) * 2 + xl) * 12 + to_core * 6 + j
    cols = lax.broadcasted_iota(jnp.int32, (D, D), 1)
    return jnp.where(cols == feature, 1.0, 0.0).astype(BF)


def own_kernel(at_ref, gain_hbm, bias_hbm, x_hbm, cot_hbm, w_hbm, wo_hbm,
               qkv_ref, dmix_ref, npt_ref, xhat_ref, rstd_ref, mt_ref, gain_ref, bias_ref, cot_ref, w_ref,
               x_ref, wo_ref, sems):
    copies = [
        pltpu.make_async_copy(x_hbm, x_ref, sems.at[0]),
        pltpu.make_async_copy(gain_hbm, gain_ref, sems.at[1]),
        pltpu.make_async_copy(bias_hbm, bias_ref, sems.at[2]),
        pltpu.make_async_copy(cot_hbm, cot_ref, sems.at[3]),
        pltpu.make_async_copy(wo_hbm, wo_ref, sems.at[4]),
    ]
    for i in range(3):
        copies.append(pltpu.make_async_copy(w_hbm.at[:, pl.ds(D * i, D)], w_ref.at[i], sems.at[5 + i]))
    for copy in copies:
        copy.start()
    mt = row_order(at_ref)
    mt_ref[...] = mt
    for copy in copies[:3]:
        copy.wait()
    normed, xhat, rstd = layer_norm(x_ref, gain_ref[...].reshape(1, D), bias_ref[...].reshape(1, D))
    xhat_ref[...] = xhat
    rstd_ref[...] = jnp.broadcast_to(rstd, (T, 128))
    npt_ref[...] = nt(mt, normed).astype(BF)
    copies[3].wait()
    copies[4].wait()
    dmix_ref[...] = nt(cot_ref[...], wo_ref[...]).astype(BF)
    for i in range(3):
        copies[5 + i].wait()
        qkv_ref[:, D * i : D * i + D] = nn(normed, w_ref[i]).astype(BF)


def head_group(g, has, qkv_ref, kvm_ref, dmix_ref):
    at = GW * g
    lanes = lax.broadcasted_iota(jnp.int32, (T, 128), 1)
    low = lanes < 64
    causal = lax.broadcasted_iota(jnp.int32, (T, T), 0) <= lax.broadcasted_iota(jnp.int32, (T, T), 1)
    low_keys = lax.broadcasted_iota(jnp.int32, (2 * T, 128), 1) < 64
    zero = jnp.zeros((), BF)
    mixes, dqs, dks, dvs = [], [], [], []
    for pair in range(2):
        cq = slice(at + 128 * pair, at + 128 * pair + 128)
        ck = slice(D + cq.start, D + cq.stop)
        cv = slice(2 * D + cq.start, 2 * D + cq.stop)
        q2 = (qkv_ref[:, cq].astype(F32) * 0.125).astype(BF)
        k2 = jnp.concatenate([qkv_ref[:, ck], kvm_ref[:, cq]], axis=0)
        v2 = jnp.concatenate([qkv_ref[:, cv], kvm_ref[:, ck]], axis=0)
        dm2 = dmix_ref[:, cq]
        k_parts = [jnp.where(low_keys, k2, zero), jnp.where(low_keys, zero, k2)]
        v_parts = [jnp.where(low_keys, v2, zero), jnp.where(low_keys, zero, v2)]
        ds_parts, p_parts, q_parts, dm_parts = [], [], [], []
        for half in range(2):
            pick = low if half == 0 else jnp.logical_not(low)
            qa = jnp.where(pick, q2, zero)
            dma = jnp.where(pick, dm2, zero)
            st = nt(k2, qa)
            st_own = jnp.where(causal, st[:T], -1e30)
            st_mem = jnp.where(has, st[T:], -1e30)
            st = jnp.concatenate([st_own, st_mem], axis=0)
            top = jnp.max(st, axis=0, keepdims=True)
            e = jnp.exp(st - top)
            p = e * (1.0 / jnp.sum(e, axis=0, keepdims=True))
            pb = p.astype(BF)
            dp = nt(v2, dma)
            ds = (p * (dp - jnp.sum(dp * p, axis=0, keepdims=True))).astype(BF)
            ds_parts.append(ds)
            p_parts.append(pb)
            q_parts.append(qa)
            dm_parts.append(dma)
        dks.append(nn(jnp.concatenate(ds_parts, axis=1), jnp.concatenate(q_parts, axis=0)).astype(BF))
        dvs.append(nn(jnp.concatenate(p_parts, axis=1), jnp.concatenate(dm_parts, axis=0)).astype(BF))
        mixes.append(tn(jnp.concatenate(p_parts, axis=0), jnp.concatenate(v_parts, axis=0)).astype(BF))
        dqs.append((tn(jnp.concatenate(ds_parts, axis=0), jnp.concatenate(k_parts, axis=0)) * 0.125).astype(BF))
    dq = jnp.concatenate(dqs, axis=1)
    dk = jnp.concatenate(dks, axis=1)
    dv = jnp.concatenate(dvs, axis=1)
    return jnp.concatenate(mixes, axis=1), dq, dk, dv


def put_rows(send_ref, keep_ref, slot, xh, lhs, rhs):
    first, second = rhs[:, :384], rhs[:, 384:]
    mine = xh == 0
    rhs = jnp.concatenate([jnp.where(mine, first, second), jnp.where(mine, second, first)], axis=1)
    for out_ref, rows in ((send_ref, lhs[:384]), (keep_ref, lhs[384:])):
        sums = nn(rows, rhs).astype(BF)
        for r in range(2):
            at = 768 * r + 384 * slot
            out_ref[0:384, at : at + 384] = sums[:, 384 * r : 384 * r + 384]


def group_outputs(g, slot, at_ref, npt_all, w_ref, grads, send_ref, keep_ref):
    dq, dk, dv = grads
    rhs = jnp.concatenate([jnp.concatenate([dq, jnp.zeros((T, GW), BF)], axis=0), dk, dv], axis=1)
    put_rows(send_ref, keep_ref, slot, at_ref[3], npt_all, rhs)
    wq, wk, wv = (w_ref[i, :, GW * g : GW * g + GW] for i in range(3))
    own = nt(dq, wq) + nt(dk[:T], wk) + nt(dv[:T], wv)
    mem = nt(dk[T:], wk) + nt(dv[T:], wv)
    return own, mem


def first_kernel(at_ref, gain_ref, bias_ref, xp_ref, w_ref, mt_ref, qkv_ref, dmix_ref, npt_ref,
                 send_ref, keep_ref, mixed_ref, dn_ref, dnm_ref, kvm_ref, npt_all_ref, xhatm_ref):
    normed, xhat, _ = layer_norm(xp_ref, gain_ref[...].reshape(1, D), bias_ref[...].reshape(1, D))
    for i in range(2):
        kvm_ref[:, D * i : D * i + D] = nn(normed, w_ref[1 + i]).astype(BF)
    xhatm_ref[...] = xhat
    npt_all_ref[:, :T] = npt_ref[...]
    npt_all_ref[:, T:] = nt(mt_ref[...], normed).astype(BF)
    has = at_ref[4] > 0
    npt_all = npt_all_ref[...]
    for g in range(2):
        mixed, *grads = head_group(g, has, qkv_ref, kvm_ref, dmix_ref)
        mixed_ref[:, GW * g : GW * g + GW] = mixed
        own, mem = group_outputs(g, g, at_ref, npt_all, w_ref, grads, send_ref, keep_ref)
        if g == 0:
            dn_ref[...] = own
            dnm_ref[...] = mem
        else:
            dn_ref[...] += own
            dnm_ref[...] += mem


def second_kernel(at_ref, w_ref, mt_ref, cot_ref, qkv_ref, dmix_ref, mixed_in, dn_in, dnm_in, kvm_ref, npt_all_ref,
                  xhat_ref, xhatm_ref, send_ref, keep_ref, mixed_ref, dn_ref):
    mixed, *grads = head_group(2, at_ref[4] > 0, qkv_ref, kvm_ref, dmix_ref)
    mixed_ref[:, : 2 * GW] = mixed_in[...]
    mixed_ref[:, 2 * GW :] = mixed
    own, mem = group_outputs(2, 0, at_ref, npt_all_ref[...], w_ref, grads, send_ref, keep_ref)
    lhs = nt(mt_ref[...], mixed_ref[...]).astype(BF)
    put_rows(send_ref, keep_ref, 1, at_ref[3], lhs, cot_ref[...])
    dn, dnm = dn_in[...] + own, dnm_in[...] + mem
    dn_ref[...] = dn
    vec = jnp.concatenate(
        [jnp.sum(dn * xhat_ref[...] + dnm * xhatm_ref[...], axis=0, keepdims=True), jnp.sum(dn + dnm, axis=0, keepdims=True)],
        axis=0,
    )
    rows = split_rows(vec)
    for out_ref in (send_ref, keep_ref):
        out_ref[384:392, 0:D] = rows


def token_kernel(gain_ref, x_ref, cot_ref, mixed_ref, wo_ref, dn_ref, xhat_ref, rstd_ref, out_ref, dx_ref):
    out_ref[...] = (x_ref[...].astype(F32) + nn(mixed_ref[...], wo_ref[...])).astype(BF)
    d_hat = dn_ref[...] * gain_ref[...].reshape(1, D)
    xhat = xhat_ref[...]
    row = rstd_ref[:, 0:1] * (
        d_hat
        - jnp.mean(d_hat, axis=-1, keepdims=True)
        - xhat * jnp.mean(d_hat * xhat, axis=-1, keepdims=True)
    )
    dx_ref[...] = (cot_ref[...].astype(F32) + row).astype(BF)


def split_rows(value):
    high = value.astype(BF)
    low = (value - high.astype(F32)).astype(BF)
    return jnp.concatenate([high, low, jnp.zeros((4, value.shape[1]), BF)], axis=0)


def join_rows(rows):
    return rows[0:2].astype(F32) + rows[2:4].astype(F32)


def fold_rows(value):
    high = value.astype(BF)
    low = (value - high.astype(F32)).astype(BF)
    return jnp.concatenate([high[:, :384], high[:, 384:], low[:, :384], low[:, 384:]], axis=0)


def unfold_rows(rows):
    rows = rows.astype(F32)
    return jnp.concatenate([rows[0:2] + rows[4:6], rows[2:4] + rows[6:8]], axis=1)


def tree(a, b, c, d):
    return (a.astype(F32) + b.astype(F32)) + (c.astype(F32) + d.astype(F32))


RING_Y = (1, 3, 2)
RING_X = (2, 3, 1)


def halving_order(ring):
    one, two, far = ring
    return [((one, far), (0, two)), ((two, far), (0, one))]


def pair_a_kernel(keep_ref, recv_ref, *outs):
    for part, groups in enumerate(halving_order(RING_Y)):
        cols = slice(768 * part, 768 * part + 768)
        for kept, places in enumerate(groups):
            for i, k in enumerate(places):
                rows = slice(96 * k, 96 * k + 96)
                outs[2 * part + kept][96 * i : 96 * i + 96, :] = (
                    keep_ref[rows, cols].astype(F32) + recv_ref[rows, cols].astype(F32)
                ).astype(BF)


def pair_b_kernel(keep_ref, recv_ref, *outs):
    for part, groups in enumerate(halving_order(RING_X)):
        for kept, places in enumerate(groups):
            out = outs[2 * part + kept]
            for i, k in enumerate(places):
                at = 768 * (k & 1) + 384 * part
                for y in range(4):
                    rows = slice(96 * y + 48 * (k >> 1), 96 * y + 48 * (k >> 1) + 48)
                    out[192 * i + 48 * y : 192 * i + 48 * y + 48, :] = (
                        keep_ref[rows, at : at + 384].astype(F32) + recv_ref[rows, at : at + 384].astype(F32)
                    ).astype(BF)
    vec = fold_rows(join_rows(keep_ref[384:392, 0:D]) + join_rows(recv_ref[384:392, 0:D]))
    outs[0][384:392, :] = vec
    outs[1][384:392, :] = vec


def step_a_kernel(recv0_ref, keep0_ref, recv1_ref, keep1_ref, send0_ref, send1_ref, own_ref):
    for part, (recv, keep, send) in enumerate(((recv0_ref, keep0_ref, send0_ref), (recv1_ref, keep1_ref, send1_ref))):
        add = lambda rows: keep[rows, :].astype(F32) + recv[rows, :].astype(F32)
        own_ref[:, 768 * part : 768 * part + 768] = add(slice(0, 96))
        send[...] = add(slice(96, 192)).astype(BF)


def step_b_kernel(recv0_ref, keep0_ref, recv1_ref, keep1_ref, send0_ref, send1_ref, own_ref, vec_ref):
    for part, (recv, keep, send) in enumerate(((recv0_ref, keep0_ref, send0_ref), (recv1_ref, keep1_ref, send1_ref))):
        add = lambda rows: keep[rows, :].astype(F32) + recv[rows, :].astype(F32)
        own_ref[:, 384 * part : 384 * part + 384] = add(slice(0, 192))
        send[0:192, :] = add(slice(192, 384)).astype(BF)
    vec = unfold_rows(keep0_ref[384:392, :]) + unfold_rows(recv0_ref[384:392, :])
    rows = fold_rows(vec)
    vec_ref[...] = unfold_rows(rows)
    send0_ref[192:200, :] = rows


def mid_a_kernel(own_ref, recv0_ref, recv1_ref, *outs):
    for k in range(4):
        rows = slice(48 * (k >> 1), 48 * (k >> 1) + 48)
        recv = recv1_ref if k & 1 else recv0_ref
        outs[k][...] = (own_ref[rows, 768 * (k & 1) : 768 * (k & 1) + 768] + recv[rows, :].astype(F32)).astype(BF)


def mid_b_kernel(own_ref, vec_ref, recv0_ref, recv1_ref, *outs):
    vec = split_rows(vec_ref[...] + unfold_rows(recv0_ref[192:200, :]))
    for k in range(4):
        rows = slice(48 * k, 48 * k + 48)
        outs[k][0:48, 0:384] = (own_ref[rows, 0:384] + recv0_ref[rows, :].astype(F32)).astype(BF)
        outs[k][0:48, 384:768] = (own_ref[rows, 384:768] + recv1_ref[rows, :].astype(F32)).astype(BF)
        outs[k][48:56, :] = vec


def plane_kernel(a0, a1, a2, a3, b0, b1, b2, b3, out_ref):
    at = slice(48, 56)
    vec = (join_rows(b0[at]) + join_rows(b1[at])) + (join_rows(b2[at]) + join_rows(b3[at]))
    vec = jnp.concatenate([vec[0:1], vec[1:2]], axis=1)
    high = vec.astype(BF).astype(F32)
    tail = jnp.concatenate([high, vec - high], axis=0)
    g = slice(0, 48)
    sums = jnp.concatenate([tree(a0[...], a1[...], a2[...], a3[...]), tree(b0[g], b1[g], b2[g], b3[g])], axis=1)
    for z in range(8):
        out_ref[z] = jnp.concatenate([sums[6 * z : 6 * z + 6], tail], axis=0).astype(BF)


def column_kernel(factor, in_ref, rows_ref, gain_ref, bias_ref):
    acc = in_ref[0].astype(F32)
    for z in range(1, 8):
        acc = acc + in_ref[z].astype(F32)
    rows_ref[...] = acc.astype(BF)
    vec = (acc[6:7] + acc[7:8]) * factor
    gain_ref[...] = vec[:, :D].reshape(D)
    bias_ref[...] = vec[:, D:].reshape(D)


def finish_kernel(factor, at_ref, mine_ref, other_ref, qkv_ref, wout_ref):
    mine, other = mine_ref[...].astype(F32) * factor, other_ref[...].astype(F32) * factor
    first = at_ref[3] == 0
    halves = [jnp.where(first, mine, other), jnp.where(first, other, mine)]
    for g in range(GROUPS + 1):
        cols = slice(384 * g, 384 * g + 384)
        full = jnp.concatenate([halves[0][0:6, cols], halves[1][0:6, cols]], axis=1)
        if g < GROUPS:
            for i in range(3):
                at = D * i + GW * g
                qkv_ref[:, at : at + GW] = full[:, GW * i : GW * i + GW]
        else:
            wout_ref[...] = full


VM = pl.BlockSpec(memory_space=pltpu.VMEM)
SM = pl.BlockSpec(memory_space=pltpu.SMEM)
HBM = pl.BlockSpec(memory_space=pltpu.MemorySpace.HBM)


def call(kernel, name, out_shape, args, scalars=0, anys=(), scratch=(), limit=16):
    specs = [SM if i < scalars else HBM if i in anys else VM for i in range(len(args))]
    args = [pltpu.with_memory_space_constraint(a, pltpu.MemorySpace.HBM) if i in anys else a for i, a in enumerate(args)]
    return pl.pallas_call(
        kernel,
        name=name,
        in_specs=specs,
        out_specs=[VM] * len(out_shape),
        out_shape=out_shape,
        scratch_shapes=scratch,
        compiler_params=pltpu.CompilerParams(vmem_limit_bytes=limit * 1024 * 1024),
    )(*args)


def sds(*shape, dtype=BF):
    return jax.ShapeDtypeStruct(shape, dtype)


def on_device(layer_input, cotangent, gain, bias, w, wo):
    x, cot = layer_input[0], cotangent[0]
    seq = lax.axis_size(SEQ)
    xp = lax.ppermute(x, SEQ, [(i, i + 1) for i in range(seq - 1)])
    place = [lax.axis_index(n) for n in ("y", "xl", "c", "xh")] + [lax.axis_index(SEQ) > 0]
    at = jnp.stack([v.astype(jnp.int32) for v in place])
    row, mat, tokens = sds(T, D, dtype=F32), sds(D, D), sds(T, D)
    one = sds(D, dtype=F32)
    qkv, dmix, npt, xhat, rstd, mt, gain_v, bias_v, cot_v, w = call(
        own_kernel, "own_part",
        [sds(T, 3 * D), tokens, sds(D, T), row, sds(T, 128, dtype=F32), mat, one, one, tokens, sds(3, D, D)],
        [at, gain, bias, x, cot, w, wo], 1, (1, 2, 3, 4, 5, 6),
        [pltpu.VMEM((T, D), BF), pltpu.VMEM((D, D), BF), pltpu.SemaphoreType.DMA((8,))],
    )
    wide = sds(384, 1536)
    send_a, keep_a, mixed, dn, dnm, kvm, npt_all, xhatm = call(
        first_kernel, "memory_and_heads",
        [wide, wide, sds(T, 2 * GW), row, row, sds(T, 2 * D), sds(D, 2 * T), row],
        [at, gain_v, bias_v, xp, w, mt, qkv, dmix, npt], 1, limit=LIMIT,
    )
    def swap(block):
        return lax.ppermute(block, "c", [(0, 1), (1, 0)])

    def permute(block, axes, k):
        n = lax.axis_size(axes)
        return lax.ppermute(block, axes, [(i, i ^ k) for i in range(n)])

    def exchange(parts, axes):
        return [parts[0]] + [permute(parts[k], axes, k) for k in (1, 2, 3)]

    half = sds(192, 768)
    send0_a, keep0_a, send1_a, keep1_a = call(pair_a_kernel, "pair_sum_a", [half] * 4, [keep_a, swap(send_a)])
    got_a = [permute(send0_a, "y", RING_Y[0]), permute(send1_a, "y", RING_Y[1])]
    keep0_a, kvm = lax.optimization_barrier((keep0_a, kvm))
    send_b, keep_b, mixed, dn = call(
        second_kernel, "heads_and_output_weight",
        [sds(392, 1536), sds(392, 1536), tokens, row],
        [at, w, mt, cot_v, qkv, dmix, mixed, dn, dnm, kvm, npt_all, xhat, xhatm], 1, limit=LIMIT,
    )

    send_b, *got_a = lax.optimization_barrier((send_b, *got_a))
    recv_b = swap(send_b)
    send0_a, send1_a, own_a = call(
        step_a_kernel, "step_sum_a", [sds(96, 768), sds(96, 768), sds(96, 1536, dtype=F32)],
        [got_a[0], keep0_a, got_a[1], keep1_a],
    )
    got_a = [permute(send0_a, "y", RING_Y[1]), permute(send1_a, "y", RING_Y[0])]
    keep_b, own_a = lax.optimization_barrier((keep_b, own_a))
    send0_b, keep0_b, send1_b, keep1_b = call(
        pair_b_kernel, "pair_sum_b", [sds(392, 384), sds(392, 384), sds(384, 384), sds(384, 384)],
        [keep_b, recv_b],
    )
    got_b = [permute(send0_b, ROW, RING_X[0]), permute(send1_b, ROW, RING_X[1])]
    out, dx = call(
        token_kernel, "token_outputs", [tokens, tokens],
        [gain, x, cot, mixed, wo, dn, xhat, rstd],
    )
    parts_a = call(mid_a_kernel, "middle_sum_a", [sds(48, 768)] * 4, [own_a, *got_a])
    parts_a = exchange(parts_a, ROW)
    keep0_b, parts_a[0] = lax.optimization_barrier((keep0_b, parts_a[0]))
    send0_b, send1_b, own_b, vec = call(
        step_b_kernel, "step_sum_b", [sds(200, 384), sds(192, 384), sds(192, 768, dtype=F32), sds(2, D, dtype=F32)],
        [got_b[0], keep0_b, got_b[1], keep1_b],
    )
    got_b = [permute(send0_b, ROW, RING_X[1]), permute(send1_b, ROW, RING_X[0])]
    own_b, *parts_a = lax.optimization_barrier((own_b, *parts_a))
    parts_b = call(mid_b_kernel, "middle_sum_b", [sds(56, 768)] * 4, [own_b, vec, *got_b])
    parts_b = exchange(parts_b, "y")
    (mine,) = call(plane_kernel, "plane_sum", [sds(8, 8, 1536)], [*parts_a, *parts_b])
    mine = lax.all_to_all(mine, "z", 0, 0, tiled=True)
    factor = 1.0 / float(seq * lax.axis_size("xh") * T) ** 0.5
    mine, grad_gain, grad_bias = call(
        functools.partial(column_kernel, factor), "column_sum",
        [sds(8, 1536), sds(D, dtype=F32), sds(D, dtype=F32)], [mine],
    )
    other = lax.ppermute(mine, "xh", [(0, 1), (1, 0)])
    grad_qkv, grad_out = call(
        functools.partial(finish_kernel, factor), "finish",
        [sds(6, 3 * D, dtype=F32), sds(6, D, dtype=F32)], [at, mine, other], 1,
    )
    return out[None], dx[None], grad_qkv, grad_out, grad_gain, grad_bias


def solution(mesh):
    torus = Mesh(mesh.devices.reshape(4, 8, 2, 2, 2), ("y", "z", "xl", "c", "xh"))
    return jax.shard_map(
        on_device,
        mesh=torus,
        in_specs=(P("xh", SEQ, None), P("xh", SEQ, None), P(), P(), P(), P()),
        out_specs=(P("xh", SEQ, None), P("xh", SEQ, None), P(SEQ, None), P(SEQ, None), P(), P()),
        check_vma=False,
    )
```

```python
import functools

import jax
import jax.numpy as jnp
from jax import lax
from jax.experimental import pallas as pl
from jax.experimental.pallas import tpu as pltpu
from jax.sharding import Mesh
from jax.sharding import PartitionSpec as P

HEADS = 12
EPS = 1e-05
SEQ = ("y", "z", "xl", "c")
ROW = ("xl", "xh")
T = 256
D = 768
GROUPS = 3
GW = 256
BF = jnp.bfloat16
F32 = jnp.float32
LIMIT = 24


def nn(a, b):
    return lax.dot_general(a, b, (((1,), (0,)), ((), ())), preferred_element_type=F32)


def nt(a, b):
    return lax.dot_general(a, b, (((1,), (1,)), ((), ())), preferred_element_type=F32)


def tn(a, b):
    return lax.dot_general(a, b, (((0,), (0,)), ((), ())), preferred_element_type=F32)


def layer_norm(x_ref, gain, bias):
    values = x_ref[...].astype(F32)
    centered = values - jnp.mean(values, axis=-1, keepdims=True)
    rstd = lax.rsqrt(jnp.mean(centered * centered, axis=-1, keepdims=True) + EPS)
    xhat = centered * rstd
    normed = (xhat * gain + bias).astype(BF)
    return normed, xhat, rstd


def row_order(at_ref):
    p = lax.broadcasted_iota(jnp.int32, (D, 1), 0)
    second = jnp.where(p >= 384, 1, 0)
    q = p - 384 * second
    owner = (q * 171) >> 13
    b = q - 48 * owner
    z = (b * 43) >> 8
    j = b - 6 * z
    y, xl = (owner >> 1) ^ at_ref[0], (owner & 1) ^ at_ref[1]
    to_core = jnp.where(second == 1, at_ref[2], 1 - at_ref[2])
    feature = ((y * 8 + z) * 2 + xl) * 12 + to_core * 6 + j
    cols = lax.broadcasted_iota(jnp.int32, (D, D), 1)
    return jnp.where(cols == feature, 1.0, 0.0).astype(BF)


def own_kernel(at_ref, gain_hbm, bias_hbm, x_hbm, cot_hbm, w_hbm, wo_hbm,
               qkv_ref, dmix_ref, npt_ref, xhat_ref, rstd_ref, mt_ref, gain_ref, bias_ref, cot_ref, w_ref,
               x_ref, wo_ref, sems):
    copies = [
        pltpu.make_async_copy(x_hbm, x_ref, sems.at[0]),
        pltpu.make_async_copy(gain_hbm, gain_ref, sems.at[1]),
        pltpu.make_async_copy(bias_hbm, bias_ref, sems.at[2]),
        pltpu.make_async_copy(cot_hbm, cot_ref, sems.at[3]),
        pltpu.make_async_copy(wo_hbm, wo_ref, sems.at[4]),
    ]
    for i in range(3):
        copies.append(pltpu.make_async_copy(w_hbm.at[:, pl.ds(D * i, D)], w_ref.at[i], sems.at[5 + i]))
    for copy in copies:
        copy.start()
    mt = row_order(at_ref)
    mt_ref[...] = mt
    for copy in copies[:3]:
        copy.wait()
    normed, xhat, rstd = layer_norm(x_ref, gain_ref[...].reshape(1, D), bias_ref[...].reshape(1, D))
    xhat_ref[...] = xhat
    rstd_ref[...] = jnp.broadcast_to(rstd, (T, 128))
    npt_ref[...] = nt(mt, normed).astype(BF)
    copies[3].wait()
    copies[4].wait()
    dmix_ref[...] = nt(cot_ref[...], wo_ref[...]).astype(BF)
    for i in range(3):
        copies[5 + i].wait()
        qkv_ref[:, D * i : D * i + D] = nn(normed, w_ref[i]).astype(BF)


def head_group(g, has, qkv_ref, kvm_ref, dmix_ref):
    at = GW * g
    lanes = lax.broadcasted_iota(jnp.int32, (T, 128), 1)
    low = lanes < 64
    causal = lax.broadcasted_iota(jnp.int32, (T, T), 0) <= lax.broadcasted_iota(jnp.int32, (T, T), 1)
    low_keys = lax.broadcasted_iota(jnp.int32, (2 * T, 128), 1) < 64
    zero = jnp.zeros((), BF)
    mixes, dqs, dks, dvs = [], [], [], []
    for pair in range(2):
        cq = slice(at + 128 * pair, at + 128 * pair + 128)
        ck = slice(D + cq.start, D + cq.stop)
        cv = slice(2 * D + cq.start, 2 * D + cq.stop)
        q2 = (qkv_ref[:, cq].astype(F32) * 0.125).astype(BF)
        k2 = jnp.concatenate([qkv_ref[:, ck], kvm_ref[:, cq]], axis=0)
        v2 = jnp.concatenate([qkv_ref[:, cv], kvm_ref[:, ck]], axis=0)
        dm2 = dmix_ref[:, cq]
        k_parts = [jnp.where(low_keys, k2, zero), jnp.where(low_keys, zero, k2)]
        v_parts = [jnp.where(low_keys, v2, zero), jnp.where(low_keys, zero, v2)]
        ds_parts, p_parts, q_parts, dm_parts = [], [], [], []
        for half in range(2):
            pick = low if half == 0 else jnp.logical_not(low)
            qa = jnp.where(pick, q2, zero)
            dma = jnp.where(pick, dm2, zero)
            st = nt(k2, qa)
            st_own = jnp.where(causal, st[:T], -1e30)
            st_mem = jnp.where(has, st[T:], -1e30)
            st = jnp.concatenate([st_own, st_mem], axis=0)
            top = jnp.max(st, axis=0, keepdims=True)
            e = jnp.exp(st - top)
            p = e * (1.0 / jnp.sum(e, axis=0, keepdims=True))
            pb = p.astype(BF)
            dp = nt(v2, dma)
            ds = (p * (dp - jnp.sum(dp * p, axis=0, keepdims=True))).astype(BF)
            ds_parts.append(ds)
            p_parts.append(pb)
            q_parts.append(qa)
            dm_parts.append(dma)
        dks.append(nn(jnp.concatenate(ds_parts, axis=1), jnp.concatenate(q_parts, axis=0)).astype(BF))
        dvs.append(nn(jnp.concatenate(p_parts, axis=1), jnp.concatenate(dm_parts, axis=0)).astype(BF))
        mixes.append(tn(jnp.concatenate(p_parts, axis=0), jnp.concatenate(v_parts, axis=0)).astype(BF))
        dqs.append((tn(jnp.concatenate(ds_parts, axis=0), jnp.concatenate(k_parts, axis=0)) * 0.125).astype(BF))
    dq = jnp.concatenate(dqs, axis=1)
    dk = jnp.concatenate(dks, axis=1)
    dv = jnp.concatenate(dvs, axis=1)
    return jnp.concatenate(mixes, axis=1), dq, dk, dv


def put_rows(send_ref, keep_ref, slot, xh, lhs, rhs):
    first, second = rhs[:, :384], rhs[:, 384:]
    mine = xh == 0
    rhs = jnp.concatenate([jnp.where(mine, first, second), jnp.where(mine, second, first)], axis=1)
    for out_ref, rows in ((send_ref, lhs[:384]), (keep_ref, lhs[384:])):
        sums = nn(rows, rhs).astype(BF)
        for r in range(2):
            at = 768 * r + 384 * slot
            out_ref[0:384, at : at + 384] = sums[:, 384 * r : 384 * r + 384]


def group_outputs(g, slot, at_ref, npt_all, w_ref, grads, send_ref, keep_ref):
    dq, dk, dv = grads
    rhs = jnp.concatenate([jnp.concatenate([dq, jnp.zeros((T, GW), BF)], axis=0), dk, dv], axis=1)
    put_rows(send_ref, keep_ref, slot, at_ref[3], npt_all, rhs)
    wq, wk, wv = (w_ref[i, :, GW * g : GW * g + GW] for i in range(3))
    own = nt(dq, wq) + nt(dk[:T], wk) + nt(dv[:T], wv)
    mem = nt(dk[T:], wk) + nt(dv[T:], wv)
    return own, mem


def first_kernel(at_ref, gain_ref, bias_ref, xp_ref, w_ref, mt_ref, qkv_ref, dmix_ref, npt_ref,
                 send_ref, keep_ref, mixed_ref, dn_ref, dnm_ref, kvm_ref, npt_all_ref, xhatm_ref):
    normed, xhat, _ = layer_norm(xp_ref, gain_ref[...].reshape(1, D), bias_ref[...].reshape(1, D))
    for i in range(2):
        kvm_ref[:, D * i : D * i + D] = nn(normed, w_ref[1 + i]).astype(BF)
    xhatm_ref[...] = xhat
    npt_all_ref[:, :T] = npt_ref[...]
    npt_all_ref[:, T:] = nt(mt_ref[...], normed).astype(BF)
    has = at_ref[4] > 0
    npt_all = npt_all_ref[...]
    for g in range(2):
        mixed, *grads = head_group(g, has, qkv_ref, kvm_ref, dmix_ref)
        mixed_ref[:, GW * g : GW * g + GW] = mixed
        own, mem = group_outputs(g, g, at_ref, npt_all, w_ref, grads, send_ref, keep_ref)
        if g == 0:
            dn_ref[...] = own
            dnm_ref[...] = mem
        else:
            dn_ref[...] += own
            dnm_ref[...] += mem


def second_kernel(at_ref, w_ref, mt_ref, cot_ref, qkv_ref, dmix_ref, mixed_in, dn_in, dnm_in, kvm_ref, npt_all_ref,
                  xhat_ref, xhatm_ref, send_ref, keep_ref, mixed_ref, dn_ref):
    mixed, *grads = head_group(2, at_ref[4] > 0, qkv_ref, kvm_ref, dmix_ref)
    mixed_ref[:, : 2 * GW] = mixed_in[...]
    mixed_ref[:, 2 * GW :] = mixed
    own, mem = group_outputs(2, 0, at_ref, npt_all_ref[...], w_ref, grads, send_ref, keep_ref)
    lhs = nt(mt_ref[...], mixed_ref[...]).astype(BF)
    put_rows(send_ref, keep_ref, 1, at_ref[3], lhs, cot_ref[...])
    dn, dnm = dn_in[...] + own, dnm_in[...] + mem
    dn_ref[...] = dn
    vec = jnp.concatenate(
        [jnp.sum(dn * xhat_ref[...] + dnm * xhatm_ref[...], axis=0, keepdims=True), jnp.sum(dn + dnm, axis=0, keepdims=True)],
        axis=0,
    )
    rows = split_rows(vec)
    for out_ref in (send_ref, keep_ref):
        out_ref[384:392, 0:D] = rows


def token_kernel(gain_ref, x_ref, cot_ref, mixed_ref, wo_ref, dn_ref, xhat_ref, rstd_ref, out_ref, dx_ref):
    out_ref[...] = (x_ref[...].astype(F32) + nn(mixed_ref[...], wo_ref[...])).astype(BF)
    d_hat = dn_ref[...] * gain_ref[...].reshape(1, D)
    xhat = xhat_ref[...]
    row = rstd_ref[:, 0:1] * (
        d_hat
        - jnp.mean(d_hat, axis=-1, keepdims=True)
        - xhat * jnp.mean(d_hat * xhat, axis=-1, keepdims=True)
    )
    dx_ref[...] = (cot_ref[...].astype(F32) + row).astype(BF)


def split_rows(value):
    high = value.astype(BF)
    low = (value - high.astype(F32)).astype(BF)
    return jnp.concatenate([high, low, jnp.zeros((4, value.shape[1]), BF)], axis=0)


def join_rows(rows):
    return rows[0:2].astype(F32) + rows[2:4].astype(F32)


def fold_rows(value):
    high = value.astype(BF)
    low = (value - high.astype(F32)).astype(BF)
    return jnp.concatenate([high[:, :384], high[:, 384:], low[:, :384], low[:, 384:]], axis=0)


def unfold_rows(rows):
    rows = rows.astype(F32)
    return jnp.concatenate([rows[0:2] + rows[4:6], rows[2:4] + rows[6:8]], axis=1)


def tree(a, b, c, d):
    return (a.astype(F32) + b.astype(F32)) + (c.astype(F32) + d.astype(F32))


RING_Y = (1, 3, 2)
RING_X = (2, 3, 1)


def halving_order(ring):
    one, two, far = ring
    return [((one, far), (0, two)), ((two, far), (0, one))]


def pair_a_kernel(keep_ref, recv_ref, *outs):
    for part, groups in enumerate(halving_order(RING_Y)):
        cols = slice(768 * part, 768 * part + 768)
        for kept, places in enumerate(groups):
            for i, k in enumerate(places):
                rows = slice(96 * k, 96 * k + 96)
                outs[2 * part + kept][96 * i : 96 * i + 96, :] = (
                    keep_ref[rows, cols].astype(F32) + recv_ref[rows, cols].astype(F32)
                ).astype(BF)


def pair_b_kernel(keep_ref, recv_ref, *outs):
    for part, groups in enumerate(halving_order(RING_X)):
        for kept, places in enumerate(groups):
            out = outs[2 * part + kept]
            for i, k in enumerate(places):
                at = 768 * (k & 1) + 384 * part
                for y in range(4):
                    rows = slice(96 * y + 48 * (k >> 1), 96 * y + 48 * (k >> 1) + 48)
                    out[192 * i + 48 * y : 192 * i + 48 * y + 48, :] = (
                        keep_ref[rows, at : at + 384].astype(F32) + recv_ref[rows, at : at + 384].astype(F32)
                    ).astype(BF)
    vec = fold_rows(join_rows(keep_ref[384:392, 0:D]) + join_rows(recv_ref[384:392, 0:D]))
    outs[0][384:392, :] = vec
    outs[1][384:392, :] = vec


def step_a_kernel(recv0_ref, keep0_ref, recv1_ref, keep1_ref, send0_ref, send1_ref, own_ref):
    for part, (recv, keep, send) in enumerate(((recv0_ref, keep0_ref, send0_ref), (recv1_ref, keep1_ref, send1_ref))):
        add = lambda rows: keep[rows, :].astype(F32) + recv[rows, :].astype(F32)
        own_ref[:, 768 * part : 768 * part + 768] = add(slice(0, 96))
        send[...] = add(slice(96, 192)).astype(BF)


def step_b_kernel(recv0_ref, keep0_ref, recv1_ref, keep1_ref, send0_ref, send1_ref, own_ref, vec_ref):
    for part, (recv, keep, send) in enumerate(((recv0_ref, keep0_ref, send0_ref), (recv1_ref, keep1_ref, send1_ref))):
        add = lambda rows: keep[rows, :].astype(F32) + recv[rows, :].astype(F32)
        own_ref[:, 384 * part : 384 * part + 384] = add(slice(0, 192))
        send[0:192, :] = add(slice(192, 384)).astype(BF)
    vec = unfold_rows(keep0_ref[384:392, :]) + unfold_rows(recv0_ref[384:392, :])
    rows = fold_rows(vec)
    vec_ref[...] = unfold_rows(rows)
    send0_ref[192:200, :] = rows


def mid_a_kernel(own_ref, recv0_ref, recv1_ref, *outs):
    for out, places in zip(outs, halving_order(RING_X)[0]):
        for i, k in enumerate(places):
            rows = slice(48 * (k >> 1), 48 * (k >> 1) + 48)
            recv = recv1_ref if k & 1 else recv0_ref
            out[48 * i : 48 * i + 48, :] = (
                own_ref[rows, 768 * (k & 1) : 768 * (k & 1) + 768] + recv[rows, :].astype(F32)
            ).astype(BF)


def last_a_kernel(recv_ref, keep_ref, send_ref, own_ref):
    own_ref[...] = keep_ref[0:48, :].astype(F32) + recv_ref[0:48, :].astype(F32)
    send_ref[...] = (keep_ref[48:96, :].astype(F32) + recv_ref[48:96, :].astype(F32)).astype(BF)


def mid_b_kernel(own_ref, vec_ref, recv0_ref, recv1_ref, *outs):
    vec = split_rows(vec_ref[...] + unfold_rows(recv0_ref[192:200, :]))
    for k in range(4):
        rows = slice(48 * k, 48 * k + 48)
        outs[k][0:48, 0:384] = (own_ref[rows, 0:384] + recv0_ref[rows, :].astype(F32)).astype(BF)
        outs[k][0:48, 384:768] = (own_ref[rows, 384:768] + recv1_ref[rows, :].astype(F32)).astype(BF)
        outs[k][48:56, :] = vec


def plane_kernel(own_a_ref, recv_a_ref, b0, b1, b2, b3, out_ref):
    at = slice(48, 56)
    vec = (join_rows(b0[at]) + join_rows(b1[at])) + (join_rows(b2[at]) + join_rows(b3[at]))
    vec = jnp.concatenate([vec[0:1], vec[1:2]], axis=1)
    high = vec.astype(BF).astype(F32)
    tail = jnp.concatenate([high, vec - high], axis=0)
    g = slice(0, 48)
    sums = jnp.concatenate([own_a_ref[...] + recv_a_ref[...].astype(F32), tree(b0[g], b1[g], b2[g], b3[g])], axis=1)
    for z in range(8):
        out_ref[z] = jnp.concatenate([sums[6 * z : 6 * z + 6], tail], axis=0).astype(BF)


def column_kernel(factor, in_ref, rows_ref, gain_ref, bias_ref):
    acc = in_ref[0].astype(F32)
    for z in range(1, 8):
        acc = acc + in_ref[z].astype(F32)
    rows_ref[...] = acc.astype(BF)
    vec = (acc[6:7] + acc[7:8]) * factor
    gain_ref[...] = vec[:, :D].reshape(D)
    bias_ref[...] = vec[:, D:].reshape(D)


def finish_kernel(factor, at_ref, mine_ref, other_ref, qkv_ref, wout_ref):
    mine, other = mine_ref[...].astype(F32) * factor, other_ref[...].astype(F32) * factor
    first = at_ref[3] == 0
    halves = [jnp.where(first, mine, other), jnp.where(first, other, mine)]
    for g in range(GROUPS + 1):
        cols = slice(384 * g, 384 * g + 384)
        full = jnp.concatenate([halves[0][0:6, cols], halves[1][0:6, cols]], axis=1)
        if g < GROUPS:
            for i in range(3):
                at = D * i + GW * g
                qkv_ref[:, at : at + GW] = full[:, GW * i : GW * i + GW]
        else:
            wout_ref[...] = full


VM = pl.BlockSpec(memory_space=pltpu.VMEM)
SM = pl.BlockSpec(memory_space=pltpu.SMEM)
HBM = pl.BlockSpec(memory_space=pltpu.MemorySpace.HBM)


def call(kernel, name, out_shape, args, scalars=0, anys=(), scratch=(), limit=16):
    specs = [SM if i < scalars else HBM if i in anys else VM for i in range(len(args))]
    args = [pltpu.with_memory_space_constraint(a, pltpu.MemorySpace.HBM) if i in anys else a for i, a in enumerate(args)]
    return pl.pallas_call(
        kernel,
        name=name,
        in_specs=specs,
        out_specs=[VM] * len(out_shape),
        out_shape=out_shape,
        scratch_shapes=scratch,
        compiler_params=pltpu.CompilerParams(vmem_limit_bytes=limit * 1024 * 1024),
    )(*args)


def sds(*shape, dtype=BF):
    return jax.ShapeDtypeStruct(shape, dtype)


def on_device(layer_input, cotangent, gain, bias, w, wo):
    x, cot = layer_input[0], cotangent[0]
    seq = lax.axis_size(SEQ)
    xp = lax.ppermute(x, SEQ, [(i, i + 1) for i in range(seq - 1)])
    place = [lax.axis_index(n) for n in ("y", "xl", "c", "xh")] + [lax.axis_index(SEQ) > 0]
    at = jnp.stack([v.astype(jnp.int32) for v in place])
    row, mat, tokens = sds(T, D, dtype=F32), sds(D, D), sds(T, D)
    one = sds(D, dtype=F32)
    qkv, dmix, npt, xhat, rstd, mt, gain_v, bias_v, cot_v, w = call(
        own_kernel, "own_part",
        [sds(T, 3 * D), tokens, sds(D, T), row, sds(T, 128, dtype=F32), mat, one, one, tokens, sds(3, D, D)],
        [at, gain, bias, x, cot, w, wo], 1, (1, 2, 3, 4, 5, 6),
        [pltpu.VMEM((T, D), BF), pltpu.VMEM((D, D), BF), pltpu.SemaphoreType.DMA((8,))],
    )
    wide = sds(384, 1536)
    send_a, keep_a, mixed, dn, dnm, kvm, npt_all, xhatm = call(
        first_kernel, "memory_and_heads",
        [wide, wide, sds(T, 2 * GW), row, row, sds(T, 2 * D), sds(D, 2 * T), row],
        [at, gain_v, bias_v, xp, w, mt, qkv, dmix, npt], 1, limit=LIMIT,
    )
    send_b, keep_b, mixed, dn = call(
        second_kernel, "heads_and_output_weight",
        [sds(392, 1536), sds(392, 1536), tokens, row],
        [at, w, mt, cot_v, qkv, dmix, mixed, dn, dnm, kvm, npt_all, xhat, xhatm], 1, limit=LIMIT,
    )

    def swap(block):
        return lax.ppermute(block, "c", [(0, 1), (1, 0)])

    def permute(block, axes, k):
        n = lax.axis_size(axes)
        return lax.ppermute(block, axes, [(i, i ^ k) for i in range(n)])

    def exchange(parts, axes):
        return [parts[0]] + [permute(parts[k], axes, k) for k in (1, 2, 3)]

    half = sds(192, 768)
    send0_a, keep0_a, send1_a, keep1_a = call(pair_a_kernel, "pair_sum_a", [half] * 4, [keep_a, swap(send_a)])
    send0_b, keep0_b, send1_b, keep1_b = call(
        pair_b_kernel, "pair_sum_b", [sds(392, 384), sds(392, 384), sds(384, 384), sds(384, 384)],
        [keep_b, swap(send_b)],
    )
    got_a = [permute(send0_a, "y", RING_Y[0]), permute(send1_a, "y", RING_Y[1])]
    got_b = [permute(send0_b, ROW, RING_X[0]), permute(send1_b, ROW, RING_X[1])]
    out, dx = call(
        token_kernel, "token_outputs", [tokens, tokens],
        [gain, x, cot, mixed, wo, dn, xhat, rstd],
    )
    send0_a, send1_a, own_a = call(
        step_a_kernel, "step_sum_a", [sds(96, 768), sds(96, 768), sds(96, 1536, dtype=F32)],
        [got_a[0], keep0_a, got_a[1], keep1_a],
    )
    got_a = [permute(send0_a, "y", RING_Y[1]), permute(send1_a, "y", RING_Y[0])]
    send0_b, send1_b, own_b, vec = call(
        step_b_kernel, "step_sum_b", [sds(200, 384), sds(192, 384), sds(192, 768, dtype=F32), sds(2, D, dtype=F32)],
        [got_b[0], keep0_b, got_b[1], keep1_b],
    )
    got_b = [permute(send0_b, ROW, RING_X[1]), permute(send1_b, ROW, RING_X[0])]
    send_a, keep_a = call(mid_a_kernel, "middle_sum_a", [sds(96, 768)] * 2, [own_a, *got_a])
    got_a = permute(send_a, ROW, RING_X[0])
    parts_b = call(mid_b_kernel, "middle_sum_b", [sds(56, 768)] * 4, [own_b, vec, *got_b])
    send_a, own_a = call(last_a_kernel, "last_sum_a", [sds(48, 768), sds(48, 768, dtype=F32)], [got_a, keep_a])
    got_a = permute(send_a, ROW, RING_X[1])
    parts_b = exchange(parts_b, "y")
    (mine,) = call(plane_kernel, "plane_sum", [sds(8, 8, 1536)], [own_a, got_a, *parts_b])
    mine = lax.all_to_all(mine, "z", 0, 0, tiled=True)
    factor = 1.0 / float(seq * lax.axis_size("xh") * T) ** 0.5
    mine, grad_gain, grad_bias = call(
        functools.partial(column_kernel, factor), "column_sum",
        [sds(8, 1536), sds(D, dtype=F32), sds(D, dtype=F32)], [mine],
    )
    other = lax.ppermute(mine, "xh", [(0, 1), (1, 0)])
    grad_qkv, grad_out = call(
        functools.partial(finish_kernel, factor), "finish",
        [sds(6, 3 * D, dtype=F32), sds(6, D, dtype=F32)], [at, mine, other], 1,
    )
    return out[None], dx[None], grad_qkv, grad_out, grad_gain, grad_bias


def solution(mesh):
    torus = Mesh(mesh.devices.reshape(4, 8, 2, 2, 2), ("y", "z", "xl", "c", "xh"))
    return jax.shard_map(
        on_device,
        mesh=torus,
        in_specs=(P("xh", SEQ, None), P("xh", SEQ, None), P(), P(), P(), P()),
        out_specs=(P("xh", SEQ, None), P("xh", SEQ, None), P(SEQ, None), P(SEQ, None), P(), P()),
        check_vma=False,
    )
```

```python
import functools

import jax
import jax.numpy as jnp
from jax import lax
from jax.experimental import pallas as pl
from jax.experimental.pallas import tpu as pltpu
from jax.sharding import Mesh
from jax.sharding import PartitionSpec as P

HEADS = 12
EPS = 1e-05
SEQ = ("y", "z", "xl", "c")
ROW = ("xl", "xh")
T = 256
D = 768
GROUPS = 3
GW = 256
BF = jnp.bfloat16
F32 = jnp.float32
LIMIT = 24


def nn(a, b):
    return lax.dot_general(a, b, (((1,), (0,)), ((), ())), preferred_element_type=F32)


def nt(a, b):
    return lax.dot_general(a, b, (((1,), (1,)), ((), ())), preferred_element_type=F32)


def tn(a, b):
    return lax.dot_general(a, b, (((0,), (0,)), ((), ())), preferred_element_type=F32)


def layer_norm(x_ref, gain, bias):
    values = x_ref[...].astype(F32)
    centered = values - jnp.mean(values, axis=-1, keepdims=True)
    rstd = lax.rsqrt(jnp.mean(centered * centered, axis=-1, keepdims=True) + EPS)
    xhat = centered * rstd
    normed = (xhat * gain + bias).astype(BF)
    return normed, xhat, rstd


def row_order(at_ref):
    p = lax.broadcasted_iota(jnp.int32, (D, 1), 0)
    second = jnp.where(p >= 384, 1, 0)
    q = p - 384 * second
    owner = (q * 171) >> 13
    b = q - 48 * owner
    z = (b * 43) >> 8
    j = b - 6 * z
    y, xl = (owner >> 1) ^ at_ref[0], (owner & 1) ^ at_ref[1]
    to_core = jnp.where(second == 1, at_ref[2], 1 - at_ref[2])
    feature = ((y * 8 + z) * 2 + xl) * 12 + to_core * 6 + j
    cols = lax.broadcasted_iota(jnp.int32, (D, D), 1)
    return jnp.where(cols == feature, 1.0, 0.0).astype(BF)


def own_kernel(at_ref, gain_hbm, bias_hbm, x_hbm, cot_hbm, w_hbm, wo_hbm,
               qkv_ref, dmix_ref, npt_ref, xhat_ref, rstd_ref, mt_ref, gain_ref, bias_ref, cot_ref, w_ref,
               x_ref, wo_ref, sems):
    copies = [
        pltpu.make_async_copy(x_hbm, x_ref, sems.at[0]),
        pltpu.make_async_copy(gain_hbm, gain_ref, sems.at[1]),
        pltpu.make_async_copy(bias_hbm, bias_ref, sems.at[2]),
        pltpu.make_async_copy(cot_hbm, cot_ref, sems.at[3]),
        pltpu.make_async_copy(wo_hbm, wo_ref, sems.at[4]),
    ]
    for i in range(3):
        copies.append(pltpu.make_async_copy(w_hbm.at[:, pl.ds(D * i, D)], w_ref.at[i], sems.at[5 + i]))
    for copy in copies:
        copy.start()
    mt = row_order(at_ref)
    mt_ref[...] = mt
    for copy in copies[:3]:
        copy.wait()
    normed, xhat, rstd = layer_norm(x_ref, gain_ref[...].reshape(1, D), bias_ref[...].reshape(1, D))
    xhat_ref[...] = xhat
    rstd_ref[...] = jnp.broadcast_to(rstd, (T, 128))
    npt_ref[...] = nt(mt, normed).astype(BF)
    copies[3].wait()
    copies[4].wait()
    dmix_ref[...] = nt(cot_ref[...], wo_ref[...]).astype(BF)
    for i in range(3):
        copies[5 + i].wait()
        qkv_ref[:, D * i : D * i + D] = nn(normed, w_ref[i]).astype(BF)


def head_group(g, has, qkv_ref, kvm_ref, dmix_ref):
    at = GW * g
    lanes = lax.broadcasted_iota(jnp.int32, (T, 128), 1)
    low = lanes < 64
    causal = lax.broadcasted_iota(jnp.int32, (T, T), 0) <= lax.broadcasted_iota(jnp.int32, (T, T), 1)
    low_keys = lax.broadcasted_iota(jnp.int32, (2 * T, 128), 1) < 64
    zero = jnp.zeros((), BF)
    mixes, dqs, dks, dvs = [], [], [], []
    for pair in range(2):
        cq = slice(at + 128 * pair, at + 128 * pair + 128)
        ck = slice(D + cq.start, D + cq.stop)
        cv = slice(2 * D + cq.start, 2 * D + cq.stop)
        q2 = (qkv_ref[:, cq].astype(F32) * 0.125).astype(BF)
        k2 = jnp.concatenate([qkv_ref[:, ck], kvm_ref[:, cq]], axis=0)
        v2 = jnp.concatenate([qkv_ref[:, cv], kvm_ref[:, ck]], axis=0)
        dm2 = dmix_ref[:, cq]
        k_parts = [jnp.where(low_keys, k2, zero), jnp.where(low_keys, zero, k2)]
        v_parts = [jnp.where(low_keys, v2, zero), jnp.where(low_keys, zero, v2)]
        ds_parts, p_parts, q_parts, dm_parts = [], [], [], []
        for half in range(2):
            pick = low if half == 0 else jnp.logical_not(low)
            qa = jnp.where(pick, q2, zero)
            dma = jnp.where(pick, dm2, zero)
            st = nt(k2, qa)
            st_own = jnp.where(causal, st[:T], -1e30)
            st_mem = jnp.where(has, st[T:], -1e30)
            st = jnp.concatenate([st_own, st_mem], axis=0)
            top = jnp.max(st, axis=0, keepdims=True)
            e = jnp.exp(st - top)
            p = e * (1.0 / jnp.sum(e, axis=0, keepdims=True))
            pb = p.astype(BF)
            dp = nt(v2, dma)
            ds = (p * (dp - jnp.sum(dp * p, axis=0, keepdims=True))).astype(BF)
            ds_parts.append(ds)
            p_parts.append(pb)
            q_parts.append(qa)
            dm_parts.append(dma)
        dks.append(nn(jnp.concatenate(ds_parts, axis=1), jnp.concatenate(q_parts, axis=0)).astype(BF))
        dvs.append(nn(jnp.concatenate(p_parts, axis=1), jnp.concatenate(dm_parts, axis=0)).astype(BF))
        mixes.append(tn(jnp.concatenate(p_parts, axis=0), jnp.concatenate(v_parts, axis=0)).astype(BF))
        dqs.append((tn(jnp.concatenate(ds_parts, axis=0), jnp.concatenate(k_parts, axis=0)) * 0.125).astype(BF))
    dq = jnp.concatenate(dqs, axis=1)
    dk = jnp.concatenate(dks, axis=1)
    dv = jnp.concatenate(dvs, axis=1)
    return jnp.concatenate(mixes, axis=1), dq, dk, dv


def put_rows(send_ref, keep_ref, slot, xh, lhs, rhs):
    first, second = rhs[:, :384], rhs[:, 384:]
    mine = xh == 0
    rhs = jnp.concatenate([jnp.where(mine, first, second), jnp.where(mine, second, first)], axis=1)
    for out_ref, rows in ((send_ref, lhs[:384]), (keep_ref, lhs[384:])):
        sums = nn(rows, rhs).astype(BF)
        for r in range(2):
            at = 768 * r + 384 * slot
            out_ref[0:384, at : at + 384] = sums[:, 384 * r : 384 * r + 384]


def group_outputs(g, slot, at_ref, npt_all, w_ref, grads, send_ref, keep_ref):
    dq, dk, dv = grads
    rhs = jnp.concatenate([jnp.concatenate([dq, jnp.zeros((T, GW), BF)], axis=0), dk, dv], axis=1)
    put_rows(send_ref, keep_ref, slot, at_ref[3], npt_all, rhs)
    wq, wk, wv = (w_ref[i, :, GW * g : GW * g + GW] for i in range(3))
    own = nt(dq, wq) + nt(dk[:T], wk) + nt(dv[:T], wv)
    mem = nt(dk[T:], wk) + nt(dv[T:], wv)
    return own, mem


def first_kernel(at_ref, gain_ref, bias_ref, xp_ref, w_ref, mt_ref, qkv_ref, dmix_ref, npt_ref,
                 send_ref, keep_ref, mixed_ref, dn_ref, dnm_ref, kvm_ref, npt_all_ref, xhatm_ref):
    normed, xhat, _ = layer_norm(xp_ref, gain_ref[...].reshape(1, D), bias_ref[...].reshape(1, D))
    for i in range(2):
        kvm_ref[:, D * i : D * i + D] = nn(normed, w_ref[1 + i]).astype(BF)
    xhatm_ref[...] = xhat
    npt_all_ref[:, :T] = npt_ref[...]
    npt_all_ref[:, T:] = nt(mt_ref[...], normed).astype(BF)
    has = at_ref[4] > 0
    npt_all = npt_all_ref[...]
    for g in range(2):
        mixed, *grads = head_group(g, has, qkv_ref, kvm_ref, dmix_ref)
        mixed_ref[:, GW * g : GW * g + GW] = mixed
        own, mem = group_outputs(g, g, at_ref, npt_all, w_ref, grads, send_ref, keep_ref)
        if g == 0:
            dn_ref[...] = own
            dnm_ref[...] = mem
        else:
            dn_ref[...] += own
            dnm_ref[...] += mem


def second_kernel(at_ref, w_ref, mt_ref, cot_ref, qkv_ref, dmix_ref, mixed_in, dn_in, dnm_in, kvm_ref, npt_all_ref,
                  xhat_ref, xhatm_ref, send_ref, keep_ref, mixed_ref, dn_ref):
    mixed, *grads = head_group(2, at_ref[4] > 0, qkv_ref, kvm_ref, dmix_ref)
    mixed_ref[:, : 2 * GW] = mixed_in[...]
    mixed_ref[:, 2 * GW :] = mixed
    own, mem = group_outputs(2, 0, at_ref, npt_all_ref[...], w_ref, grads, send_ref, keep_ref)
    lhs = nt(mt_ref[...], mixed_ref[...]).astype(BF)
    put_rows(send_ref, keep_ref, 1, at_ref[3], lhs, cot_ref[...])
    dn, dnm = dn_in[...] + own, dnm_in[...] + mem
    dn_ref[...] = dn
    vec = jnp.concatenate(
        [jnp.sum(dn * xhat_ref[...] + dnm * xhatm_ref[...], axis=0, keepdims=True), jnp.sum(dn + dnm, axis=0, keepdims=True)],
        axis=0,
    )
    rows = split_rows(vec)
    for out_ref in (send_ref, keep_ref):
        out_ref[384:392, 0:D] = rows


def token_kernel(gain_ref, x_ref, cot_ref, mixed_ref, wo_ref, dn_ref, xhat_ref, rstd_ref, out_ref, dx_ref):
    out_ref[...] = (x_ref[...].astype(F32) + nn(mixed_ref[...], wo_ref[...])).astype(BF)
    d_hat = dn_ref[...] * gain_ref[...].reshape(1, D)
    xhat = xhat_ref[...]
    row = rstd_ref[:, 0:1] * (
        d_hat
        - jnp.mean(d_hat, axis=-1, keepdims=True)
        - xhat * jnp.mean(d_hat * xhat, axis=-1, keepdims=True)
    )
    dx_ref[...] = (cot_ref[...].astype(F32) + row).astype(BF)


def split_rows(value):
    high = value.astype(BF)
    low = (value - high.astype(F32)).astype(BF)
    return jnp.concatenate([high, low, jnp.zeros((4, value.shape[1]), BF)], axis=0)


def join_rows(rows):
    return rows[0:2].astype(F32) + rows[2:4].astype(F32)


def fold_rows(value):
    high = value.astype(BF)
    low = (value - high.astype(F32)).astype(BF)
    return jnp.concatenate([high[:, :384], high[:, 384:], low[:, :384], low[:, 384:]], axis=0)


def unfold_rows(rows):
    rows = rows.astype(F32)
    return jnp.concatenate([rows[0:2] + rows[4:6], rows[2:4] + rows[6:8]], axis=1)


def tree(a, b, c, d):
    return (a.astype(F32) + b.astype(F32)) + (c.astype(F32) + d.astype(F32))


RING_Y = (1, 3, 2)
RING_X = (2, 3, 1)


def halving_order(ring):
    one, two, far = ring
    return [((one, far), (0, two)), ((two, far), (0, one))]


def pair_a_kernel(keep_ref, recv_ref, *outs):
    for part, groups in enumerate(halving_order(RING_Y)):
        cols = slice(768 * part, 768 * part + 768)
        for kept, places in enumerate(groups):
            for i, k in enumerate(places):
                rows = slice(96 * k, 96 * k + 96)
                outs[2 * part + kept][96 * i : 96 * i + 96, :] = (
                    keep_ref[rows, cols].astype(F32) + recv_ref[rows, cols].astype(F32)
                ).astype(BF)


def pair_b_kernel(keep_ref, recv_ref, *outs):
    for part, groups in enumerate(halving_order(RING_X)):
        for kept, places in enumerate(groups):
            out = outs[2 * part + kept]
            for i, k in enumerate(places):
                at = 768 * (k & 1) + 384 * part
                for y in range(4):
                    rows = slice(96 * y + 48 * (k >> 1), 96 * y + 48 * (k >> 1) + 48)
                    out[192 * i + 48 * y : 192 * i + 48 * y + 48, :] = (
                        keep_ref[rows, at : at + 384].astype(F32) + recv_ref[rows, at : at + 384].astype(F32)
                    ).astype(BF)
    vec = fold_rows(join_rows(keep_ref[384:392, 0:D]) + join_rows(recv_ref[384:392, 0:D]))
    outs[0][384:392, :] = vec
    outs[1][384:392, :] = vec


def step_a_kernel(recv0_ref, keep0_ref, recv1_ref, keep1_ref, send0_ref, send1_ref, own_ref):
    for part, (recv, keep, send) in enumerate(((recv0_ref, keep0_ref, send0_ref), (recv1_ref, keep1_ref, send1_ref))):
        add = lambda rows: keep[rows, :].astype(F32) + recv[rows, :].astype(F32)
        own_ref[:, 768 * part : 768 * part + 768] = add(slice(0, 96))
        send[...] = add(slice(96, 192)).astype(BF)


def step_b_kernel(recv0_ref, keep0_ref, recv1_ref, keep1_ref, send0_ref, send1_ref, own_ref, vec_ref):
    for part, (recv, keep, send) in enumerate(((recv0_ref, keep0_ref, send0_ref), (recv1_ref, keep1_ref, send1_ref))):
        add = lambda rows: keep[rows, :].astype(F32) + recv[rows, :].astype(F32)
        own_ref[:, 384 * part : 384 * part + 384] = add(slice(0, 192))
        send[0:192, :] = add(slice(192, 384)).astype(BF)
    vec = unfold_rows(keep0_ref[384:392, :]) + unfold_rows(recv0_ref[384:392, :])
    rows = fold_rows(vec)
    vec_ref[...] = unfold_rows(rows)
    send0_ref[192:200, :] = rows


def mid_a_kernel(own_ref, recv0_ref, recv1_ref, *outs):
    for out, places in zip(outs, halving_order(RING_X)[0]):
        for i, k in enumerate(places):
            rows = slice(48 * (k >> 1), 48 * (k >> 1) + 48)
            recv = recv1_ref if k & 1 else recv0_ref
            out[48 * i : 48 * i + 48, :] = (
                own_ref[rows, 768 * (k & 1) : 768 * (k & 1) + 768] + recv[rows, :].astype(F32)
            ).astype(BF)


def last_a_kernel(recv_ref, keep_ref, send_ref, own_ref):
    own_ref[...] = keep_ref[0:48, :].astype(F32) + recv_ref[0:48, :].astype(F32)
    send_ref[...] = (keep_ref[48:96, :].astype(F32) + recv_ref[48:96, :].astype(F32)).astype(BF)


def mid_b_kernel(own_ref, vec_ref, recv0_ref, recv1_ref, *outs):
    vec = split_rows(vec_ref[...] + unfold_rows(recv0_ref[192:200, :]))
    for k in range(4):
        rows = slice(48 * k, 48 * k + 48)
        outs[k][0:48, 0:384] = (own_ref[rows, 0:384] + recv0_ref[rows, :].astype(F32)).astype(BF)
        outs[k][0:48, 384:768] = (own_ref[rows, 384:768] + recv1_ref[rows, :].astype(F32)).astype(BF)
        outs[k][48:56, :] = vec


def plane_kernel(own_a_ref, recv_a_ref, b0, b1, b2, b3, out_ref):
    at = slice(48, 56)
    vec = (join_rows(b0[at]) + join_rows(b1[at])) + (join_rows(b2[at]) + join_rows(b3[at]))
    vec = jnp.concatenate([vec[0:1], vec[1:2]], axis=1)
    high = vec.astype(BF).astype(F32)
    tail = jnp.concatenate([high, vec - high], axis=0)
    g = slice(0, 48)
    sums = jnp.concatenate([own_a_ref[...] + recv_a_ref[...].astype(F32), tree(b0[g], b1[g], b2[g], b3[g])], axis=1)
    for z in range(8):
        out_ref[z] = jnp.concatenate([sums[6 * z : 6 * z + 6], tail], axis=0).astype(BF)


def column_kernel(factor, in_ref, rows_ref, gain_ref, bias_ref):
    acc = in_ref[0].astype(F32)
    for z in range(1, 8):
        acc = acc + in_ref[z].astype(F32)
    rows_ref[...] = acc.astype(BF)
    vec = (acc[6:7] + acc[7:8]) * factor
    gain_ref[...] = vec[:, :D].reshape(D)
    bias_ref[...] = vec[:, D:].reshape(D)


def finish_kernel(factor, at_ref, mine_ref, other_ref, qkv_ref, wout_ref):
    mine, other = mine_ref[...].astype(F32) * factor, other_ref[...].astype(F32) * factor
    first = at_ref[3] == 0
    halves = [jnp.where(first, mine, other), jnp.where(first, other, mine)]
    for g in range(GROUPS + 1):
        cols = slice(384 * g, 384 * g + 384)
        full = jnp.concatenate([halves[0][0:6, cols], halves[1][0:6, cols]], axis=1)
        if g < GROUPS:
            for i in range(3):
                at = D * i + GW * g
                qkv_ref[:, at : at + GW] = full[:, GW * i : GW * i + GW]
        else:
            wout_ref[...] = full


VM = pl.BlockSpec(memory_space=pltpu.VMEM)
SM = pl.BlockSpec(memory_space=pltpu.SMEM)
HBM = pl.BlockSpec(memory_space=pltpu.MemorySpace.HBM)


def call(kernel, name, out_shape, args, scalars=0, anys=(), scratch=(), limit=16):
    specs = [SM if i < scalars else HBM if i in anys else VM for i in range(len(args))]
    args = [pltpu.with_memory_space_constraint(a, pltpu.MemorySpace.HBM) if i in anys else a for i, a in enumerate(args)]
    return pl.pallas_call(
        kernel,
        name=name,
        in_specs=specs,
        out_specs=[VM] * len(out_shape),
        out_shape=out_shape,
        scratch_shapes=scratch,
        compiler_params=pltpu.CompilerParams(vmem_limit_bytes=limit * 1024 * 1024),
    )(*args)


def sds(*shape, dtype=BF):
    return jax.ShapeDtypeStruct(shape, dtype)


def on_device(layer_input, cotangent, gain, bias, w, wo):
    x, cot = layer_input[0], cotangent[0]
    seq = lax.axis_size(SEQ)
    xp = lax.ppermute(x, SEQ, [(i, i + 1) for i in range(seq - 1)])
    place = [lax.axis_index(n) for n in ("y", "xl", "c", "xh")] + [lax.axis_index(SEQ) > 0]
    at = jnp.stack([v.astype(jnp.int32) for v in place])
    row, mat, tokens = sds(T, D, dtype=F32), sds(D, D), sds(T, D)
    one = sds(D, dtype=F32)
    qkv, dmix, npt, xhat, rstd, mt, gain_v, bias_v, cot_v, w = call(
        own_kernel, "own_part",
        [sds(T, 3 * D), tokens, sds(D, T), row, sds(T, 128, dtype=F32), mat, one, one, tokens, sds(3, D, D)],
        [at, gain, bias, x, cot, w, wo], 1, (1, 2, 3, 4, 5, 6),
        [pltpu.VMEM((T, D), BF), pltpu.VMEM((D, D), BF), pltpu.SemaphoreType.DMA((8,))],
    )
    wide = sds(384, 1536)
    send_a, keep_a, mixed, dn, dnm, kvm, npt_all, xhatm = call(
        first_kernel, "memory_and_heads",
        [wide, wide, sds(T, 2 * GW), row, row, sds(T, 2 * D), sds(D, 2 * T), row],
        [at, gain_v, bias_v, xp, w, mt, qkv, dmix, npt], 1, limit=LIMIT,
    )
    send_b, keep_b, mixed, dn = call(
        second_kernel, "heads_and_output_weight",
        [sds(392, 1536), sds(392, 1536), tokens, row],
        [at, w, mt, cot_v, qkv, dmix, mixed, dn, dnm, kvm, npt_all, xhat, xhatm], 1, limit=LIMIT,
    )

    def swap(block):
        return lax.ppermute(block, "c", [(0, 1), (1, 0)])

    def permute(block, axes, k):
        n = lax.axis_size(axes)
        return lax.ppermute(block, axes, [(i, i ^ k) for i in range(n)])

    def exchange(parts, axes):
        got = {k: permute(parts[k], axes, k) for k in (2, 1, 3)}
        return [parts[0], got[1], got[2], got[3]]

    half = sds(192, 768)
    send0_a, keep0_a, send1_a, keep1_a = call(pair_a_kernel, "pair_sum_a", [half] * 4, [keep_a, swap(send_a)])
    send0_b, keep0_b, send1_b, keep1_b = call(
        pair_b_kernel, "pair_sum_b", [sds(392, 384), sds(392, 384), sds(384, 384), sds(384, 384)],
        [keep_b, swap(send_b)],
    )
    got_a = [permute(send0_a, "y", RING_Y[0]), permute(send1_a, "y", RING_Y[1])]
    got_b = [permute(send0_b, ROW, RING_X[0]), permute(send1_b, ROW, RING_X[1])]
    out, dx = call(
        token_kernel, "token_outputs", [tokens, tokens],
        [gain, x, cot, mixed, wo, dn, xhat, rstd],
    )
    send0_a, send1_a, own_a = call(
        step_a_kernel, "step_sum_a", [sds(96, 768), sds(96, 768), sds(96, 1536, dtype=F32)],
        [got_a[0], keep0_a, got_a[1], keep1_a],
    )
    got_a = [permute(send0_a, "y", RING_Y[1]), permute(send1_a, "y", RING_Y[0])]
    send0_b, send1_b, own_b, vec = call(
        step_b_kernel, "step_sum_b", [sds(200, 384), sds(192, 384), sds(192, 768, dtype=F32), sds(2, D, dtype=F32)],
        [got_b[0], keep0_b, got_b[1], keep1_b],
    )
    got_b = [permute(send0_b, ROW, RING_X[1]), permute(send1_b, ROW, RING_X[0])]
    send_a, keep_a = call(mid_a_kernel, "middle_sum_a", [sds(96, 768)] * 2, [own_a, *got_a])
    got_a = permute(send_a, ROW, RING_X[0])
    parts_b = call(mid_b_kernel, "middle_sum_b", [sds(56, 768)] * 4, [own_b, vec, *got_b])
    send_a, own_a = call(last_a_kernel, "last_sum_a", [sds(48, 768), sds(48, 768, dtype=F32)], [got_a, keep_a])
    got_a = permute(send_a, ROW, RING_X[1])
    parts_b = exchange(parts_b, "y")
    (mine,) = call(plane_kernel, "plane_sum", [sds(8, 8, 1536)], [own_a, got_a, *parts_b])
    mine = lax.all_to_all(mine, "z", 0, 0, tiled=True)
    factor = 1.0 / float(seq * lax.axis_size("xh") * T) ** 0.5
    mine, grad_gain, grad_bias = call(
        functools.partial(column_kernel, factor), "column_sum",
        [sds(8, 1536), sds(D, dtype=F32), sds(D, dtype=F32)], [mine],
    )
    other = lax.ppermute(mine, "xh", [(0, 1), (1, 0)])
    grad_qkv, grad_out = call(
        functools.partial(finish_kernel, factor), "finish",
        [sds(6, 3 * D, dtype=F32), sds(6, D, dtype=F32)], [at, mine, other], 1,
    )
    return out[None], dx[None], grad_qkv, grad_out, grad_gain, grad_bias


def solution(mesh):
    torus = Mesh(mesh.devices.reshape(4, 8, 2, 2, 2), ("y", "z", "xl", "c", "xh"))
    return jax.shard_map(
        on_device,
        mesh=torus,
        in_specs=(P("xh", SEQ, None), P("xh", SEQ, None), P(), P(), P(), P()),
        out_specs=(P("xh", SEQ, None), P("xh", SEQ, None), P(SEQ, None), P(SEQ, None), P(), P()),
        check_vma=False,
    )
```
